32 devices in a mesh: region: 32 (over z, y, x, core).
Axes of the slice: x: 2, y: 2, z: 4, core: 2. Of those that a mesh axis runs over, the one named last changes fastest.
Arguments:
- gaussians: float32 [32, 9, 4096], P('region')
- depth: int32 [32, 512, 8], P('region'), may hold values from 0 to 7, each once within a row
- coverage: int32 [32, 512], P('region'), may hold values 0 or 1
- flips: int32 [512, 31], replicated, may hold values 0 or 1
- features: bfloat16 [131072, 384], P('region'), may hold values from -6 to 6
- w_first: bfloat16 [384, 384], replicated, may hold values from -0.3125 to 0.3125
- b_first: float32 [384], replicated, may hold values from -3 to 3
- w_second: bfloat16 [384], replicated, may hold values from -0.3125 to 0.3125
- target: float32 [3, 131072], P(None, 'region'), may hold values from 0 to 1
Outputs:
- pixel_loss: float32 [131072], P('region')
- splat_grads: float32 [32, 9, 4096], P('region')
The draws below stay inside these ranges and needn't reach their ends.
Inputs may be any that keep to these rules, and one draw needn't show every extreme that they name: Each tile's 8 depth ranks of one region are a permutation of 0 to 7.
All inputs are finite; a program needn't handle non-finite values. No bound on the sum of `coverage` on one device may be relied on, other than what follows from the above.
Results may differ from the reference program's by a relative error of at most 0.0022.
Values sent between devices are 32-bit elements; how exact they have to be, the bound alone decides.
A program may use at most 64 MiB of HBM per device.

```python
import math
import jax
import jax.numpy as jnp
from jax import lax

TILES = 512
TSIDE = 16
GPT = 8
FEAT = 384
HID = 384
REGIONS = 32
NODES = 31
PIXELS = 131072


def draw_gaussians(key, part):
    lower = jnp.array([-1.0, -1.0, 0.0, 0.0, -1.5, -4.0, -2.5, -2.5, -2.5], jnp.float32)
    upper = jnp.array([TSIDE + 1.0, TSIDE + 1.0, math.log(TSIDE * 0.5), math.log(TSIDE * 0.5), 1.5, 1.0, 2.5, 2.5, 2.5], jnp.float32)
    uniform_draw = jax.random.uniform(key, (REGIONS, 9, TILES * GPT), jnp.float32)
    return lower[None, :, None] + (upper - lower)[None, :, None] * uniform_draw


def with_ends(values, rng, smallest, high):
    index_at = [jax.random.randint(jax.random.fold_in(rng, axis), (), 0, length) for axis, length in enumerate(values.shape)]
    longest = values.shape.index(max(values.shape))
    next_to = index_at[:longest] + [(index_at[longest] + 1) % values.shape[longest]] + index_at[longest + 1:]
    return values.at[tuple(index_at)].set(smallest).at[tuple(next_to)].set(high)


def shard_levels(own_key, dims, cuts, smallest, high):
    def one(dim, parts):
        heights = jax.random.uniform(jax.random.fold_in(jax.random.fold_in(own_key, 6), dim), (parts,), jnp.float32, smallest / len(cuts), high / len(cuts))
        return jnp.repeat(jnp.exp(heights), dims[dim] // parts).reshape((-1,) + (1,) * (len(dims) - dim - 1))

    loudness = one(*cuts[0])
    for cut in cuts[1:]:
        loudness = loudness * one(*cut)
    return loudness


def normal_values(stream_key, dims, deviation, bound, split=(), dtype=jnp.bfloat16):
    entries = deviation * jax.random.normal(stream_key, dims, jnp.float32)
    if split:
        entries = entries * shard_levels(stream_key, dims, split, -0.22, 0.18)
    return jnp.clip(entries, -bound, bound).astype(dtype)


def setup_inputs(seed: int = 0) -> dict:
    key_list = jax.random.split(jax.random.key(seed), 10)
    gaussians = draw_gaussians(jax.random.fold_in(key_list[9], 71), 0)
    depth = jax.vmap(lambda own: jax.random.permutation(own, GPT))(jax.random.split(key_list[1], REGIONS * TILES)).reshape((REGIONS, TILES, GPT)).astype(jnp.int32)
    coverage = with_ends((jax.random.randint(key_list[2], (REGIONS, TILES), 0, 4) < 1).astype(jnp.int32), jax.random.fold_in(key_list[2], 1), 0, 1)
    flips = with_ends((jax.random.randint(key_list[3], (TILES, NODES), 0, 2) < 1).astype(jnp.int32), jax.random.fold_in(key_list[3], 1), 0, 1)
    features = normal_values(key_list[4], (PIXELS, FEAT), 1.0, 6.0, ((0, 32),))
    w_first = normal_values(key_list[5], (FEAT, HID), FEAT ** -0.5, 0.3125)
    b_first = normal_values(key_list[6], (HID,), 0.5, 3.0, (), jnp.float32)
    w_second = normal_values(key_list[7], (HID,), HID ** -0.5, 0.3125)
    target = jnp.clip(1.0 * jax.random.uniform(key_list[8], (3, PIXELS), jnp.float32) ** shard_levels(key_list[8], (3, PIXELS), ((1, 32),), -0.2, 0.2), 0.0, 1.0)
    return {"gaussians": gaussians, "depth": depth, "coverage": coverage, "flips": flips, "features": features, "w_first": w_first, "b_first": b_first, "w_second": w_second, "target": target}


def render_tiles(params, splat_ranks, covered):
    pixel_index = jnp.arange(TSIDE * TSIDE)
    column_pos = (pixel_index % TSIDE).astype(jnp.float32) + 0.5
    row_pos = (pixel_index // TSIDE).astype(jnp.float32) + 0.5
    delta_x = column_pos[None, None, :] - params[0][:, :, None]
    delta_y = row_pos[None, None, :] - params[1][:, :, None]
    unit_x = delta_x * jnp.exp(-params[2])[:, :, None]
    unit_y = delta_y * jnp.exp(-params[3])[:, :, None]
    correlation = (0.9 * jnp.tanh(params[4]))[:, :, None]
    quadratic = (unit_x * unit_x - 2.0 * correlation * unit_x * unit_y + unit_y * unit_y) / (1.0 - correlation * correlation)
    opacity = 0.99 * jax.nn.sigmoid(params[5]) * covered[:, None].astype(jnp.float32)
    absorb = opacity[:, :, None] * jnp.exp(-0.5 * quadratic)
    log_trans = jnp.log1p(-absorb)
    prior = (splat_ranks[:, None, :] < splat_ranks[:, :, None]).astype(jnp.float32)
    leading = jnp.einsum('tgh,thp->tgp', prior, log_trans, precision=lax.Precision.HIGHEST)
    weight = jnp.exp(leading) * absorb
    colors = jax.nn.sigmoid(params[6:9])
    color_sum = lax.optimization_barrier(jnp.sum(colors[:, :, :, None] * weight[None], 2))
    transmit = jnp.exp(lax.optimization_barrier(jnp.sum(log_trans, axis=1)))
    return jnp.concatenate([color_sum, transmit[None]], 0)

def over_pair(front_layer, back_layer):
    blended = front_layer[:, :3] + front_layer[:, 3:4] * back_layer[:, :3]
    transmit = front_layer[:, 3:4] * back_layer[:, 3:4]
    return jnp.concatenate([blended, transmit], 1)

def tree_levels(stack, stripe_flips):
    number = stack.shape[0]
    while number > 1:
        half_count = number // 2
        in_front = (stripe_flips[:, half_count - 1:2 * half_count - 1].T > 0)[:, None, :, None]
        paired = stack.reshape((half_count, 2) + stack.shape[1:])
        front_layer = jnp.where(in_front, paired[:, 1], paired[:, 0])
        back_layer = jnp.where(in_front, paired[:, 0], paired[:, 1])
        stack = over_pair(front_layer, back_layer)
        number = half_count
    return stack[0]

def uncertainty(stripe_feats, w_first, b_first, w_second):
    hidden = jax.nn.gelu(jnp.dot(stripe_feats, w_first, preferred_element_type=jnp.float32) + b_first).astype(jnp.bfloat16)
    return 0.5 + jax.nn.softplus(jnp.dot(hidden, w_second, preferred_element_type=jnp.float32))

def reference(gaussians, depth, coverage, flips, features, w_first, b_first, w_second, target):
    regions = gaussians.shape[0]
    tile_count = depth.shape[1]
    splats = depth.shape[2]
    stripe_tiles = tile_count // regions
    tile_pixels = TSIDE * TSIDE
    grid_params = gaussians.reshape(regions, 9, tile_count, splats)

    def stripe_work(stripe_index):
        first_tile = (stripe_index * stripe_tiles).astype(jnp.int32)
        params = lax.dynamic_slice_in_dim(grid_params, first_tile, stripe_tiles, 2)
        splat_ranks = lax.dynamic_slice_in_dim(depth, first_tile, stripe_tiles, 1)
        covered = lax.dynamic_slice_in_dim(coverage, first_tile, stripe_tiles, 1)
        stripe_flips = lax.dynamic_slice_in_dim(flips, first_tile, stripe_tiles, 0)
        first_pixel = (first_tile * tile_pixels).astype(jnp.int32)
        stripe_feats = lax.dynamic_slice_in_dim(features, first_pixel, stripe_tiles * tile_pixels, 0)
        wanted = lax.dynamic_slice_in_dim(target, first_pixel, stripe_tiles * tile_pixels, 1).reshape(3, stripe_tiles, tile_pixels)
        spread = uncertainty(stripe_feats, w_first, b_first, w_second).reshape(stripe_tiles, tile_pixels)

        def stripe_loss(region_params):
            pieces = jax.vmap(render_tiles)(region_params, splat_ranks, covered)
            composite = tree_levels(pieces, stripe_flips)
            residual = composite[:3] + composite[3:4] - wanted
            return lax.optimization_barrier(jnp.sum(residual * residual, 0)) / (2.0 * spread * spread)
        loss_part, pull_back = jax.vjp(stripe_loss, params)
        gradient, = pull_back(jnp.ones_like(loss_part))
        return (loss_part + jnp.log(spread), gradient)
    losses, gradients = lax.map(stripe_work, jnp.arange(regions).astype(jnp.int32))
    pixel_loss = losses.reshape(tile_count * tile_pixels)
    splat_grads = gradients.transpose(1, 2, 0, 3, 4).reshape(regions, 9, tile_count * splats)
    return (pixel_loss, splat_grads)
```

```python
import jax
import jax.numpy as jnp
from jax import lax
from jax.experimental import pallas as pl
from jax.experimental.pallas import tpu as pltpu
from jax.sharding import PartitionSpec as P

TSIDE = 16
LANES = 128
SPLATS = 8
NPAR = 9
NMOM = 6
BATCH = 8
EARLY = 4
LOG2E = 1.4426950408889634
MESH = pl.DeviceIdType.MESH


def iota(shape, dim):
    return lax.broadcasted_iota(jnp.int32, shape, dim)


def dot(x, y, transposed=False, selector=1, pieces=3):
    dims = (((1,), (1 if transposed else 0,)), ((), ()))
    bf16 = jnp.bfloat16
    sel, val = (y, x) if selector == 1 else (x, y)
    sel = sel.astype(bf16)
    total = None
    for _ in range(pieces):
        piece = val.astype(bf16)
        val = val - piece.astype(jnp.float32)
        pair = (piece, sel) if selector == 1 else (sel, piece)
        part = lax.dot_general(*pair, dims, preferred_element_type=jnp.float32)
        total = part if total is None else total + part
    return total


def same(shape, first, second):
    return (first(iota(shape, 0)) == second(iota(shape, 1))).astype(jnp.float32)


def along_lanes(x, index):
    return jnp.take_along_axis(x, index, axis=1)


def to_lanes(x):
    row, lane = iota((8, LANES), 0), iota((8, LANES), 1)
    x = along_lanes(x, ((lane // 16 - row) & 7) * 16 + (lane & 15))
    x = jnp.take_along_axis(x, (lane // 16 - row) & 7, axis=0)
    return along_lanes(x, ((row + (lane & 7)) & 7) * 16 + lane // 8)


def splat_kernel(
    gauss_ref, depth_ref, cover_ref, flips_ref, feat_hbm, first_ref, bias_ref, second_ref,
    target_ref, loss_ref, grads_ref,
    feat_ref, feat_sem, send_ref, recv_ref, send_sem, recv_sem, gsend_ref, gsend_sem,
    grecv_sem, flip_ref, spread_ref, wanted_ref,
    ex_ref, a_ref, w_ref, tree_ref, down_ref, g_ref, lossy_ref, rhs_ref, stage_ref, basis_ref, fold_ref,
):
    regions = recv_ref.shape[1]
    rows = wanted_ref.shape[1]
    nv = rows // 8
    tile_count = depth_ref.shape[1]
    stripe_tiles = tile_count // regions
    group = stripe_tiles * SPLATS
    per = LANES // group
    span = LANES // stripe_tiles
    inner = regions - 1
    batches = regions // BATCH
    pixels = TSIDE * TSIDE
    f32, bf16 = jnp.float32, jnp.bfloat16
    me = lax.axis_index("region")

    load = pltpu.make_async_copy(feat_hbm, feat_ref, feat_sem)
    load.start()
    barrier = pltpu.get_barrier_semaphore()

    def greet(i, carry):
        pl.semaphore_signal(
            barrier, inc=1, device_id=(lax.rem(me + i, regions),), device_id_type=MESH
        )
        return carry

    lax.fori_loop(1, regions, greet, 0)

    row8, lane8 = iota((8, LANES), 0), iota((8, LANES), 1)

    for c in range(tile_count // LANES):
        tiles = slice(c * LANES, (c + 1) * LANES)
        order = jnp.zeros((SPLATS, LANES), jnp.int32)
        for g in range(SPLATS):
            order = jnp.where(depth_ref[g:g + 1, tiles] == row8, g, order)
        index = (lane8 & -SPLATS) + to_lanes(order)
        cover = along_lanes(
            jnp.broadcast_to(cover_ref[:, tiles], (8, LANES)), row8 * 16 + lane8 // SPLATS
        )
        part = slice(8 * c, 8 * c + 8)
        x = [gauss_ref[p, part, :] for p in range(9)]
        rho = 0.9 * jnp.tanh(x[4])
        scale = (0.5 * LOG2E) ** 0.5
        norm = lax.rsqrt(1.0 - rho * rho) * scale
        inv_y = jnp.exp(-x[3])
        values = [
            x[0],
            x[1],
            jnp.exp(-x[2]) * norm,
            inv_y * (rho * norm),
            inv_y * scale,
            0.99 * jax.nn.sigmoid(x[5]),
            jax.nn.sigmoid(x[6]),
            jax.nn.sigmoid(x[7]),
            jax.nn.sigmoid(x[8]),
        ]
        for p in range(9):
            value = along_lanes(values[p], index)
            if p == 5:
                value = jnp.log2(value * cover.astype(f32))
            for j in range(per):
                shifted = pltpu.roll(value, LANES - j * group, 1) if j else value
                if per == 1:
                    send_ref[p, part, :] = shifted
                else:
                    send_ref[p, pl.ds(8 * c * per + j, 8, stride=per), :] = shifted

    bias = bias_ref[...].reshape(1, bias_ref.shape[0])
    second = jnp.broadcast_to(
        second_ref[...].astype(f32).reshape(1, second_ref.shape[0]), (16, second_ref.shape[0])
    ).astype(bf16)

    block = max(16, span)
    per_block = block // span

    def network(j, carry):
        feats = feat_ref[:, pl.ds(pl.multiple_of(j * block, block), block), :]
        feats = feats.reshape(stripe_tiles * block, feat_ref.shape[2])
        hidden = jax.nn.gelu(
            jnp.dot(feats, first_ref[...], preferred_element_type=f32) + bias
        )
        hidden = hidden.reshape(stripe_tiles, per_block, span, hidden.shape[-1])
        for i in range(per_block):
            part = hidden[:, i].reshape(LANES, hidden.shape[-1]).astype(bf16)
            logits = lax.dot_general(
                second, part, (((1,), (1,)), ((), ())), preferred_element_type=f32,
            )
            spread_ref[pl.ds(j * per_block + i, 1), :] = logits[0:1]
        return carry

    steps = pixels // block
    early = min(EARLY, steps // 2)
    load.wait()
    if early:
        lax.fori_loop(0, early, network, 0, unroll=2)
    pl.semaphore_wait(barrier, regions - 1)

    def send(i, carry):
        peer = lax.rem(me + i, regions)
        pltpu.make_async_remote_copy(
            src_ref=send_ref.at[:, pl.ds(peer, 1), :], dst_ref=recv_ref.at[:, pl.ds(me, 1), :],
            send_sem=send_sem, recv_sem=recv_sem, device_id=(peer,), device_id_type=MESH,
        ).start()
        return carry

    lax.fori_loop(1, regions, send, 0)
    for p in range(9):
        recv_ref[p, pl.ds(me, 1), :] = send_ref[p, pl.ds(me, 1), :]
    lax.fori_loop(early, steps, network, 0, unroll=2)

    tile_lane = same((LANES, stripe_tiles), lambda i: i // span, lambda j: j)
    lane_pixel = same((LANES, pixels), lambda i: i & (span - 1), lambda j: j & (span - 1))
    row_pixel = same((rows, pixels), lambda i: i, lambda j: j // span)
    for k in range(3):
        flat = jnp.concatenate(
            [target_ref[k:k + 1, t * pixels:(t + 1) * pixels] for t in range(stripe_tiles)], 0
        )
        wanted_ref[k] = dot(row_pixel, dot(tile_lane, flat, selector=0) * lane_pixel, True, selector=0)
    my_tiles = same(
        (tile_count, LANES), lambda i: i - me * stripe_tiles, lambda j: j // span
    ).astype(bf16)
    flip_ref[...] = jnp.dot(
        flips_ref[...].astype(f32).astype(bf16), my_tiles, preferred_element_type=f32,
    )

    wide = min(span, TSIDE)
    half = (TSIDE - wide) / 2

    def x_row(i):
        return ((i * span) & (TSIDE - 1)).astype(f32) - half

    def y_row(i):
        return (i * span // TSIDE).astype(f32) - 7.5

    x_lane = (lane8 & (wide - 1)).astype(f32) + (half + 0.5)
    y_lane = ((lane8 & (span - 1)) // TSIDE).astype(f32) + 8.0
    depth_rows = SPLATS * rows
    at = iota((SPLATS, depth_rows), 1)
    mine = at // rows == iota((SPLATS, depth_rows), 0)
    xr, yr = x_row(at & (rows - 1)), y_row(at & (rows - 1))
    terms = [jnp.ones_like(xr), xr, yr, xr * xr, xr * yr, yr * yr]
    basis_ref[...] = jnp.concatenate([jnp.where(mine, term, 0.0) for term in terms], 0).astype(bf16)
    for s in range(SPLATS):
        fold_ref[s * LANES:(s + 1) * LANES, :] = same(
            (LANES, LANES), lambda i: i // span * SPLATS + s, lambda j: j
        ).astype(bf16)

    everyone = pl.ds(0, regions - 1)
    pltpu.make_async_remote_copy(
        src_ref=send_ref.at[:, everyone, :], dst_ref=recv_ref.at[:, everyone, :],
        send_sem=send_sem, recv_sem=recv_sem, device_id=(me,), device_id_type=MESH,
    ).wait()

    def expand(c, carry):
        base = pl.multiple_of(c * BATCH, BATCH)
        for p in range(NPAR):
            value = recv_ref[p, pl.ds(base, BATCH), :]
            for s in range(SPLATS):
                first = pl.multiple_of((c * NPAR + p) * SPLATS * BATCH, BATCH) + s * BATCH
                ex_ref[pl.ds(first, BATCH), :] = along_lanes(
                    value, lane8 // span * SPLATS + s
                )
        return carry

    lax.fori_loop(0, batches, expand, 0)

    vs = [slice(8 * v, 8 * v + 8) for v in range(nv)]
    xpos = x_row(row8) + x_lane
    ypos = [y_row(row8 + 8 * v) + y_lane for v in range(nv)]

    def first_row(r, p):
        return (r // BATCH * NPAR + p) * (SPLATS * BATCH) + (r & (BATCH - 1))

    def row(r, p, s):
        return ex_ref[pl.ds(first_row(r, p) + s * BATCH, 1), :]

    def forward(r, carry):
        trans = [jnp.ones((8, LANES), f32)] * nv
        color = [[jnp.zeros((8, LANES), f32)] * nv for _ in range(3)]
        for s in range(SPLATS):
            us = (xpos - row(r, 0, s)) * row(r, 2, s)
            m_y, skew, inv_y, level = row(r, 1, s), row(r, 3, s), row(r, 4, s), row(r, 5, s)
            ks = [row(r, 6 + k, s) for k in range(3)]
            for v in range(nv):
                dy = ypos[v] - m_y
                w = dy * inv_y
                p = us - dy * skew
                alpha = jnp.exp2(level - (p * p + w * w))
                weight = trans[v] * alpha
                a_ref[r * SPLATS + s, vs[v]] = alpha
                w_ref[r * SPLATS + s, vs[v]] = weight
                for k in range(3):
                    color[k][v] = color[k][v] + weight * ks[k]
                trans[v] = trans[v] - weight
        for v in range(nv):
            for k in range(3):
                tree_ref[inner + r, k, vs[v]] = color[k][v]
            tree_ref[inner + r, 3, vs[v]] = trans[v]
        return carry

    lax.fori_loop(0, regions, forward, 0)

    def flipped(n):
        return jnp.broadcast_to(flip_ref[pl.ds(n, 1), :], (8, LANES)) > 0.0

    def merge(i, carry):
        n = inner - 1 - i
        flip = flipped(n)
        for v in range(nv):
            low = [tree_ref[2 * n + 1, k, vs[v]] for k in range(4)]
            high = [tree_ref[2 * n + 2, k, vs[v]] for k in range(4)]
            over_low = jnp.where(flip, high[3], 1.0)
            over_high = jnp.where(flip, 1.0, low[3])
            for k in range(3):
                tree_ref[n, k, vs[v]] = over_low * low[k] + over_high * high[k]
            tree_ref[n, 3, vs[v]] = low[3] * high[3]
        return carry

    lax.fori_loop(0, inner, merge, 0)

    for v in range(nv):
        logit = spread_ref[vs[v]]
        spread = 0.5 + jnp.maximum(logit, 0.0) + jnp.log1p(jnp.exp(-jnp.abs(logit)))
        inv_square = 1.0 / (spread * spread)
        clear = tree_ref[0, 3, vs[v]]
        residual = [tree_ref[0, k, vs[v]] + clear - wanted_ref[k, vs[v]] for k in range(3)]
        total = residual[0] * residual[0] + residual[1] * residual[1] + residual[2] * residual[2]
        lossy_ref[vs[v]] = 0.5 * total * inv_square + jnp.log(spread)
        gs = [res * inv_square for res in residual]
        for k in range(3):
            g_ref[k, vs[v]] = gs[k]
        down_ref[0, 0, vs[v]] = jnp.ones((8, LANES), f32)
        down_ref[0, 1, vs[v]] = gs[0] + gs[1] + gs[2]

    def split(n, carry):
        flip = flipped(n)
        for v in range(nv):
            low = [tree_ref[2 * n + 1, k, vs[v]] for k in range(4)]
            high = [tree_ref[2 * n + 2, k, vs[v]] for k in range(4)]
            g = [g_ref[k, vs[v]] for k in range(3)]
            front, behind = down_ref[n, 0, vs[v]], down_ref[n, 1, vs[v]]
            back = [jnp.where(flip, l, h) for l, h in zip(low, high)]
            through = front * jnp.where(flip, high[3], low[3])
            value = g[0] * back[0] + g[1] * back[1] + g[2] * back[2] + back[3] * behind
            down_ref[2 * n + 1, 0, vs[v]] = jnp.where(flip, through, front)
            down_ref[2 * n + 2, 0, vs[v]] = jnp.where(flip, front, through)
            down_ref[2 * n + 1, 1, vs[v]] = jnp.where(flip, behind, value)
            down_ref[2 * n + 2, 1, vs[v]] = jnp.where(flip, value, behind)
        return carry

    lax.fori_loop(0, inner, split, 0)

    def backward(r, carry):
        front = [down_ref[inner + r, 0, vs[v]] for v in range(nv)]
        gs = [[front[v] * g_ref[k, vs[v]] for v in range(nv)] for k in range(3)]
        behind = [front[v] * down_ref[inner + r, 1, vs[v]] for v in range(nv)]
        for s in reversed(range(SPLATS)):
            ks = [row(r, 6 + k, s) for k in range(3)]
            parts = [[], [], [], []]
            for v in range(nv):
                alpha = a_ref[r * SPLATS + s, vs[v]]
                weight = w_ref[r * SPLATS + s, vs[v]]
                shade = ks[0] * gs[0][v] + ks[1] * gs[1][v] + ks[2] * gs[2][v]
                diff = shade - behind[v]
                behind[v] = behind[v] + alpha * diff
                parts[0].append(weight * diff)
                for k in range(3):
                    parts[1 + k].append(weight * gs[k][v])
            for q in range(4):
                rhs_ref[s * rows:(s + 1) * rows, q * LANES:(q + 1) * LANES] = jnp.concatenate(
                    parts[q], 0
                ).astype(bf16)
        summed = jnp.dot(basis_ref[...], rhs_ref[...], preferred_element_type=f32)
        h, hx, hy, hxx, hxy, hyy = [
            summed[b * SPLATS:(b + 1) * SPLATS, 0:LANES] for b in range(NMOM)
        ]
        dx = x_lane - ex_ref[pl.ds(first_row(r, 0), SPLATS, stride=BATCH), :]
        dy = y_lane - ex_ref[pl.ds(first_row(r, 1), SPLATS, stride=BATCH), :]
        about_x = hx + dx * h
        about_y = hy + dy * h
        moments = [
            h,
            about_x,
            about_y,
            hxx + dx * (hx + about_x),
            hxy + dx * hy + dy * about_x,
            hyy + dy * (hy + about_y),
        ]
        for k in range(3):
            moments.append(summed[0:SPLATS, (1 + k) * LANES:(2 + k) * LANES])
        for p in range(9):
            first = p * SPLATS * BATCH + (r & (BATCH - 1))
            stage_ref[pl.ds(first, SPLATS, stride=BATCH), :] = moments[p]
        return carry

    def finish(i, carry):
        which = lax.rem(i + 1 + me // BATCH, batches)
        base = pl.multiple_of(which * BATCH, BATCH)
        lax.fori_loop(base, base + BATCH, backward, 0)
        wide = [
            jnp.concatenate(
                [stage_ref[(p * SPLATS + s) * BATCH:(p * SPLATS + s + 1) * BATCH, :] for s in range(SPLATS)], 1
            )
            for p in range(9)
        ]
        folded = dot(jnp.concatenate(wide, 0), fold_ref[...], pieces=2)
        for p in range(9):
            gsend_ref[p, pl.ds(base, BATCH), :] = folded[p * BATCH:(p + 1) * BATCH]

        def back(j, carry):
            peer = base + j

            @pl.when(peer != me)
            def _():
                pltpu.make_async_remote_copy(
                    src_ref=gsend_ref.at[:, pl.ds(peer, 1), :],
                    dst_ref=grads_ref.at[:, pl.ds(me, 1), :],
                    send_sem=gsend_sem, recv_sem=grecv_sem,
                    device_id=(peer,), device_id_type=MESH,
                ).start()

            return carry

        lax.fori_loop(0, BATCH, back, 0)
        return carry

    lax.fori_loop(0, batches, finish, 0)
    for p in range(9):
        grads_ref[p, pl.ds(me, 1), :] = gsend_ref[p, pl.ds(me, 1), :]

    lane_tile = same((stripe_tiles, LANES), lambda i: i, lambda j: j // span)
    pixel_row = same((pixels, rows), lambda i: i // span, lambda j: j)
    pixel_lane = same((pixels, LANES), lambda i: i & (span - 1), lambda j: j & (span - 1))
    flat = dot(lane_tile, dot(pixel_row, lossy_ref[...], selector=0) * pixel_lane, True, selector=0)
    for t in range(stripe_tiles):
        loss_ref[0:1, t * pixels:(t + 1) * pixels] = flat[t:t + 1]

    pltpu.make_async_remote_copy(
        src_ref=gsend_ref.at[:, everyone, :], dst_ref=grads_ref.at[:, everyone, :],
        send_sem=gsend_sem, recv_sem=grecv_sem, device_id=(me,), device_id_type=MESH,
    ).wait()


def chain_kernel(gauss_ref, depth_ref, moment_ref, loss_in, grads_ref, loss_out):
    loss_out[...] = loss_in[...]
    tile_count = depth_ref.shape[1]
    regions = moment_ref.shape[1]
    group = tile_count // regions * SPLATS
    per = LANES // group
    lane8 = iota((8, LANES), 1)
    for c in range(tile_count // LANES):
        part = slice(8 * c, 8 * c + 8)
        index = (lane8 & -SPLATS) + to_lanes(depth_ref[:, c * LANES:(c + 1) * LANES])
        x = [gauss_ref[p, part, :] for p in range(9)]
        sums = []
        for p in range(9):
            if per == 1:
                value = moment_ref[p, part, :]
            else:
                value = jnp.zeros((8, LANES), jnp.float32)
                for j in range(per):
                    piece = moment_ref[p, pl.ds(8 * c * per + j, 8, stride=per), :]
                    piece = pltpu.roll(piece, j * group, 1) if j else piece
                    value = jnp.where(lane8 // group == j, piece, value)
            sums.append(along_lanes(value, index))
        squash = jnp.tanh(x[4])
        rho = 0.9 * squash
        inv = 1.0 / (1.0 - rho * rho)
        inv_x, inv_y = jnp.exp(-x[2]), jnp.exp(-x[3])
        hu, hv = inv_x * sums[1], inv_y * sums[2]
        huu = inv_x * (inv_x * sums[3])
        huv = inv_x * (inv_y * sums[4])
        hvv = inv_y * (inv_y * sums[5])
        hq = inv * (huu - 2.0 * rho * huv + hvv)
        results = [
            inv_x * inv * (hu - rho * hv),
            inv_y * inv * (hv - rho * hu),
            inv * (huu - rho * huv),
            inv * (hvv - rho * huv),
            inv * (huv - rho * hq) * (0.9 * (1.0 - squash * squash)),
            sums[0] * jax.nn.sigmoid(-x[5]),
        ]
        for k in range(3):
            tone = jax.nn.sigmoid(x[6 + k])
            results.append(sums[6 + k] * tone * (1.0 - tone))
        for p in range(9):
            grads_ref[p, part, :] = results[p]


def shards(gaussians, depth, coverage, flips, features, w_first, b_first, w_second, target):
    regions = lax.axis_size("region")
    tile_count = depth.shape[1]
    stripe_tiles = tile_count // regions
    pixels = TSIDE * TSIDE
    rows = pixels * stripe_tiles // LANES
    nodes = 2 * regions - 1
    width = features.shape[1]
    f32, bf16 = jnp.float32, jnp.bfloat16
    vmem = pl.BlockSpec(memory_space=pltpu.VMEM)
    dma = pltpu.SemaphoreType.DMA
    dense = gaussians.reshape(9, tile_count * SPLATS // LANES, LANES)
    ranks = depth[0].T
    loss, moments = pl.pallas_call(
        splat_kernel,
        out_shape=(
            jax.ShapeDtypeStruct((1, stripe_tiles * pixels), f32),
            jax.ShapeDtypeStruct((9, regions, LANES), f32),
        ),
        in_specs=[vmem] * 4 + [pl.BlockSpec(memory_space=pl.ANY)] + [vmem] * 4,
        out_specs=(vmem, vmem),
        scratch_shapes=[
            pltpu.VMEM((stripe_tiles, pixels, width), features.dtype),
            dma(()),
            pltpu.VMEM((9, regions, LANES), f32),
            pltpu.VMEM((9, regions, LANES), f32),
            dma(()),
            dma(()),
            pltpu.VMEM((9, regions, LANES), f32),
            dma(()),
            dma(()),
            pltpu.VMEM((regions - 1, LANES), f32),
            pltpu.VMEM((rows, LANES), f32),
            pltpu.VMEM((3, rows, LANES), f32),
            pltpu.VMEM((NPAR * SPLATS * regions, LANES), f32),
            pltpu.VMEM((regions * SPLATS, rows, LANES), f32),
            pltpu.VMEM((regions * SPLATS, rows, LANES), f32),
            pltpu.VMEM((nodes, 4, rows, LANES), f32),
            pltpu.VMEM((nodes, 2, rows, LANES), f32),
            pltpu.VMEM((3, rows, LANES), f32),
            pltpu.VMEM((rows, LANES), f32),
            pltpu.VMEM((SPLATS * rows, 4 * LANES), bf16),
            pltpu.VMEM((9 * BATCH * SPLATS, LANES), f32),
            pltpu.VMEM((NMOM * SPLATS, SPLATS * rows), bf16),
            pltpu.VMEM((SPLATS * LANES, LANES), bf16),
        ],
        compiler_params=pltpu.CompilerParams(
            vmem_limit_bytes=56 * 1024 * 1024, collective_id=0, has_side_effects=True
        ),
    )(
        dense,
        ranks,
        coverage,
        flips.T,
        features.reshape(stripe_tiles, pixels, width),
        w_first,
        b_first,
        w_second,
        target,
    )
    grads, loss = pl.pallas_call(
        chain_kernel,
        out_shape=(
            jax.ShapeDtypeStruct(dense.shape, f32), jax.ShapeDtypeStruct(loss.shape, f32)
        ),
        in_specs=[vmem] * 4,
        out_specs=(vmem, vmem),
    )(dense, ranks, moments, loss)
    return (loss.reshape(-1), grads.reshape(gaussians.shape))


def solution(mesh):
    placed = (
        P("region", None, None),
        P("region", None, None),
        P("region", None),
        P(),
        P("region", None),
        P(),
        P(),
        P(),
        P(None, "region"),
    )
    return jax.shard_map(
        shards,
        mesh=mesh,
        in_specs=placed,
        out_specs=(P("region"), P("region", None, None)),
        check_vma=False,
    )
```

```python
import jax
import jax.numpy as jnp
from jax import lax
from jax.experimental import pallas as pl
from jax.experimental.pallas import tpu as pltpu
from jax.sharding import PartitionSpec as P

TSIDE = 16
LANES = 128
SPLATS = 8
NPAR = 9
NMOM = 6
BATCH = 8
EARLY = 4
LOWEST = -1e4
CHUNK = 32
LOG2E = 1.4426950408889634
MESH = pl.DeviceIdType.MESH


def iota(shape, dim):
    return lax.broadcasted_iota(jnp.int32, shape, dim)


def dot(x, y, transposed=False, selector=1, pieces=3):
    dims = (((1,), (1 if transposed else 0,)), ((), ()))
    bf16 = jnp.bfloat16
    sel, val = (y, x) if selector == 1 else (x, y)
    sel = sel.astype(bf16)
    total = None
    for _ in range(pieces):
        piece = val.astype(bf16)
        val = val - piece.astype(jnp.float32)
        pair = (piece, sel) if selector == 1 else (sel, piece)
        part = lax.dot_general(*pair, dims, preferred_element_type=jnp.float32)
        total = part if total is None else total + part
    return total


def same(shape, first, second):
    return (first(iota(shape, 0)) == second(iota(shape, 1))).astype(jnp.float32)


def along_lanes(x, index):
    return jnp.take_along_axis(x, index, axis=1)


def to_lanes(x):
    row, lane = iota((8, LANES), 0), iota((8, LANES), 1)
    x = along_lanes(x, ((lane // 16 - row) & 7) * 16 + (lane & 15))
    x = jnp.take_along_axis(x, (lane // 16 - row) & 7, axis=0)
    return along_lanes(x, ((row + (lane & 7)) & 7) * 16 + lane // 8)


def splat_kernel(
    gauss_ref, depth_ref, cover_ref, flips_ref, feat_hbm, first_ref, bias_ref, second_ref,
    target_ref, loss_ref, grads_ref,
    feat_ref, feat_sem, send_ref, recv_ref, send_sem, recv_sem, gsend_ref, gsend_sem,
    grecv_sem, flip_ref, spread_ref, wanted_ref,
    ex_ref, a_ref, w_ref, tree_ref, down_ref, g_ref, lossy_ref, rhs_ref, tone_ref, stage_ref,
    basis_ref, ones_ref, fold_ref, widen_ref,
):
    regions = recv_ref.shape[1]
    rows = wanted_ref.shape[1]
    nv = rows // 8
    tile_count = depth_ref.shape[1]
    stripe_tiles = tile_count // regions
    group = stripe_tiles * SPLATS
    per = LANES // group
    span = LANES // stripe_tiles
    inner = regions - 1
    batches = regions // BATCH
    pixels = TSIDE * TSIDE
    f32, bf16 = jnp.float32, jnp.bfloat16
    me = lax.axis_index("region")

    load = pltpu.make_async_copy(feat_hbm, feat_ref, feat_sem)
    load.start()
    barrier = pltpu.get_barrier_semaphore()

    def greet(i, carry):
        pl.semaphore_signal(
            barrier, inc=1, device_id=(lax.rem(me + i, regions),), device_id_type=MESH
        )
        return carry

    lax.fori_loop(1, regions, greet, 0)

    row8, lane8 = iota((8, LANES), 0), iota((8, LANES), 1)

    for c in range(tile_count // LANES):
        tiles = slice(c * LANES, (c + 1) * LANES)
        order = jnp.zeros((SPLATS, LANES), jnp.int32)
        for g in range(SPLATS):
            order = jnp.where(depth_ref[g:g + 1, tiles] == row8, g, order)
        index = (lane8 & -SPLATS) + to_lanes(order)
        cover = along_lanes(
            jnp.broadcast_to(cover_ref[:, tiles], (8, LANES)), row8 * 16 + lane8 // SPLATS
        )
        part = slice(8 * c, 8 * c + 8)
        x = [gauss_ref[p, part, :] for p in range(9)]
        rho = 0.9 * jnp.tanh(x[4])
        scale = (0.5 * LOG2E) ** 0.5
        norm = lax.rsqrt(1.0 - rho * rho) * scale
        inv_y = jnp.exp(-x[3])
        values = [
            x[0],
            x[1],
            jnp.exp(-x[2]) * norm,
            inv_y * (rho * norm),
            inv_y * scale,
            0.99 * jax.nn.sigmoid(x[5]),
            jax.nn.sigmoid(x[6]),
            jax.nn.sigmoid(x[7]),
            jax.nn.sigmoid(x[8]),
        ]
        for p in range(9):
            value = along_lanes(values[p], index)
            if p == 5:
                value = jnp.maximum(jnp.log2(value * cover.astype(f32)), LOWEST)
            for j in range(per):
                shifted = pltpu.roll(value, LANES - j * group, 1) if j else value
                if per == 1:
                    send_ref[p, part, :] = shifted
                else:
                    send_ref[p, pl.ds(8 * c * per + j, 8, stride=per), :] = shifted

    bias = bias_ref[...].reshape(1, bias_ref.shape[0])
    second = jnp.broadcast_to(
        second_ref[...].astype(f32).reshape(1, second_ref.shape[0]), (16, second_ref.shape[0])
    ).astype(bf16)

    block = max(16, span)
    per_block = block // span

    def network(j, carry):
        feats = feat_ref[:, pl.ds(pl.multiple_of(j * block, block), block), :]
        feats = feats.reshape(stripe_tiles * block, feat_ref.shape[2])
        hidden = jax.nn.gelu(
            jnp.dot(feats, first_ref[...], preferred_element_type=f32) + bias
        )
        hidden = hidden.reshape(stripe_tiles, per_block, span, hidden.shape[-1])
        for i in range(per_block):
            part = hidden[:, i].reshape(LANES, hidden.shape[-1]).astype(bf16)
            logits = lax.dot_general(
                second, part, (((1,), (1,)), ((), ())), preferred_element_type=f32,
            )
            spread_ref[pl.ds(j * per_block + i, 1), :] = logits[0:1]
        return carry

    steps = pixels // block
    early = min(EARLY, steps // 2)
    load.wait()
    if early:
        lax.fori_loop(0, early, network, 0, unroll=2)
    pl.semaphore_wait(barrier, regions - 1)

    def send(i, carry):
        peer = lax.rem(me + i, regions)
        pltpu.make_async_remote_copy(
            src_ref=send_ref.at[:, pl.ds(peer, 1), :], dst_ref=recv_ref.at[:, pl.ds(me, 1), :],
            send_sem=send_sem, recv_sem=recv_sem, device_id=(peer,), device_id_type=MESH,
        ).start()
        return carry

    lax.fori_loop(1, regions, send, 0)
    for p in range(9):
        recv_ref[p, pl.ds(me, 1), :] = send_ref[p, pl.ds(me, 1), :]
    lax.fori_loop(early, steps, network, 0, unroll=2)

    tile_lane = same((LANES, stripe_tiles), lambda i: i // span, lambda j: j)
    lane_pixel = same((LANES, pixels), lambda i: i & (span - 1), lambda j: j & (span - 1))
    row_pixel = same((rows, pixels), lambda i: i, lambda j: j // span)
    for k in range(3):
        flat = jnp.concatenate(
            [target_ref[k:k + 1, t * pixels:(t + 1) * pixels] for t in range(stripe_tiles)], 0
        )
        wanted_ref[k] = dot(row_pixel, dot(tile_lane, flat, selector=0) * lane_pixel, True, selector=0)
    my_tiles = same(
        (tile_count, LANES), lambda i: i - me * stripe_tiles, lambda j: j // span
    ).astype(bf16)
    flip_ref[...] = jnp.dot(
        flips_ref[...].astype(f32).astype(bf16), my_tiles, preferred_element_type=f32,
    )

    wide = min(span, TSIDE)
    half = (TSIDE - wide) / 2

    def x_row(i):
        return ((i * span) & (TSIDE - 1)).astype(f32) - half

    def y_row(i):
        return (i * span // TSIDE).astype(f32) - 7.5

    x_lane = (lane8 & (wide - 1)).astype(f32) + (half + 0.5)
    y_lane = ((lane8 & (span - 1)) // TSIDE).astype(f32) + 8.0
    depth_rows = SPLATS * rows
    at = iota((SPLATS, depth_rows), 1)
    mine = at // rows == iota((SPLATS, depth_rows), 0)
    xr, yr = x_row(at & (rows - 1)), y_row(at & (rows - 1))
    terms = [jnp.ones_like(xr), xr, yr, xr * xr, xr * yr, yr * yr]
    basis_ref[...] = jnp.concatenate([jnp.where(mine, term, 0.0) for term in terms], 0).astype(bf16)
    ones_ref[...] = (
        iota(ones_ref.shape, 1) // 8 == iota(ones_ref.shape, 0)
    ).astype(f32).astype(bf16)
    for s in range(SPLATS):
        fold_ref[s * LANES:(s + 1) * LANES, :] = same(
            (LANES, LANES), lambda i: i // span * SPLATS + s, lambda j: j
        ).astype(bf16)

    for s in range(SPLATS):
        picks = same((LANES, LANES), lambda i: i, lambda j: j // span * SPLATS + s).astype(bf16)
        for k in range(3):
            widen_ref[k * LANES:(k + 1) * LANES, s * LANES:(s + 1) * LANES] = picks
    for buf in (rhs_ref, tone_ref):
        buf[...] = jnp.zeros(buf.shape, bf16)

    everyone = pl.ds(0, regions - 1)
    pltpu.make_async_remote_copy(
        src_ref=send_ref.at[:, everyone, :], dst_ref=recv_ref.at[:, everyone, :],
        send_sem=send_sem, recv_sem=recv_sem, device_id=(me,), device_id_type=MESH,
    ).wait()

    chunk = min(CHUNK, regions)

    def expand(c, carry):
        base = pl.multiple_of(c * chunk, chunk)
        value = jnp.concatenate(
            [recv_ref[p, pl.ds(base, chunk), :] for p in range(NPAR)], 0
        )
        pieces = []
        for _ in range(3):
            piece = value.astype(bf16)
            value = value - piece.astype(f32)
            pieces.append(piece)
        spread = jnp.dot(
            jnp.concatenate(pieces, 1), widen_ref[...], preferred_element_type=f32
        )
        for p in range(NPAR):
            for s in range(SPLATS):
                lanes = slice(s * LANES, (s + 1) * LANES)
                for b in range(chunk // BATCH):
                    first = pl.multiple_of(
                        ((c * (chunk // BATCH) + b) * NPAR + p) * SPLATS * BATCH, BATCH
                    ) + s * BATCH
                    ex_ref[pl.ds(first, BATCH), :] = spread[
                        p * chunk + b * BATCH:p * chunk + (b + 1) * BATCH, lanes
                    ]
        return carry

    lax.fori_loop(0, regions // chunk, expand, 0)

    vs = [slice(8 * v, 8 * v + 8) for v in range(nv)]
    xpos = x_row(row8) + x_lane
    ypos = [y_row(row8 + 8 * v) + y_lane for v in range(nv)]

    def first_row(r, p):
        return (r // BATCH * NPAR + p) * (SPLATS * BATCH) + (r & (BATCH - 1))

    def row(r, p, s):
        return ex_ref[pl.ds(first_row(r, p) + s * BATCH, 1), :]

    def forward(r, carry):
        trans = [jnp.ones((8, LANES), f32)] * nv
        color = [[jnp.zeros((8, LANES), f32)] * nv for _ in range(3)]
        for s in range(SPLATS):
            us = (xpos - row(r, 0, s)) * row(r, 2, s)
            m_y, skew, inv_y, level = row(r, 1, s), row(r, 3, s), row(r, 4, s), row(r, 5, s)
            ks = [row(r, 6 + k, s) for k in range(3)]
            for v in range(nv):
                dy = ypos[v] - m_y
                w = dy * inv_y
                p = us - dy * skew
                alpha = jnp.exp2(level - (p * p + w * w))
                weight = trans[v] * alpha
                a_ref[r * SPLATS + s, vs[v]] = alpha
                w_ref[r * SPLATS + s, vs[v]] = weight
                for k in range(3):
                    color[k][v] = color[k][v] + weight * ks[k]
                trans[v] = trans[v] - weight
        for v in range(nv):
            for k in range(3):
                tree_ref[inner + r, k, vs[v]] = color[k][v]
            tree_ref[inner + r, 3, vs[v]] = trans[v]
        return carry

    lax.fori_loop(0, regions, forward, 0)

    def flipped(n):
        return jnp.broadcast_to(flip_ref[pl.ds(n, 1), :], (8, LANES)) > 0.0

    def merge(n):
        flip = flipped(n)
        for v in range(nv):
            low = [tree_ref[2 * n + 1, k, vs[v]] for k in range(4)]
            high = [tree_ref[2 * n + 2, k, vs[v]] for k in range(4)]
            over_low = jnp.where(flip, high[3], 1.0)
            over_high = jnp.where(flip, 1.0, low[3])
            for k in range(3):
                tree_ref[n, k, vs[v]] = over_low * low[k] + over_high * high[k]
            tree_ref[n, 3, vs[v]] = low[3] * high[3]

    for n in reversed(range(inner)):
        merge(n)

    for v in range(nv):
        logit = spread_ref[vs[v]]
        spread = 0.5 + jnp.maximum(logit, 0.0) + jnp.log1p(jnp.exp(-jnp.abs(logit)))
        inv_square = 1.0 / (spread * spread)
        clear = tree_ref[0, 3, vs[v]]
        residual = [tree_ref[0, k, vs[v]] + clear - wanted_ref[k, vs[v]] for k in range(3)]
        total = residual[0] * residual[0] + residual[1] * residual[1] + residual[2] * residual[2]
        lossy_ref[vs[v]] = 0.5 * total * inv_square + jnp.log(spread)
        gs = [res * inv_square for res in residual]
        for k in range(3):
            g_ref[k, vs[v]] = gs[k]
        down_ref[0, 0, vs[v]] = jnp.ones((8, LANES), f32)
        down_ref[0, 1, vs[v]] = gs[0] + gs[1] + gs[2]

    def split(n):
        flip = flipped(n)
        for v in range(nv):
            low = [tree_ref[2 * n + 1, k, vs[v]] for k in range(4)]
            high = [tree_ref[2 * n + 2, k, vs[v]] for k in range(4)]
            g = [g_ref[k, vs[v]] for k in range(3)]
            front, behind = down_ref[n, 0, vs[v]], down_ref[n, 1, vs[v]]
            back = [jnp.where(flip, l, h) for l, h in zip(low, high)]
            through = front * jnp.where(flip, high[3], low[3])
            value = g[0] * back[0] + g[1] * back[1] + g[2] * back[2] + back[3] * behind
            down_ref[2 * n + 1, 0, vs[v]] = jnp.where(flip, through, front)
            down_ref[2 * n + 2, 0, vs[v]] = jnp.where(flip, front, through)
            down_ref[2 * n + 1, 1, vs[v]] = jnp.where(flip, behind, value)
            down_ref[2 * n + 2, 1, vs[v]] = jnp.where(flip, value, behind)

    for n in range(inner):
        split(n)

    def backward(r, slot):
        front = [down_ref[inner + r, 0, vs[v]] for v in range(nv)]
        gs = [[front[v] * g_ref[k, vs[v]] for v in range(nv)] for k in range(3)]
        behind = [front[v] * down_ref[inner + r, 1, vs[v]] for v in range(nv)]
        colors = [[], [], []]
        for s in reversed(range(SPLATS)):
            ks = [row(r, 6 + k, s) for k in range(3)]
            pulls, tones = [], [None] * 3
            for v in range(nv):
                alpha = a_ref[r * SPLATS + s, vs[v]]
                weight = w_ref[r * SPLATS + s, vs[v]]
                shade = ks[0] * gs[0][v] + ks[1] * gs[1][v] + ks[2] * gs[2][v]
                diff = shade - behind[v]
                behind[v] = behind[v] + alpha * diff
                pulls.append(weight * diff)
                for k in range(3):
                    tone = weight * gs[k][v]
                    tones[k] = tone if v == 0 else tones[k] + tone
            rhs_ref[slot, s * rows:(s + 1) * rows, :] = jnp.concatenate(pulls, 0).astype(bf16)
            for k in range(3):
                colors[k].insert(0, tones[k])
            if s % 2 == 0:
                for k in range(3):
                    tone_ref[slot, s * 8:(s + 2) * 8, k * LANES:(k + 1) * LANES] = (
                        jnp.concatenate(colors[k][:2], 0).astype(bf16)
                    )

    def reduce(r, slot):
        summed = jnp.dot(basis_ref[...], rhs_ref[slot], preferred_element_type=f32)
        toned = jnp.dot(ones_ref[...], tone_ref[slot], preferred_element_type=f32)
        h, hx, hy, hxx, hxy, hyy = [
            summed[b * SPLATS:(b + 1) * SPLATS] for b in range(NMOM)
        ]
        dx = x_lane - ex_ref[pl.ds(first_row(r, 0), SPLATS, stride=BATCH), :]
        dy = y_lane - ex_ref[pl.ds(first_row(r, 1), SPLATS, stride=BATCH), :]
        about_x = hx + dx * h
        about_y = hy + dy * h
        moments = [
            h,
            about_x,
            about_y,
            hxx + dx * (hx + about_x),
            hxy + dx * hy + dy * about_x,
            hyy + dy * (hy + about_y),
        ]
        for k in range(3):
            moments.append(toned[0:SPLATS, k * LANES:(k + 1) * LANES])
        for p in range(9):
            first = p * SPLATS * BATCH + (r & (BATCH - 1))
            stage_ref[pl.ds(first, SPLATS, stride=BATCH), :] = moments[p]

    def finish(i, carry):
        which = lax.rem(i + 1 + me // BATCH, batches)
        base = pl.multiple_of(which * BATCH, BATCH)

        def pair(j, carry):
            r = base + 2 * j
            before = base + 2 * jnp.maximum(j - 1, 0)
            for k in range(2):
                reduce(before + k, k)
            for k in range(2):
                backward(r + k, k)
            return carry

        lax.fori_loop(0, BATCH // 2, pair, 0)
        for k in range(2):
            reduce(base + BATCH - 2 + k, k)
        wide = [
            jnp.concatenate(
                [stage_ref[(p * SPLATS + s) * BATCH:(p * SPLATS + s + 1) * BATCH, :] for s in range(SPLATS)], 1
            )
            for p in range(9)
        ]
        folded = dot(jnp.concatenate(wide, 0), fold_ref[...], pieces=2)
        for p in range(9):
            gsend_ref[p, pl.ds(base, BATCH), :] = folded[p * BATCH:(p + 1) * BATCH]

        def back(j, carry):
            peer = base + j

            @pl.when(peer != me)
            def _():
                pltpu.make_async_remote_copy(
                    src_ref=gsend_ref.at[:, pl.ds(peer, 1), :],
                    dst_ref=grads_ref.at[:, pl.ds(me, 1), :],
                    send_sem=gsend_sem, recv_sem=grecv_sem,
                    device_id=(peer,), device_id_type=MESH,
                ).start()

            return carry

        lax.fori_loop(0, BATCH, back, 0)
        return carry

    lax.fori_loop(0, batches, finish, 0)
    for p in range(9):
        grads_ref[p, pl.ds(me, 1), :] = gsend_ref[p, pl.ds(me, 1), :]

    lane_tile = same((stripe_tiles, LANES), lambda i: i, lambda j: j // span)
    pixel_row = same((pixels, rows), lambda i: i // span, lambda j: j)
    pixel_lane = same((pixels, LANES), lambda i: i & (span - 1), lambda j: j & (span - 1))
    flat = dot(lane_tile, dot(pixel_row, lossy_ref[...], selector=0) * pixel_lane, True, selector=0)
    for t in range(stripe_tiles):
        loss_ref[0:1, t * pixels:(t + 1) * pixels] = flat[t:t + 1]

    pltpu.make_async_remote_copy(
        src_ref=gsend_ref.at[:, everyone, :], dst_ref=grads_ref.at[:, everyone, :],
        send_sem=gsend_sem, recv_sem=grecv_sem, device_id=(me,), device_id_type=MESH,
    ).wait()


def chain_kernel(gauss_ref, depth_ref, moment_ref, loss_in, grads_ref, loss_out):
    loss_out[...] = loss_in[...]
    tile_count = depth_ref.shape[1]
    regions = moment_ref.shape[1]
    group = tile_count // regions * SPLATS
    per = LANES // group
    lane8 = iota((8, LANES), 1)
    for c in range(tile_count // LANES):
        part = slice(8 * c, 8 * c + 8)
        index = (lane8 & -SPLATS) + to_lanes(depth_ref[:, c * LANES:(c + 1) * LANES])
        x = [gauss_ref[p, part, :] for p in range(9)]
        sums = []
        for p in range(9):
            if per == 1:
                value = moment_ref[p, part, :]
            else:
                value = jnp.zeros((8, LANES), jnp.float32)
                for j in range(per):
                    piece = moment_ref[p, pl.ds(8 * c * per + j, 8, stride=per), :]
                    piece = pltpu.roll(piece, j * group, 1) if j else piece
                    value = jnp.where(lane8 // group == j, piece, value)
            sums.append(along_lanes(value, index))
        squash = jnp.tanh(x[4])
        rho = 0.9 * squash
        inv = 1.0 / (1.0 - rho * rho)
        inv_x, inv_y = jnp.exp(-x[2]), jnp.exp(-x[3])
        hu, hv = inv_x * sums[1], inv_y * sums[2]
        huu = inv_x * (inv_x * sums[3])
        huv = inv_x * (inv_y * sums[4])
        hvv = inv_y * (inv_y * sums[5])
        hq = inv * (huu - 2.0 * rho * huv + hvv)
        results = [
            inv_x * inv * (hu - rho * hv),
            inv_y * inv * (hv - rho * hu),
            inv * (huu - rho * huv),
            inv * (hvv - rho * huv),
            inv * (huv - rho * hq) * (0.9 * (1.0 - squash * squash)),
            sums[0] * jax.nn.sigmoid(-x[5]),
        ]
        for k in range(3):
            tone = jax.nn.sigmoid(x[6 + k])
            results.append(sums[6 + k] * tone * (1.0 - tone))
        for p in range(9):
            grads_ref[p, part, :] = results[p]


def shards(gaussians, depth, coverage, flips, features, w_first, b_first, w_second, target):
    regions = lax.axis_size("region")
    tile_count = depth.shape[1]
    stripe_tiles = tile_count // regions
    pixels = TSIDE * TSIDE
    rows = pixels * stripe_tiles // LANES
    nodes = 2 * regions - 1
    width = features.shape[1]
    f32, bf16 = jnp.float32, jnp.bfloat16
    vmem = pl.BlockSpec(memory_space=pltpu.VMEM)
    dma = pltpu.SemaphoreType.DMA
    dense = gaussians.reshape(9, tile_count * SPLATS // LANES, LANES)
    ranks = depth[0].T
    loss, moments = pl.pallas_call(
        splat_kernel,
        out_shape=(
            jax.ShapeDtypeStruct((1, stripe_tiles * pixels), f32),
            jax.ShapeDtypeStruct((9, regions, LANES), f32),
        ),
        in_specs=[vmem] * 4 + [pl.BlockSpec(memory_space=pl.ANY)] + [vmem] * 4,
        out_specs=(vmem, vmem),
        scratch_shapes=[
            pltpu.VMEM((stripe_tiles, pixels, width), features.dtype),
            dma(()),
            pltpu.VMEM((9, regions, LANES), f32),
            pltpu.VMEM((9, regions, LANES), f32),
            dma(()),
            dma(()),
            pltpu.VMEM((9, regions, LANES), f32),
            dma(()),
            dma(()),
            pltpu.VMEM((regions - 1, LANES), f32),
            pltpu.VMEM((rows, LANES), f32),
            pltpu.VMEM((3, rows, LANES), f32),
            pltpu.VMEM((NPAR * SPLATS * regions, LANES), f32),
            pltpu.VMEM((regions * SPLATS, rows, LANES), f32),
            pltpu.VMEM((regions * SPLATS, rows, LANES), f32),
            pltpu.VMEM((nodes, 4, rows, LANES), f32),
            pltpu.VMEM((nodes, 2, rows, LANES), f32),
            pltpu.VMEM((3, rows, LANES), f32),
            pltpu.VMEM((rows, LANES), f32),
            pltpu.VMEM((2, SPLATS * rows, LANES), bf16),
            pltpu.VMEM((2, SPLATS * 8, 3 * LANES), bf16),
            pltpu.VMEM((9 * BATCH * SPLATS, LANES), f32),
            pltpu.VMEM((NMOM * SPLATS, SPLATS * rows), bf16),
            pltpu.VMEM((16, SPLATS * 8), bf16),
            pltpu.VMEM((SPLATS * LANES, LANES), bf16),
            pltpu.VMEM((3 * LANES, SPLATS * LANES), bf16),
        ],
        compiler_params=pltpu.CompilerParams(
            vmem_limit_bytes=56 * 1024 * 1024, collective_id=0, has_side_effects=True
        ),
    )(
        dense,
        ranks,
        coverage,
        flips.T,
        features.reshape(stripe_tiles, pixels, width),
        w_first,
        b_first,
        w_second,
        target,
    )
    grads, loss = pl.pallas_call(
        chain_kernel,
        out_shape=(
            jax.ShapeDtypeStruct(dense.shape, f32), jax.ShapeDtypeStruct(loss.shape, f32)
        ),
        in_specs=[vmem] * 4,
        out_specs=(vmem, vmem),
    )(dense, ranks, moments, loss)
    return (loss.reshape(-1), grads.reshape(gaussians.shape))


def solution(mesh):
    placed = (
        P("region", None, None),
        P("region", None, None),
        P("region", None),
        P(),
        P("region", None),
        P(),
        P(),
        P(),
        P(None, "region"),
    )
    return jax.shard_map(
        shards,
        mesh=mesh,
        in_specs=placed,
        out_specs=(P("region"), P("region", None, None)),
        check_vma=False,
    )
```

```python
import jax
import jax.numpy as jnp
from jax import lax
from jax.experimental import pallas as pl
from jax.experimental.pallas import tpu as pltpu
from jax.sharding import PartitionSpec as P

TSIDE = 16
LANES = 128
SPLATS = 8
NPAR = 9
NMOM = 6
BATCH = 8
EARLY = 4
LOWEST = -1e4
CHUNK = 32
LOG2E = 1.4426950408889634
MESH = pl.DeviceIdType.MESH


def iota(shape, dim):
    return lax.broadcasted_iota(jnp.int32, shape, dim)


def dot(x, y, transposed=False, selector=1, pieces=3):
    dims = (((1,), (1 if transposed else 0,)), ((), ()))
    bf16 = jnp.bfloat16
    sel, val = (y, x) if selector == 1 else (x, y)
    sel = sel.astype(bf16)
    total = None
    for _ in range(pieces):
        piece = val.astype(bf16)
        val = val - piece.astype(jnp.float32)
        pair = (piece, sel) if selector == 1 else (sel, piece)
        part = lax.dot_general(*pair, dims, preferred_element_type=jnp.float32)
        total = part if total is None else total + part
    return total


def same(shape, first, second):
    return (first(iota(shape, 0)) == second(iota(shape, 1))).astype(jnp.float32)


def along_lanes(x, index):
    return jnp.take_along_axis(x, index, axis=1)


def to_lanes(x):
    row, lane = iota((8, LANES), 0), iota((8, LANES), 1)
    x = along_lanes(x, ((lane // 16 - row) & 7) * 16 + (lane & 15))
    x = jnp.take_along_axis(x, (lane // 16 - row) & 7, axis=0)
    return along_lanes(x, ((row + (lane & 7)) & 7) * 16 + lane // 8)


def splat_kernel(
    gauss_hbm, depth_hbm, cover_hbm, flips_hbm, feat_hbm, first_hbm, bias_hbm, second_hbm,
    target_hbm, loss_hbm, grads_hbm,
    gauss_ref, depth_ref, cover_ref, flips_ref, feat_ref, first_ref, bias_ref, second_ref,
    target_ref, load_sem, loss_ref, loss_sem, own_sem, send_ref, recv_ref, send_sem, recv_sem, gsend_ref, gsend_sem,
    grecv_sem, flip_ref, spread_ref, wanted_ref,
    ex_ref, a_ref, w_ref, tree_ref, down_ref, g_ref, lossy_ref, rhs_ref, tone_ref, stage_ref,
    basis_ref, ones_ref, fold_ref, widen_ref,
):
    regions = recv_ref.shape[1]
    rows = wanted_ref.shape[1]
    nv = rows // 8
    tile_count = depth_ref.shape[1]
    stripe_tiles = tile_count // regions
    group = stripe_tiles * SPLATS
    per = LANES // group
    span = LANES // stripe_tiles
    inner = regions - 1
    batches = regions // BATCH
    pixels = TSIDE * TSIDE
    f32, bf16 = jnp.float32, jnp.bfloat16
    me = lax.axis_index("region")

    barrier = pltpu.get_barrier_semaphore()

    def greet(i, carry):
        pl.semaphore_signal(
            barrier, inc=1, device_id=(lax.rem(me + i, regions),), device_id_type=MESH
        )
        return carry

    lax.fori_loop(1, regions, greet, 0)
    pairs = [
        (gauss_hbm, gauss_ref), (depth_hbm, depth_ref), (cover_hbm, cover_ref),
        (feat_hbm, feat_ref), (first_hbm, first_ref), (bias_hbm, bias_ref),
        (second_hbm, second_ref), (target_hbm, target_ref), (flips_hbm, flips_ref),
    ]
    loads = [pltpu.make_async_copy(*x, load_sem.at[i]) for i, x in enumerate(pairs)]
    for load in loads:
        load.start()
    for load in loads[:3]:
        load.wait()

    row8, lane8 = iota((8, LANES), 0), iota((8, LANES), 1)

    for c in range(tile_count // LANES):
        tiles = slice(c * LANES, (c + 1) * LANES)
        order = jnp.zeros((SPLATS, LANES), jnp.int32)
        for g in range(SPLATS):
            order = jnp.where(depth_ref[g:g + 1, tiles] == row8, g, order)
        index = (lane8 & -SPLATS) + to_lanes(order)
        cover = along_lanes(
            jnp.broadcast_to(cover_ref[:, tiles], (8, LANES)), row8 * 16 + lane8 // SPLATS
        )
        part = slice(8 * c, 8 * c + 8)
        x = [gauss_ref[p, part, :] for p in range(9)]
        rho = 0.9 * jnp.tanh(x[4])
        scale = (0.5 * LOG2E) ** 0.5
        norm = lax.rsqrt(1.0 - rho * rho) * scale
        inv_y = jnp.exp(-x[3])
        values = [
            x[0],
            x[1],
            jnp.exp(-x[2]) * norm,
            inv_y * (rho * norm),
            inv_y * scale,
            0.99 * jax.nn.sigmoid(x[5]),
            jax.nn.sigmoid(x[6]),
            jax.nn.sigmoid(x[7]),
            jax.nn.sigmoid(x[8]),
        ]
        for p in range(9):
            value = along_lanes(values[p], index)
            if p == 5:
                value = jnp.maximum(jnp.log2(value * cover.astype(f32)), LOWEST)
            for j in range(per):
                shifted = pltpu.roll(value, LANES - j * group, 1) if j else value
                if per == 1:
                    send_ref[p, part, :] = shifted
                else:
                    send_ref[p, pl.ds(8 * c * per + j, 8, stride=per), :] = shifted

    for load in loads[3:7]:
        load.wait()
    bias = bias_ref[...].reshape(1, bias_ref.shape[0])
    second = jnp.broadcast_to(
        second_ref[...].astype(f32).reshape(1, second_ref.shape[0]), (16, second_ref.shape[0])
    ).astype(bf16)

    block = max(16, span)
    per_block = block // span

    def network(j, carry):
        feats = feat_ref[:, pl.ds(pl.multiple_of(j * block, block), block), :]
        feats = feats.reshape(stripe_tiles * block, feat_ref.shape[2])
        hidden = jax.nn.gelu(
            jnp.dot(feats, first_ref[...], preferred_element_type=f32) + bias
        )
        hidden = hidden.reshape(stripe_tiles, per_block, span, hidden.shape[-1])
        for i in range(per_block):
            part = hidden[:, i].reshape(LANES, hidden.shape[-1]).astype(bf16)
            logits = lax.dot_general(
                second, part, (((1,), (1,)), ((), ())), preferred_element_type=f32,
            )
            spread_ref[pl.ds(j * per_block + i, 1), :] = logits[0:1]
        return carry

    steps = pixels // block
    early = min(EARLY, steps // 2)
    if early:
        lax.fori_loop(0, early, network, 0, unroll=4)
    pl.semaphore_wait(barrier, regions - 1)

    def send(i, carry):
        peer = lax.rem(me + i, regions)
        pltpu.make_async_remote_copy(
            src_ref=send_ref.at[:, pl.ds(peer, 1), :], dst_ref=recv_ref.at[:, pl.ds(me, 1), :],
            send_sem=send_sem, recv_sem=recv_sem, device_id=(peer,), device_id_type=MESH,
        ).start()
        return carry

    lax.fori_loop(1, regions, send, 0)
    for p in range(9):
        recv_ref[p, pl.ds(me, 1), :] = send_ref[p, pl.ds(me, 1), :]
    lax.fori_loop(early, steps, network, 0, unroll=4)

    for load in loads[7:]:
        load.wait()
    tile_lane = same((LANES, stripe_tiles), lambda i: i // span, lambda j: j)
    lane_pixel = same((LANES, pixels), lambda i: i & (span - 1), lambda j: j & (span - 1))
    row_pixel = same((rows, pixels), lambda i: i, lambda j: j // span)
    for k in range(3):
        flat = jnp.concatenate(
            [target_ref[k:k + 1, t * pixels:(t + 1) * pixels] for t in range(stripe_tiles)], 0
        )
        wanted_ref[k] = dot(row_pixel, dot(tile_lane, flat, selector=0) * lane_pixel, True, selector=0)
    my_tiles = same(
        (tile_count, LANES), lambda i: i - me * stripe_tiles, lambda j: j // span
    ).astype(bf16)
    flip_ref[...] = jnp.dot(
        flips_ref[...].astype(f32).astype(bf16), my_tiles, preferred_element_type=f32,
    )

    wide = min(span, TSIDE)
    half = (TSIDE - wide) / 2

    def x_row(i):
        return ((i * span) & (TSIDE - 1)).astype(f32) - half

    def y_row(i):
        return (i * span // TSIDE).astype(f32) - 7.5

    x_lane = (lane8 & (wide - 1)).astype(f32) + (half + 0.5)
    y_lane = ((lane8 & (span - 1)) // TSIDE).astype(f32) + 8.0
    depth_rows = SPLATS * rows
    at = iota((SPLATS, depth_rows), 1)
    mine = at // rows == iota((SPLATS, depth_rows), 0)
    xr, yr = x_row(at & (rows - 1)), y_row(at & (rows - 1))
    terms = [jnp.ones_like(xr), xr, yr, xr * xr, xr * yr, yr * yr]
    basis_ref[...] = jnp.concatenate([jnp.where(mine, term, 0.0) for term in terms], 0).astype(bf16)
    ones_ref[...] = (
        iota(ones_ref.shape, 1) // 8 == iota(ones_ref.shape, 0)
    ).astype(f32).astype(bf16)
    for s in range(SPLATS):
        fold_ref[s * LANES:(s + 1) * LANES, :] = same(
            (LANES, LANES), lambda i: i // span * SPLATS + s, lambda j: j
        ).astype(bf16)

    for s in range(SPLATS):
        picks = same((LANES, LANES), lambda i: i, lambda j: j // span * SPLATS + s).astype(bf16)
        for k in range(3):
            widen_ref[k * LANES:(k + 1) * LANES, s * LANES:(s + 1) * LANES] = picks
    for buf in (rhs_ref, tone_ref):
        buf[...] = jnp.zeros(buf.shape, bf16)

    everyone = pl.ds(0, regions - 1)
    pltpu.make_async_remote_copy(
        src_ref=send_ref.at[:, everyone, :], dst_ref=recv_ref.at[:, everyone, :],
        send_sem=send_sem, recv_sem=recv_sem, device_id=(me,), device_id_type=MESH,
    ).wait()

    chunk = min(CHUNK, regions)

    def expand(c, carry):
        base = pl.multiple_of(c * chunk, chunk)
        value = jnp.concatenate(
            [recv_ref[p, pl.ds(base, chunk), :] for p in range(NPAR)], 0
        )
        pieces = []
        for _ in range(3):
            piece = value.astype(bf16)
            value = value - piece.astype(f32)
            pieces.append(piece)
        spread = jnp.dot(
            jnp.concatenate(pieces, 1), widen_ref[...], preferred_element_type=f32
        )
        for p in range(NPAR):
            for s in range(SPLATS):
                lanes = slice(s * LANES, (s + 1) * LANES)
                for b in range(chunk // BATCH):
                    first = pl.multiple_of(
                        ((c * (chunk // BATCH) + b) * NPAR + p) * SPLATS * BATCH, BATCH
                    ) + s * BATCH
                    ex_ref[pl.ds(first, BATCH), :] = spread[
                        p * chunk + b * BATCH:p * chunk + (b + 1) * BATCH, lanes
                    ]
        return carry

    lax.fori_loop(0, regions // chunk, expand, 0)

    vs = [slice(8 * v, 8 * v + 8) for v in range(nv)]
    xpos = x_row(row8) + x_lane
    ypos = [y_row(row8 + 8 * v) + y_lane for v in range(nv)]

    def first_row(r, p):
        return (r // BATCH * NPAR + p) * (SPLATS * BATCH) + (r & (BATCH - 1))

    def row(r, p, s):
        return ex_ref[pl.ds(first_row(r, p) + s * BATCH, 1), :]

    def forward(r, carry):
        trans = [jnp.ones((8, LANES), f32)] * nv
        color = [[jnp.zeros((8, LANES), f32)] * nv for _ in range(3)]
        for s in range(SPLATS):
            us = (xpos - row(r, 0, s)) * row(r, 2, s)
            m_y, skew, inv_y, level = row(r, 1, s), row(r, 3, s), row(r, 4, s), row(r, 5, s)
            ks = [row(r, 6 + k, s) for k in range(3)]
            for v in range(nv):
                dy = ypos[v] - m_y
                w = dy * inv_y
                p = us - dy * skew
                alpha = jnp.exp2(level - (p * p + w * w))
                weight = trans[v] * alpha
                a_ref[r * SPLATS + s, vs[v]] = alpha
                w_ref[r * SPLATS + s, vs[v]] = weight
                for k in range(3):
                    color[k][v] = color[k][v] + weight * ks[k]
                trans[v] = trans[v] - weight
        for v in range(nv):
            for k in range(3):
                tree_ref[inner + r, k, vs[v]] = color[k][v]
            tree_ref[inner + r, 3, vs[v]] = trans[v]
        return carry

    lax.fori_loop(0, regions, forward, 0, unroll=2)

    def flipped(n):
        return jnp.broadcast_to(flip_ref[pl.ds(n, 1), :], (8, LANES)) > 0.0

    def merge(n):
        flip = flipped(n)
        for v in range(nv):
            low = [tree_ref[2 * n + 1, k, vs[v]] for k in range(4)]
            high = [tree_ref[2 * n + 2, k, vs[v]] for k in range(4)]
            over_low = jnp.where(flip, high[3], 1.0)
            over_high = jnp.where(flip, 1.0, low[3])
            for k in range(3):
                tree_ref[n, k, vs[v]] = over_low * low[k] + over_high * high[k]
            tree_ref[n, 3, vs[v]] = low[3] * high[3]

    for n in reversed(range(inner)):
        merge(n)

    for v in range(nv):
        logit = spread_ref[vs[v]]
        spread = 0.5 + jnp.maximum(logit, 0.0) + jnp.log1p(jnp.exp(-jnp.abs(logit)))
        inv_square = 1.0 / (spread * spread)
        clear = tree_ref[0, 3, vs[v]]
        residual = [tree_ref[0, k, vs[v]] + clear - wanted_ref[k, vs[v]] for k in range(3)]
        total = residual[0] * residual[0] + residual[1] * residual[1] + residual[2] * residual[2]
        lossy_ref[vs[v]] = 0.5 * total * inv_square + jnp.log(spread)
        gs = [res * inv_square for res in residual]
        for k in range(3):
            g_ref[k, vs[v]] = gs[k]
        down_ref[0, 0, vs[v]] = jnp.ones((8, LANES), f32)
        down_ref[0, 1, vs[v]] = gs[0] + gs[1] + gs[2]

    def split(n):
        flip = flipped(n)
        for v in range(nv):
            low = [tree_ref[2 * n + 1, k, vs[v]] for k in range(4)]
            high = [tree_ref[2 * n + 2, k, vs[v]] for k in range(4)]
            g = [g_ref[k, vs[v]] for k in range(3)]
            front, behind = down_ref[n, 0, vs[v]], down_ref[n, 1, vs[v]]
            back = [jnp.where(flip, l, h) for l, h in zip(low, high)]
            through = front * jnp.where(flip, high[3], low[3])
            value = g[0] * back[0] + g[1] * back[1] + g[2] * back[2] + back[3] * behind
            down_ref[2 * n + 1, 0, vs[v]] = jnp.where(flip, through, front)
            down_ref[2 * n + 2, 0, vs[v]] = jnp.where(flip, front, through)
            down_ref[2 * n + 1, 1, vs[v]] = jnp.where(flip, behind, value)
            down_ref[2 * n + 2, 1, vs[v]] = jnp.where(flip, value, behind)

    for n in range(inner):
        split(n)

    def backward(r, slot):
        front = [down_ref[inner + r, 0, vs[v]] for v in range(nv)]
        gs = [[front[v] * g_ref[k, vs[v]] for v in range(nv)] for k in range(3)]
        behind = [front[v] * down_ref[inner + r, 1, vs[v]] for v in range(nv)]
        colors = [[], [], []]
        for s in reversed(range(SPLATS)):
            ks = [row(r, 6 + k, s) for k in range(3)]
            pulls, tones = [], [None] * 3
            for v in range(nv):
                alpha = a_ref[r * SPLATS + s, vs[v]]
                weight = w_ref[r * SPLATS + s, vs[v]]
                shade = ks[0] * gs[0][v] + ks[1] * gs[1][v] + ks[2] * gs[2][v]
                diff = shade - behind[v]
                behind[v] = behind[v] + alpha * diff
                pulls.append(weight * diff)
                for k in range(3):
                    tone = weight * gs[k][v]
                    tones[k] = tone if v == 0 else tones[k] + tone
            rhs_ref[slot, s * rows:(s + 1) * rows, :] = jnp.concatenate(pulls, 0).astype(bf16)
            for k in range(3):
                colors[k].insert(0, tones[k])
            if s % 2 == 0:
                for k in range(3):
                    tone_ref[slot, s * 8:(s + 2) * 8, k * LANES:(k + 1) * LANES] = (
                        jnp.concatenate(colors[k][:2], 0).astype(bf16)
                    )

    def reduce(r, slot):
        summed = jnp.dot(basis_ref[...], rhs_ref[slot], preferred_element_type=f32)
        toned = jnp.dot(ones_ref[...], tone_ref[slot], preferred_element_type=f32)
        h, hx, hy, hxx, hxy, hyy = [
            summed[b * SPLATS:(b + 1) * SPLATS] for b in range(NMOM)
        ]
        dx = x_lane - ex_ref[pl.ds(first_row(r, 0), SPLATS, stride=BATCH), :]
        dy = y_lane - ex_ref[pl.ds(first_row(r, 1), SPLATS, stride=BATCH), :]
        about_x = hx + dx * h
        about_y = hy + dy * h
        moments = [
            h,
            about_x,
            about_y,
            hxx + dx * (hx + about_x),
            hxy + dx * hy + dy * about_x,
            hyy + dy * (hy + about_y),
        ]
        for k in range(3):
            moments.append(toned[0:SPLATS, k * LANES:(k + 1) * LANES])
        for p in range(9):
            first = p * SPLATS * BATCH + (r & (BATCH - 1))
            stage_ref[pl.ds(first, SPLATS, stride=BATCH), :] = moments[p]

    def finish(i, carry):
        which = lax.rem(i + 1 + me // BATCH, batches)
        base = pl.multiple_of(which * BATCH, BATCH)

        def pair(j, carry):
            r = base + 2 * j
            before = base + 2 * jnp.maximum(j - 1, 0)
            for k in range(2):
                reduce(before + k, k)
            for k in range(2):
                backward(r + k, k)
            return carry

        lax.fori_loop(0, BATCH // 2, pair, 0)
        for k in range(2):
            reduce(base + BATCH - 2 + k, k)
        wide = [
            jnp.concatenate(
                [stage_ref[(p * SPLATS + s) * BATCH:(p * SPLATS + s + 1) * BATCH, :] for s in range(SPLATS)], 1
            )
            for p in range(9)
        ]
        folded = dot(jnp.concatenate(wide, 0), fold_ref[...], pieces=2)
        for p in range(9):
            gsend_ref[p, pl.ds(base, BATCH), :] = folded[p * BATCH:(p + 1) * BATCH]

        def back(j, carry):
            peer = base + j

            @pl.when(peer != me)
            def _():
                pltpu.make_async_remote_copy(
                    src_ref=gsend_ref.at[:, pl.ds(peer, 1), :],
                    dst_ref=grads_hbm.at[:, pl.ds(me, 1), :],
                    send_sem=gsend_sem, recv_sem=grecv_sem,
                    device_id=(peer,), device_id_type=MESH,
                ).start()

            return carry

        lax.fori_loop(0, BATCH, back, 0)
        return carry

    lax.fori_loop(0, batches, finish, 0)
    own = pltpu.make_async_copy(
        gsend_ref.at[:, pl.ds(me, 1), :], grads_hbm.at[:, pl.ds(me, 1), :], own_sem
    )
    own.start()

    lane_tile = same((stripe_tiles, LANES), lambda i: i, lambda j: j // span)
    pixel_row = same((pixels, rows), lambda i: i // span, lambda j: j)
    pixel_lane = same((pixels, LANES), lambda i: i & (span - 1), lambda j: j & (span - 1))
    flat = dot(lane_tile, dot(pixel_row, lossy_ref[...], selector=0) * pixel_lane, True, selector=0)
    for t in range(stripe_tiles):
        loss_ref[0:1, t * pixels:(t + 1) * pixels] = flat[t:t + 1]
    keep = pltpu.make_async_copy(loss_ref, loss_hbm, loss_sem)
    keep.start()

    pltpu.make_async_remote_copy(
        src_ref=gsend_ref.at[:, everyone, :], dst_ref=grads_hbm.at[:, everyone, :],
        send_sem=gsend_sem, recv_sem=grecv_sem, device_id=(me,), device_id_type=MESH,
    ).wait()
    own.wait()
    keep.wait()


def chain_kernel(
    gauss_hbm, depth_hbm, moment_hbm, loss_in, grads_hbm, loss_out,
    gauss_ref, depth_ref, moment_ref, grads_ref, load_sem, moment_sem, store_sem, loss_sem,
):
    tile_count = depth_ref.shape[1]
    regions = moment_ref.shape[1]
    group = tile_count // regions * SPLATS
    per = LANES // group
    chunks = tile_count // LANES
    width = regions // chunks
    moments = [
        pltpu.make_async_copy(
            moment_hbm.at[:, c * width:(c + 1) * width, :],
            moment_ref.at[:, c * width:(c + 1) * width, :], moment_sem.at[c],
        )
        for c in range(chunks)
    ]
    loads = [
        pltpu.make_async_copy(gauss_hbm, gauss_ref, load_sem.at[0]),
        pltpu.make_async_copy(depth_hbm, depth_ref, load_sem.at[1]),
    ]
    keep = pltpu.make_async_copy(loss_in, loss_out, loss_sem)
    for copy in loads + moments + [keep]:
        copy.start()
    for copy in loads:
        copy.wait()
    lane8 = iota((8, LANES), 1)
    stores = []
    for c in range(chunks):
        part = slice(8 * c, 8 * c + 8)
        moments[c].wait()
        index = (lane8 & -SPLATS) + to_lanes(depth_ref[:, c * LANES:(c + 1) * LANES])
        x = [gauss_ref[p, part, :] for p in range(9)]
        sums = []
        for p in range(9):
            if per == 1:
                value = moment_ref[p, part, :]
            else:
                value = jnp.zeros((8, LANES), jnp.float32)
                for j in range(per):
                    piece = moment_ref[p, pl.ds(8 * c * per + j, 8, stride=per), :]
                    piece = pltpu.roll(piece, j * group, 1) if j else piece
                    value = jnp.where(lane8 // group == j, piece, value)
            sums.append(along_lanes(value, index))
        squash = jnp.tanh(x[4])
        rho = 0.9 * squash
        inv = 1.0 / (1.0 - rho * rho)
        inv_x, inv_y = jnp.exp(-x[2]), jnp.exp(-x[3])
        hu, hv = inv_x * sums[1], inv_y * sums[2]
        huu = inv_x * (inv_x * sums[3])
        huv = inv_x * (inv_y * sums[4])
        hvv = inv_y * (inv_y * sums[5])
        hq = inv * (huu - 2.0 * rho * huv + hvv)
        results = [
            inv_x * inv * (hu - rho * hv),
            inv_y * inv * (hv - rho * hu),
            inv * (huu - rho * huv),
            inv * (hvv - rho * huv),
            inv * (huv - rho * hq) * (0.9 * (1.0 - squash * squash)),
            sums[0] * jax.nn.sigmoid(-x[5]),
        ]
        for k in range(3):
            tone = jax.nn.sigmoid(x[6 + k])
            results.append(sums[6 + k] * tone * (1.0 - tone))
        for p in range(9):
            grads_ref[p, part, :] = results[p]
        stores.append(
            pltpu.make_async_copy(
                grads_ref.at[:, part, :], grads_hbm.at[:, part, :], store_sem.at[c]
            )
        )
        stores[-1].start()
    for copy in stores:
        copy.wait()
    keep.wait()


def shards(gaussians, depth, coverage, flips, features, w_first, b_first, w_second, target):
    regions = lax.axis_size("region")
    tile_count = depth.shape[1]
    stripe_tiles = tile_count // regions
    pixels = TSIDE * TSIDE
    rows = pixels * stripe_tiles // LANES
    nodes = 2 * regions - 1
    width = features.shape[1]
    f32, bf16 = jnp.float32, jnp.bfloat16
    dma = pltpu.SemaphoreType.DMA
    dense = gaussians.reshape(9, tile_count * SPLATS // LANES, LANES)
    ranks = depth[0].T
    anywhere = pl.BlockSpec(memory_space=pl.ANY)
    operands = (
        dense,
        ranks,
        coverage,
        flips.T,
        features.reshape(stripe_tiles, pixels, width),
        w_first,
        b_first,
        w_second,
        target,
    )
    loss, moments = pl.pallas_call(
        splat_kernel,
        out_shape=(
            jax.ShapeDtypeStruct((1, stripe_tiles * pixels), f32),
            jax.ShapeDtypeStruct((9, regions, LANES), f32),
        ),
        in_specs=[anywhere] * 9,
        out_specs=(anywhere, anywhere),
        scratch_shapes=[pltpu.VMEM(x.shape, x.dtype) for x in operands] + [
            dma((9,)),
            pltpu.VMEM((1, stripe_tiles * pixels), f32),
            dma(()),
            dma(()),
            pltpu.VMEM((9, regions, LANES), f32),
            pltpu.VMEM((9, regions, LANES), f32),
            dma(()),
            dma(()),
            pltpu.VMEM((9, regions, LANES), f32),
            dma(()),
            dma(()),
            pltpu.VMEM((regions - 1, LANES), f32),
            pltpu.VMEM((rows, LANES), f32),
            pltpu.VMEM((3, rows, LANES), f32),
            pltpu.VMEM((NPAR * SPLATS * regions, LANES), f32),
            pltpu.VMEM((regions * SPLATS, rows, LANES), f32),
            pltpu.VMEM((regions * SPLATS, rows, LANES), f32),
            pltpu.VMEM((nodes, 4, rows, LANES), f32),
            pltpu.VMEM((nodes, 2, rows, LANES), f32),
            pltpu.VMEM((3, rows, LANES), f32),
            pltpu.VMEM((rows, LANES), f32),
            pltpu.VMEM((2, SPLATS * rows, LANES), bf16),
            pltpu.VMEM((2, SPLATS * 8, 3 * LANES), bf16),
            pltpu.VMEM((9 * BATCH * SPLATS, LANES), f32),
            pltpu.VMEM((NMOM * SPLATS, SPLATS * rows), bf16),
            pltpu.VMEM((16, SPLATS * 8), bf16),
            pltpu.VMEM((SPLATS * LANES, LANES), bf16),
            pltpu.VMEM((3 * LANES, SPLATS * LANES), bf16),
        ],
        compiler_params=pltpu.CompilerParams(
            vmem_limit_bytes=56 * 1024 * 1024, collective_id=0, has_side_effects=True
        ),
    )(*operands)
    grads, loss = pl.pallas_call(
        chain_kernel,
        out_shape=(
            jax.ShapeDtypeStruct(dense.shape, f32), jax.ShapeDtypeStruct(loss.shape, f32)
        ),
        in_specs=[anywhere] * 4,
        out_specs=(anywhere, anywhere),
        scratch_shapes=[
            pltpu.VMEM(dense.shape, f32),
            pltpu.VMEM(ranks.shape, ranks.dtype),
            pltpu.VMEM(moments.shape, f32),
            pltpu.VMEM(dense.shape, f32),
            dma((2,)),
            dma((tile_count // LANES,)),
            dma((tile_count // LANES,)),
            dma(()),
        ],
    )(dense, ranks, moments, loss)
    return (loss.reshape(-1), grads.reshape(gaussians.shape))


def solution(mesh):
    placed = (
        P("region", None, None),
        P("region", None, None),
        P("region", None),
        P(),
        P("region", None),
        P(),
        P(),
        P(),
        P(None, "region"),
    )
    return jax.shard_map(
        shards,
        mesh=mesh,
        in_specs=placed,
        out_specs=(P("region"), P("region", None, None)),
        check_vma=False,
    )
```

```python
import jax
import jax.numpy as jnp
from jax import lax
from jax.experimental import pallas as pl
from jax.experimental.pallas import tpu as pltpu
from jax.sharding import PartitionSpec as P

TSIDE = 16
LANES = 128
SPLATS = 8
NPAR = 9
NMOM = 6
BATCH = 8
BLOCK = 32
UNROLL = 2
GELU = (2.0 / 3.141592653589793) ** 0.5
EARLY = 3
LOWEST = -1e4
FUNROLL = 8
PUNROLL = 3
LOG2E = 1.4426950408889634
MESH = pl.DeviceIdType.MESH


def iota(shape, dim):
    return lax.broadcasted_iota(jnp.int32, shape, dim)


def dot(x, y, transposed=False, selector=1, pieces=3):
    dims = (((1,), (1 if transposed else 0,)), ((), ()))
    bf16 = jnp.bfloat16
    sel, val = (y, x) if selector == 1 else (x, y)
    sel = sel.astype(bf16)
    total = None
    for _ in range(pieces):
        piece = val.astype(bf16)
        val = val - piece.astype(jnp.float32)
        pair = (piece, sel) if selector == 1 else (sel, piece)
        part = lax.dot_general(*pair, dims, preferred_element_type=jnp.float32)
        total = part if total is None else total + part
    return total


def same(shape, first, second):
    return (first(iota(shape, 0)) == second(iota(shape, 1))).astype(jnp.float32)


def along_lanes(x, index):
    return jnp.take_along_axis(x, index, axis=1)


def to_lanes(x):
    row, lane = iota((8, LANES), 0), iota((8, LANES), 1)
    x = along_lanes(x, ((lane // 16 - row) & 7) * 16 + (lane & 15))
    x = jnp.take_along_axis(x, (lane // 16 - row) & 7, axis=0)
    return along_lanes(x, ((row + (lane & 7)) & 7) * 16 + lane // 8)


def splat_kernel(
    gauss_hbm, depth_hbm, cover_hbm, flips_hbm, feat_hbm, first_hbm, bias_hbm, second_hbm,
    target_hbm, loss_hbm, grads_hbm, factor_hbm, place_hbm,
    gauss_ref, depth_ref, cover_ref, flips_ref, feat_ref, first_ref, bias_ref, second_ref,
    target_ref, load_sem, half_ref, loss_ref, factor_ref, place_ref, keep_sem, own_sem, send_ref, recv_ref, send_sem, recv_sem, gsend_ref, gsend_sem,
    grecv_sem, flip_ref, spread_ref, wanted_ref,
    ex_ref, a_ref, w_ref, tree_ref, down_ref, g_ref, lossy_ref, rhs_ref, tone_ref, stage_ref,
    basis_ref, ones_ref, fold_ref, widen_ref,
):
    regions = recv_ref.shape[1]
    rows = wanted_ref.shape[1]
    nv = rows // 8
    tile_count = depth_ref.shape[1]
    stripe_tiles = tile_count // regions
    group = stripe_tiles * SPLATS
    per = LANES // group
    span = LANES // stripe_tiles
    inner = regions - 1
    batches = regions // BATCH
    pixels = TSIDE * TSIDE
    f32, bf16 = jnp.float32, jnp.bfloat16
    me = lax.axis_index("region")

    barrier = pltpu.get_barrier_semaphore()

    def greet(i, carry):
        pl.semaphore_signal(
            barrier, inc=1, device_id=(lax.rem(me + i, regions),), device_id_type=MESH
        )
        return carry

    lax.fori_loop(1, regions, greet, 0)
    pairs = [
        (gauss_hbm, gauss_ref), (depth_hbm, depth_ref), (cover_hbm, cover_ref),
        (feat_hbm, feat_ref), (first_hbm, first_ref), (bias_hbm, bias_ref),
        (second_hbm, second_ref), (target_hbm, target_ref), (flips_hbm, flips_ref),
    ]
    loads = [pltpu.make_async_copy(*x, load_sem.at[i]) for i, x in enumerate(pairs)]
    for load in loads:
        load.start()
    for load in loads[:3]:
        load.wait()

    row8, lane8 = iota((8, LANES), 0), iota((8, LANES), 1)

    for c in range(tile_count // LANES):
        tiles = slice(c * LANES, (c + 1) * LANES)
        order = jnp.zeros((SPLATS, LANES), jnp.int32)
        for g in range(SPLATS):
            order = jnp.where(depth_ref[g:g + 1, tiles] == row8, g, order)
        index = (lane8 & -SPLATS) + to_lanes(order)
        cover = along_lanes(
            jnp.broadcast_to(cover_ref[:, tiles], (8, LANES)), row8 * 16 + lane8 // SPLATS
        )
        part = slice(8 * c, 8 * c + 8)
        x = [gauss_ref[p, part, :] for p in range(9)]
        rho = 0.9 * jnp.tanh(x[4])
        scale = (0.5 * LOG2E) ** 0.5
        norm = lax.rsqrt(1.0 - rho * rho) * scale
        inv_y = jnp.exp(-x[3])
        values = [
            x[0],
            x[1],
            jnp.exp(-x[2]) * norm,
            inv_y * (rho * norm),
            inv_y * scale,
            0.99 * jax.nn.sigmoid(x[5]),
            jax.nn.sigmoid(x[6]),
            jax.nn.sigmoid(x[7]),
            jax.nn.sigmoid(x[8]),
        ]
        for p in range(9):
            value = along_lanes(values[p], index)
            if p == 5:
                value = jnp.maximum(jnp.log2(value * cover.astype(f32)), LOWEST)
            for j in range(per):
                shifted = pltpu.roll(value, LANES - j * group, 1) if j else value
                if per == 1:
                    send_ref[p, part, :] = shifted
                else:
                    send_ref[p, pl.ds(8 * c * per + j, 8, stride=per), :] = shifted

    for load in loads[3:7]:
        load.wait()
    bias = 0.5 * bias_ref[...].reshape(1, bias_ref.shape[0])
    half_ref[...] = first_ref[...] * bf16(0.5)
    second = jnp.broadcast_to(
        second_ref[...].astype(f32).reshape(1, second_ref.shape[0]), (16, second_ref.shape[0])
    ).astype(bf16)

    block = max(BLOCK, span)
    per_block = block // span

    def network(j, carry):
        feats = feat_ref[:, pl.ds(pl.multiple_of(j * block, block), block), :]
        feats = feats.reshape(stripe_tiles * block, feat_ref.shape[2])
        z = jnp.dot(feats, half_ref[...], preferred_element_type=f32) + bias
        hidden = z + z * jnp.tanh(z * (2.0 * GELU + (8.0 * 0.044715 * GELU) * (z * z)))
        hidden = hidden.reshape(stripe_tiles, per_block, span, hidden.shape[-1])
        for i in range(per_block):
            part = hidden[:, i].reshape(LANES, hidden.shape[-1]).astype(bf16)
            logits = lax.dot_general(
                second, part, (((1,), (1,)), ((), ())), preferred_element_type=f32,
            )
            spread_ref[pl.ds(j * per_block + i, 1), :] = logits[0:1]
        return carry

    steps = pixels // block
    early = min(EARLY, steps // 2)
    if early:
        lax.fori_loop(0, early, network, 0, unroll=UNROLL)
    pl.semaphore_wait(barrier, regions - 1)

    def send(i, carry):
        peer = lax.rem(me + i, regions)
        pltpu.make_async_remote_copy(
            src_ref=send_ref.at[:, pl.ds(peer, 1), :], dst_ref=recv_ref.at[:, pl.ds(me, 1), :],
            send_sem=send_sem, recv_sem=recv_sem.at[me // BATCH], device_id=(peer,),
            device_id_type=MESH,
        ).start()
        return carry

    lax.fori_loop(1, regions, send, 0)
    for p in range(9):
        recv_ref[p, pl.ds(me, 1), :] = send_ref[p, pl.ds(me, 1), :]
    lax.fori_loop(early, steps, network, 0, unroll=UNROLL)

    for load in loads[7:]:
        load.wait()
    tile_lane = same((LANES, stripe_tiles), lambda i: i // span, lambda j: j)
    lane_pixel = same((LANES, pixels), lambda i: i & (span - 1), lambda j: j & (span - 1))
    row_pixel = same((rows, pixels), lambda i: i, lambda j: j // span)
    for k in range(3):
        flat = jnp.concatenate(
            [target_ref[k:k + 1, t * pixels:(t + 1) * pixels] for t in range(stripe_tiles)], 0
        )
        wanted_ref[k] = dot(
            row_pixel, dot(tile_lane, flat, selector=0, pieces=2) * lane_pixel, True, selector=0, pieces=2
        )
    my_tiles = same(
        (tile_count, LANES), lambda i: i - me * stripe_tiles, lambda j: j // span
    ).astype(bf16)
    flip_ref[...] = jnp.dot(
        flips_ref[...].astype(f32).astype(bf16), my_tiles, preferred_element_type=f32,
    )

    wide = min(span, TSIDE)
    half = (TSIDE - wide) / 2

    def x_row(i):
        return ((i * span) & (TSIDE - 1)).astype(f32) - half

    def y_row(i):
        return (i * span // TSIDE).astype(f32) - 7.5

    x_lane = (lane8 & (wide - 1)).astype(f32) + (half + 0.5)
    y_lane = ((lane8 & (span - 1)) // TSIDE).astype(f32) + 8.0
    depth_rows = SPLATS * rows
    at = iota((SPLATS, depth_rows), 1)
    mine = at // rows == iota((SPLATS, depth_rows), 0)
    xr, yr = x_row(at & (rows - 1)), y_row(at & (rows - 1))
    terms = [jnp.ones_like(xr), xr, yr, xr * xr, xr * yr, yr * yr]
    basis_ref[...] = jnp.concatenate([jnp.where(mine, term, 0.0) for term in terms], 0).astype(bf16)
    ones_ref[...] = (
        iota(ones_ref.shape, 1) // 8 == iota(ones_ref.shape, 0)
    ).astype(f32).astype(bf16)
    for s in range(SPLATS):
        fold_ref[s * LANES:(s + 1) * LANES, :] = same(
            (LANES, LANES), lambda i: i // span * SPLATS + s, lambda j: j
        ).astype(bf16)

    for s in range(SPLATS):
        picks = same((LANES, LANES), lambda i: i, lambda j: j // span * SPLATS + s).astype(bf16)
        for k in range(3):
            widen_ref[k * LANES:(k + 1) * LANES, s * LANES:(s + 1) * LANES] = picks
    for buf in (rhs_ref, tone_ref, stage_ref):
        buf[...] = jnp.zeros(buf.shape, buf.dtype)

    def arrive(batch, count):
        some = pl.ds(0, count)
        pltpu.make_async_remote_copy(
            src_ref=send_ref.at[:, some, :], dst_ref=recv_ref.at[:, some, :],
            send_sem=send_sem, recv_sem=recv_sem.at[batch], device_id=(me,), device_id_type=MESH,
        ).wait_recv()

    def expand(c):
        base = pl.multiple_of(c * BATCH, BATCH)
        value = jnp.concatenate(
            [recv_ref[p, pl.ds(base, BATCH), :] for p in range(NPAR)], 0
        )
        pieces = []
        for _ in range(3):
            piece = value.astype(bf16)
            value = value - piece.astype(f32)
            pieces.append(piece)
        spread = jnp.dot(
            jnp.concatenate(pieces, 1), widen_ref[...], preferred_element_type=f32
        )
        for p in range(NPAR):
            for s in range(SPLATS):
                first = pl.multiple_of((c * NPAR + p) * SPLATS * BATCH, BATCH) + s * BATCH
                ex_ref[pl.ds(first, BATCH), :] = spread[
                    p * BATCH:(p + 1) * BATCH, s * LANES:(s + 1) * LANES
                ]

    vs = [slice(8 * v, 8 * v + 8) for v in range(nv)]
    xpos = x_row(row8) + x_lane
    ypos = y_row(row8) + y_lane
    step = float(8 * span // TSIDE)

    def first_row(r, p):
        return (r // BATCH * NPAR + p) * (SPLATS * BATCH) + (r & (BATCH - 1))

    def row(r, p, s):
        return ex_ref[pl.ds(first_row(r, p) + s * BATCH, 1), :]

    def forward(r, carry):
        trans = [jnp.ones((8, LANES), f32)] * nv
        color = [[jnp.zeros((8, LANES), f32)] * nv for _ in range(3)]
        for s in range(SPLATS):
            us = (xpos - row(r, 0, s)) * row(r, 2, s)
            m_y, skew, inv_y, level = row(r, 1, s), row(r, 3, s), row(r, 4, s), row(r, 5, s)
            ks = [row(r, 6 + k, s) for k in range(3)]
            dy = ypos - m_y
            w, p = dy * inv_y, us - dy * skew
            rise_w, rise_p = step * inv_y, step * skew
            for v in range(nv):
                if v:
                    w, p = w + rise_w, p - rise_p
                alpha = jnp.exp2(level - (p * p + w * w))
                weight = trans[v] * alpha
                a_ref[r * SPLATS + s, vs[v]] = alpha
                w_ref[r * SPLATS + s, vs[v]] = weight
                for k in range(3):
                    color[k][v] = color[k][v] + weight * ks[k]
                trans[v] = trans[v] - weight
        for v in range(nv):
            for k in range(3):
                tree_ref[inner + r, k, vs[v]] = color[k][v]
            tree_ref[inner + r, 3, vs[v]] = trans[v]
        return carry

    def render(i, carry):
        batch = lax.rem(me // BATCH + i, batches)

        @pl.when(i == 0)
        def _():
            arrive(batch, BATCH - 1)

        @pl.when(i > 0)
        def _():
            arrive(batch, BATCH)

        expand(batch)
        lax.fori_loop(0, BATCH, lambda j, c: forward(batch * BATCH + j, c), 0, unroll=FUNROLL)
        return carry

    lax.fori_loop(0, batches, render, 0)
    everyone = pl.ds(0, regions - 1)
    pltpu.make_async_remote_copy(
        src_ref=send_ref.at[:, everyone, :], dst_ref=recv_ref.at[:, everyone, :],
        send_sem=send_sem, recv_sem=recv_sem.at[0], device_id=(me,), device_id_type=MESH,
    ).wait_send()

    def flipped(n):
        return jnp.broadcast_to(flip_ref[pl.ds(n, 1), :], (8, LANES)) > 0.0

    def merge(n, v):
        if n >= inner:
            return [tree_ref[n, k, vs[v]] for k in range(4)]
        low, high = merge(2 * n + 1, v), merge(2 * n + 2, v)
        flip = flipped(n)
        over_low = jnp.where(flip, high[3], 1.0)
        over_high = jnp.where(flip, 1.0, low[3])
        both = [over_low * low[k] + over_high * high[k] for k in range(3)] + [low[3] * high[3]]
        for k in range(4):
            tree_ref[n, k, vs[v]] = both[k]
        return both

    for v in range(nv):
        merge(0, v)

    for v in range(nv):
        logit = spread_ref[vs[v]]
        spread = 0.5 + jnp.maximum(logit, 0.0) + jnp.log1p(jnp.exp(-jnp.abs(logit)))
        inv_square = 1.0 / (spread * spread)
        clear = tree_ref[0, 3, vs[v]]
        residual = [tree_ref[0, k, vs[v]] + clear - wanted_ref[k, vs[v]] for k in range(3)]
        total = residual[0] * residual[0] + residual[1] * residual[1] + residual[2] * residual[2]
        lossy_ref[vs[v]] = 0.5 * total * inv_square + jnp.log(spread)
        gs = [res * inv_square for res in residual]
        for k in range(3):
            g_ref[k, vs[v]] = gs[k]

    def split(n, v, g, front, behind):
        if n >= inner:
            down_ref[n - inner, 0, vs[v]] = front
            down_ref[n - inner, 1, vs[v]] = behind
            return
        flip = flipped(n)
        low = [tree_ref[2 * n + 1, k, vs[v]] for k in range(4)]
        high = [tree_ref[2 * n + 2, k, vs[v]] for k in range(4)]
        back = [jnp.where(flip, l, h) for l, h in zip(low, high)]
        through = front * jnp.where(flip, high[3], low[3])
        value = g[0] * back[0] + g[1] * back[1] + g[2] * back[2] + back[3] * behind
        split(2 * n + 1, v, g, jnp.where(flip, through, front), jnp.where(flip, behind, value))
        split(2 * n + 2, v, g, jnp.where(flip, front, through), jnp.where(flip, value, behind))

    for v in range(nv):
        g = [g_ref[k, vs[v]] for k in range(3)]
        split(0, v, g, jnp.ones((8, LANES), f32), g[0] + g[1] + g[2])

    def backward(r, slot):
        front = [down_ref[r, 0, vs[v]] for v in range(nv)]
        gs = [[front[v] * g_ref[k, vs[v]] for v in range(nv)] for k in range(3)]
        behind = [front[v] * down_ref[r, 1, vs[v]] for v in range(nv)]
        colors = [[], [], []]
        for s in reversed(range(SPLATS)):
            ks = [row(r, 6 + k, s) for k in range(3)]
            pulls, tones = [], [None] * 3
            for v in range(nv):
                alpha = a_ref[r * SPLATS + s, vs[v]]
                weight = w_ref[r * SPLATS + s, vs[v]]
                shade = ks[0] * gs[0][v] + ks[1] * gs[1][v] + ks[2] * gs[2][v]
                diff = shade - behind[v]
                behind[v] = behind[v] + alpha * diff
                pulls.append(weight * diff)
                for k in range(3):
                    tone = weight * gs[k][v]
                    tones[k] = tone if v == 0 else tones[k] + tone
            rhs_ref[slot, s * rows:(s + 1) * rows, :] = jnp.concatenate(pulls, 0).astype(bf16)
            for k in range(3):
                colors[k].insert(0, tones[k])
            if s % 2 == 0:
                for k in range(3):
                    tone_ref[slot, s * 8:(s + 2) * 8, k * LANES:(k + 1) * LANES] = (
                        jnp.concatenate(colors[k][:2], 0).astype(bf16)
                    )

    def reduce(r, slot):
        summed = jnp.dot(basis_ref[...], rhs_ref[slot], preferred_element_type=f32)
        toned = jnp.dot(ones_ref[...], tone_ref[slot], preferred_element_type=f32)
        h, hx, hy, hxx, hxy, hyy = [
            summed[b * SPLATS:(b + 1) * SPLATS] for b in range(NMOM)
        ]
        dx = x_lane - ex_ref[pl.ds(first_row(r, 0), SPLATS, stride=BATCH), :]
        dy = y_lane - ex_ref[pl.ds(first_row(r, 1), SPLATS, stride=BATCH), :]
        about_x = hx + dx * h
        about_y = hy + dy * h
        moments = [
            h,
            about_x,
            about_y,
            hxx + dx * (hx + about_x),
            hxy + dx * hy + dy * about_x,
            hyy + dy * (hy + about_y),
        ]
        for k in range(3):
            moments.append(toned[0:SPLATS, k * LANES:(k + 1) * LANES])
        for p in range(9):
            first = p * SPLATS * BATCH + (r & (BATCH - 1))
            stage_ref[pl.ds(first, SPLATS, stride=BATCH), :] = moments[p]

    def fold(base):
        wide = [
            jnp.concatenate(
                [stage_ref[(p * SPLATS + s) * BATCH:(p * SPLATS + s + 1) * BATCH, :] for s in range(SPLATS)], 1
            )
            for p in range(9)
        ]
        whole = jnp.concatenate(wide, 0)
        coarse = whole.astype(bf16).astype(f32)
        folded = jnp.dot(
            jnp.concatenate([coarse, whole - coarse], 0).astype(bf16), fold_ref[...],
            preferred_element_type=f32,
        )
        folded = folded[:9 * BATCH] + folded[9 * BATCH:]
        for p in range(9):
            gsend_ref[p, pl.ds(base, BATCH), :] = folded[p * BATCH:(p + 1) * BATCH]

    def give_back(base):
        def back(j, carry):
            peer = base + j

            @pl.when(peer != me)
            def _():
                pltpu.make_async_remote_copy(
                    src_ref=gsend_ref.at[:, pl.ds(peer, 1), :],
                    dst_ref=grads_hbm.at[:, pl.ds(me, 1), :],
                    send_sem=gsend_sem, recv_sem=grecv_sem,
                    device_id=(peer,), device_id_type=MESH,
                ).start()

            return carry

        lax.fori_loop(0, BATCH, back, 0)

    def base_of(i):
        return pl.multiple_of(lax.rem(i + me // BATCH, batches) * BATCH, BATCH)

    def finish(i, carry):
        base, past = base_of(i + 1), base_of(i)
        for k in range(2):
            reduce(past + BATCH - 2 + k, k)
        fold(past)
        for k in range(2):
            backward(base + k, k)

        @pl.when(i > 0)
        def _():
            give_back(past)

        def pair(j, carry):
            r = base + 2 * j
            for k in range(2):
                reduce(r - 2 + k, k)
            for k in range(2):
                backward(r + k, k)
            return carry

        lax.fori_loop(1, BATCH // 2, pair, 0, unroll=PUNROLL)
        return carry

    lax.fori_loop(0, batches, finish, 0)
    last = base_of(batches)
    for k in range(2):
        reduce(last + BATCH - 2 + k, k)
    fold(last)
    give_back(last)
    own = pltpu.make_async_copy(
        gsend_ref.at[:, pl.ds(me, 1), :], grads_hbm.at[:, pl.ds(me, 1), :], own_sem
    )
    own.start()

    lane_tile = same((stripe_tiles, LANES), lambda i: i, lambda j: j // span)
    pixel_row = same((pixels, rows), lambda i: i // span, lambda j: j)
    pixel_lane = same((pixels, LANES), lambda i: i & (span - 1), lambda j: j & (span - 1))
    flat = dot(
        lane_tile, dot(pixel_row, lossy_ref[...], selector=0, pieces=2) * pixel_lane, True,
        selector=0, pieces=2,
    )
    for t in range(stripe_tiles):
        loss_ref[0:1, t * pixels:(t + 1) * pixels] = flat[t:t + 1]
    for c in range(tile_count // LANES):
        part = slice(8 * c, 8 * c + 8)
        place_ref[part, :] = (lane8 & -SPLATS) + to_lanes(depth_ref[:, c * LANES:(c + 1) * LANES])
        x = [gauss_ref[p, part, :] for p in range(9)]
        squash = jnp.tanh(x[4])
        rho = 0.9 * squash
        inv = 1.0 / (1.0 - rho * rho)
        tones = [jax.nn.sigmoid(x[6 + k]) for k in range(3)]
        factors = [
            jnp.exp(-x[2]), jnp.exp(-x[3]), inv, inv * rho,
            inv * (0.9 * (1.0 - squash * squash)), inv * rho * (0.9 * (1.0 - squash * squash)),
            jax.nn.sigmoid(-x[5]),
        ] + [tone * (1.0 - tone) for tone in tones]
        for p in range(10):
            factor_ref[p, part, :] = factors[p]
    keeps = [
        pltpu.make_async_copy(loss_ref, loss_hbm, keep_sem.at[0]),
        pltpu.make_async_copy(factor_ref, factor_hbm, keep_sem.at[1]),
        pltpu.make_async_copy(place_ref, place_hbm, keep_sem.at[2]),
    ]
    for keep in keeps:
        keep.start()

    pltpu.make_async_remote_copy(
        src_ref=gsend_ref.at[:, everyone, :], dst_ref=grads_hbm.at[:, everyone, :],
        send_sem=gsend_sem, recv_sem=grecv_sem, device_id=(me,), device_id_type=MESH,
    ).wait()
    own.wait()
    for keep in keeps:
        keep.wait()


def chain_kernel(moment_ref, factor_ref, place_ref, loss_in, grads_ref, loss_out):
    loss_out[...] = loss_in[...]
    regions, count = moment_ref.shape[1], place_ref.shape[0]
    per = regions // count
    group = LANES // per
    lane8 = iota((8, LANES), 1)
    for c in range(count // 8):
        part = slice(8 * c, 8 * c + 8)
        index = place_ref[part, :]
        sums = []
        for p in range(9):
            if per == 1:
                value = moment_ref[p, part, :]
            else:
                value = jnp.zeros((8, LANES), jnp.float32)
                for j in range(per):
                    piece = moment_ref[p, pl.ds(8 * c * per + j, 8, stride=per), :]
                    piece = pltpu.roll(piece, j * group, 1) if j else piece
                    value = jnp.where(lane8 // group == j, piece, value)
            sums.append(along_lanes(value, index))
        inv_x, inv_y, inv, skew, bend, lean, hide = [factor_ref[p, part, :] for p in range(7)]
        hu, hv = inv_x * sums[1], inv_y * sums[2]
        huu = inv_x * (inv_x * sums[3])
        huv = inv_x * (inv_y * sums[4])
        hvv = inv_y * (inv_y * sums[5])
        wide = inv * huu - skew * huv
        tall = inv * hvv - skew * huv
        results = [
            inv_x * (inv * hu - skew * hv),
            inv_y * (inv * hv - skew * hu),
            wide,
            tall,
            bend * huv - lean * (wide + tall),
            hide * sums[0],
        ]
        for k in range(3):
            results.append(sums[6 + k] * factor_ref[7 + k, part, :])
        for p in range(9):
            grads_ref[p, part, :] = results[p]


def shards(gaussians, depth, coverage, flips, features, w_first, b_first, w_second, target):
    regions = lax.axis_size("region")
    tile_count = depth.shape[1]
    stripe_tiles = tile_count // regions
    pixels = TSIDE * TSIDE
    rows = pixels * stripe_tiles // LANES
    nodes = 2 * regions - 1
    width = features.shape[1]
    f32, bf16 = jnp.float32, jnp.bfloat16
    dma = pltpu.SemaphoreType.DMA
    dense = gaussians.reshape(9, tile_count * SPLATS // LANES, LANES)
    ranks = depth[0].T
    anywhere = pl.BlockSpec(memory_space=pl.ANY)
    vmem = pl.BlockSpec(memory_space=pltpu.VMEM)
    operands = (
        dense,
        ranks,
        coverage,
        flips.T,
        features.reshape(stripe_tiles, pixels, width),
        w_first,
        b_first,
        w_second,
        target,
    )
    loss, moments, factors, places = pl.pallas_call(
        splat_kernel,
        out_shape=(
            jax.ShapeDtypeStruct((1, stripe_tiles * pixels), f32),
            jax.ShapeDtypeStruct((9, regions, LANES), f32),
            jax.ShapeDtypeStruct((10,) + dense.shape[1:], f32),
            jax.ShapeDtypeStruct(dense.shape[1:], jnp.int32),
        ),
        in_specs=[anywhere] * 9,
        out_specs=(anywhere,) * 4,
        scratch_shapes=[pltpu.VMEM(x.shape, x.dtype) for x in operands] + [
            dma((9,)),
            pltpu.VMEM(w_first.shape, w_first.dtype),
            pltpu.VMEM((1, stripe_tiles * pixels), f32),
            pltpu.VMEM((10,) + dense.shape[1:], f32),
            pltpu.VMEM(dense.shape[1:], jnp.int32),
            dma((3,)),
            dma(()),
            pltpu.VMEM((9, regions, LANES), f32),
            pltpu.VMEM((9, regions, LANES), f32),
            dma(()),
            dma((regions // BATCH,)),
            pltpu.VMEM((9, regions, LANES), f32),
            dma(()),
            dma(()),
            pltpu.VMEM((regions - 1, LANES), f32),
            pltpu.VMEM((rows, LANES), f32),
            pltpu.VMEM((3, rows, LANES), f32),
            pltpu.VMEM((NPAR * SPLATS * regions, LANES), f32),
            pltpu.VMEM((regions * SPLATS, rows, LANES), f32),
            pltpu.VMEM((regions * SPLATS, rows, LANES), f32),
            pltpu.VMEM((nodes, 4, rows, LANES), f32),
            pltpu.VMEM((regions, 2, rows, LANES), f32),
            pltpu.VMEM((3, rows, LANES), f32),
            pltpu.VMEM((rows, LANES), f32),
            pltpu.VMEM((2, SPLATS * rows, LANES), bf16),
            pltpu.VMEM((2, SPLATS * 8, 3 * LANES), bf16),
            pltpu.VMEM((9 * BATCH * SPLATS, LANES), f32),
            pltpu.VMEM((NMOM * SPLATS, SPLATS * rows), bf16),
            pltpu.VMEM((16, SPLATS * 8), bf16),
            pltpu.VMEM((SPLATS * LANES, LANES), bf16),
            pltpu.VMEM((3 * LANES, SPLATS * LANES), bf16),
        ],
        compiler_params=pltpu.CompilerParams(
            vmem_limit_bytes=56 * 1024 * 1024, collective_id=0, has_side_effects=True
        ),
    )(*operands)
    grads, loss = pl.pallas_call(
        chain_kernel,
        out_shape=(
            jax.ShapeDtypeStruct(dense.shape, f32), jax.ShapeDtypeStruct(loss.shape, f32)
        ),
        in_specs=[vmem] * 4,
        out_specs=(vmem, vmem),
    )(moments, factors, places, loss)
    return (loss.reshape(-1), grads.reshape(gaussians.shape))


def solution(mesh):
    placed = (
        P("region", None, None),
        P("region", None, None),
        P("region", None),
        P(),
        P("region", None),
        P(),
        P(),
        P(),
        P(None, "region"),
    )
    return jax.shard_map(
        shards,
        mesh=mesh,
        in_specs=placed,
        out_specs=(P("region"), P("region", None, None)),
        check_vma=False,
    )
```

```python
import jax
import jax.numpy as jnp
from jax import lax
from jax.experimental import pallas as pl
from jax.experimental.pallas import tpu as pltpu
from jax.sharding import PartitionSpec as P

TSIDE = 16
LANES = 128
SPLATS = 8
NPAR = 9
NMOM = 6
BATCH = 8
BLOCK = 32
UNROLL = 2
GELU = (2.0 / 3.141592653589793) ** 0.5
EARLY = 3
LOWEST = -1e4
FUNROLL = 8
PUNROLL = 3
LOG2E = 1.4426950408889634
MESH = pl.DeviceIdType.MESH


def iota(shape, dim):
    return lax.broadcasted_iota(jnp.int32, shape, dim)


def dot(x, y, transposed=False, selector=1, pieces=3):
    dims = (((1,), (1 if transposed else 0,)), ((), ()))
    bf16 = jnp.bfloat16
    sel, val = (y, x) if selector == 1 else (x, y)
    sel = sel.astype(bf16)
    total = None
    for _ in range(pieces):
        piece = val.astype(bf16)
        val = val - piece.astype(jnp.float32)
        pair = (piece, sel) if selector == 1 else (sel, piece)
        part = lax.dot_general(*pair, dims, preferred_element_type=jnp.float32)
        total = part if total is None else total + part
    return total


def same(shape, first, second):
    return (first(iota(shape, 0)) == second(iota(shape, 1))).astype(jnp.float32)


def along_lanes(x, index):
    return jnp.take_along_axis(x, index, axis=1)


def to_lanes(x):
    row, lane = iota((8, LANES), 0), iota((8, LANES), 1)
    x = along_lanes(x, ((lane // 16 - row) & 7) * 16 + (lane & 15))
    x = jnp.take_along_axis(x, (lane // 16 - row) & 7, axis=0)
    return along_lanes(x, ((row + (lane & 7)) & 7) * 16 + lane // 8)


def splat_kernel(
    gauss_hbm, depth_hbm, cover_hbm, flips_hbm, feat_hbm, first_hbm, bias_hbm, second_hbm,
    target_hbm, loss_hbm, grads_hbm, factor_hbm, place_hbm,
    gauss_ref, depth_ref, cover_ref, flips_ref, feat_ref, first_ref, bias_ref, second_ref,
    target_ref, load_sem, half_ref, loss_ref, factor_ref, place_ref, keep_sem, own_sem, send_ref, recv_ref, send_sem, recv_sem, gsend_ref, gsend_sem,
    grecv_sem, flip_ref, spread_ref, wanted_ref,
    ex_ref, a_ref, w_ref, tree_ref, down_ref, g_ref, lossy_ref, rhs_ref, tone_ref, stage_ref,
    basis_ref, ones_ref, fold_ref, widen_ref,
):
    regions = recv_ref.shape[1]
    rows = wanted_ref.shape[1]
    nv = rows // 8
    tile_count = depth_ref.shape[1]
    stripe_tiles = tile_count // regions
    group = stripe_tiles * SPLATS
    per = LANES // group
    span = LANES // stripe_tiles
    inner = regions - 1
    batches = regions // BATCH
    pixels = TSIDE * TSIDE
    f32, bf16 = jnp.float32, jnp.bfloat16
    me = lax.axis_index("region")

    barrier = pltpu.get_barrier_semaphore()

    def greet(i, carry):
        pl.semaphore_signal(
            barrier, inc=1, device_id=(lax.rem(me + i, regions),), device_id_type=MESH
        )
        return carry

    lax.fori_loop(1, regions, greet, 0)
    pairs = [
        (gauss_hbm, gauss_ref), (depth_hbm, depth_ref), (cover_hbm, cover_ref),
        (feat_hbm, feat_ref), (first_hbm, first_ref), (bias_hbm, bias_ref),
        (second_hbm, second_ref), (target_hbm, target_ref), (flips_hbm, flips_ref),
    ]
    loads = [pltpu.make_async_copy(*x, load_sem.at[i]) for i, x in enumerate(pairs)]
    for load in loads:
        load.start()
    for load in loads[:3]:
        load.wait()

    row8, lane8 = iota((8, LANES), 0), iota((8, LANES), 1)

    for c in range(tile_count // LANES):
        tiles = slice(c * LANES, (c + 1) * LANES)
        order = jnp.zeros((SPLATS, LANES), jnp.int32)
        for g in range(SPLATS):
            order = jnp.where(depth_ref[g:g + 1, tiles] == row8, g, order)
        index = (lane8 & -SPLATS) + to_lanes(order)
        cover = along_lanes(
            jnp.broadcast_to(cover_ref[:, tiles], (8, LANES)), row8 * 16 + lane8 // SPLATS
        )
        part = slice(8 * c, 8 * c + 8)
        x = [gauss_ref[p, part, :] for p in range(9)]
        rho = 0.9 * jnp.tanh(x[4])
        scale = (0.5 * LOG2E) ** 0.5
        norm = lax.rsqrt(1.0 - rho * rho) * scale
        inv_y = jnp.exp(-x[3])
        values = [
            x[0],
            x[1],
            jnp.exp(-x[2]) * norm,
            inv_y * (rho * norm),
            inv_y * scale,
            0.99 * jax.nn.sigmoid(x[5]),
            jax.nn.sigmoid(x[6]),
            jax.nn.sigmoid(x[7]),
            jax.nn.sigmoid(x[8]),
        ]
        for p in range(9):
            value = along_lanes(values[p], index)
            if p == 5:
                value = jnp.maximum(jnp.log2(value * cover.astype(f32)), LOWEST)
            for j in range(per):
                shifted = pltpu.roll(value, LANES - j * group, 1) if j else value
                if per == 1:
                    send_ref[p, part, :] = shifted
                else:
                    send_ref[p, pl.ds(8 * c * per + j, 8, stride=per), :] = shifted

    for load in loads[3:7]:
        load.wait()
    bias = 0.5 * bias_ref[...].reshape(1, bias_ref.shape[0])
    half_ref[...] = first_ref[...] * bf16(0.5)
    second = jnp.broadcast_to(
        second_ref[...].astype(f32).reshape(1, second_ref.shape[0]), (16, second_ref.shape[0])
    ).astype(bf16)

    block = max(BLOCK, span)
    per_block = block // span

    def network(j, carry):
        feats = feat_ref[:, pl.ds(pl.multiple_of(j * block, block), block), :]
        feats = feats.reshape(stripe_tiles * block, feat_ref.shape[2])
        z = jnp.dot(feats, half_ref[...], preferred_element_type=f32) + bias
        hidden = z + z * jnp.tanh(z * (2.0 * GELU + (8.0 * 0.044715 * GELU) * (z * z)))
        hidden = hidden.reshape(stripe_tiles, per_block, span, hidden.shape[-1])
        for i in range(per_block):
            part = hidden[:, i].reshape(LANES, hidden.shape[-1]).astype(bf16)
            logits = lax.dot_general(
                second, part, (((1,), (1,)), ((), ())), preferred_element_type=f32,
            )
            spread_ref[pl.ds(j * per_block + i, 1), :] = logits[0:1]
        return carry

    steps = pixels // block
    early = min(EARLY, steps // 2)
    if early:
        lax.fori_loop(0, early, network, 0, unroll=UNROLL)
    pl.semaphore_wait(barrier, regions - 1)

    def send(i, carry):
        peer = lax.rem(me + i, regions)
        pltpu.make_async_remote_copy(
            src_ref=send_ref.at[:, pl.ds(peer, 1), :], dst_ref=recv_ref.at[:, pl.ds(me, 1), :],
            send_sem=send_sem, recv_sem=recv_sem.at[me // BATCH], device_id=(peer,),
            device_id_type=MESH,
        ).start()
        return carry

    lax.fori_loop(1, regions, send, 0)
    for p in range(9):
        recv_ref[p, pl.ds(me, 1), :] = send_ref[p, pl.ds(me, 1), :]
    lax.fori_loop(early, steps, network, 0, unroll=UNROLL)

    for load in loads[7:]:
        load.wait()
    tile_lane = same((LANES, stripe_tiles), lambda i: i // span, lambda j: j)
    lane_pixel = same((LANES, pixels), lambda i: i & (span - 1), lambda j: j & (span - 1))
    row_pixel = same((rows, pixels), lambda i: i, lambda j: j // span)
    for k in range(3):
        flat = jnp.concatenate(
            [target_ref[k:k + 1, t * pixels:(t + 1) * pixels] for t in range(stripe_tiles)], 0
        )
        wanted_ref[k] = dot(
            row_pixel, dot(tile_lane, flat, selector=0, pieces=2) * lane_pixel, True, selector=0, pieces=2
        )
    my_tiles = same(
        (tile_count, LANES), lambda i: i - me * stripe_tiles, lambda j: j // span
    ).astype(bf16)
    flip_ref[...] = jnp.dot(
        flips_ref[...].astype(f32).astype(bf16), my_tiles, preferred_element_type=f32,
    )

    wide = min(span, TSIDE)
    half = (TSIDE - wide) / 2

    def x_row(i):
        return ((i * span) & (TSIDE - 1)).astype(f32) - half

    def y_row(i):
        return (i * span // TSIDE).astype(f32) - 7.5

    x_lane = (lane8 & (wide - 1)).astype(f32) + (half + 0.5)
    y_lane = ((lane8 & (span - 1)) // TSIDE).astype(f32) + 8.0
    depth_rows = SPLATS * rows
    at = iota((SPLATS, depth_rows), 1)
    mine = at // rows == iota((SPLATS, depth_rows), 0)
    xr, yr = x_row(at & (rows - 1)), y_row(at & (rows - 1))
    terms = [jnp.ones_like(xr), xr, yr, xr * xr, xr * yr, yr * yr]
    basis_ref[...] = jnp.concatenate([jnp.where(mine, term, 0.0) for term in terms], 0).astype(bf16)
    ones_ref[...] = (
        iota(ones_ref.shape, 1) // 8 == iota(ones_ref.shape, 0)
    ).astype(f32).astype(bf16)
    for s in range(SPLATS):
        fold_ref[s * LANES:(s + 1) * LANES, :] = same(
            (LANES, LANES), lambda i: i // span * SPLATS + s, lambda j: j
        ).astype(bf16)

    for s in range(SPLATS):
        picks = same((LANES, LANES), lambda i: i, lambda j: j // span * SPLATS + s).astype(bf16)
        for k in range(3):
            widen_ref[k * LANES:(k + 1) * LANES, s * LANES:(s + 1) * LANES] = picks
    for buf in (rhs_ref, tone_ref, stage_ref):
        buf[...] = jnp.zeros(buf.shape, buf.dtype)

    def arrive(batch, count):
        some = pl.ds(0, count)
        pltpu.make_async_remote_copy(
            src_ref=send_ref.at[:, some, :], dst_ref=recv_ref.at[:, some, :],
            send_sem=send_sem, recv_sem=recv_sem.at[batch], device_id=(me,), device_id_type=MESH,
        ).wait_recv()

    def expand(c):
        base = pl.multiple_of(c * BATCH, BATCH)
        value = jnp.concatenate(
            [recv_ref[p, pl.ds(base, BATCH), :] for p in range(NPAR)], 0
        )
        pieces = []
        for _ in range(3):
            piece = value.astype(bf16)
            value = value - piece.astype(f32)
            pieces.append(piece)
        spread = jnp.dot(
            jnp.concatenate(pieces, 1), widen_ref[...], preferred_element_type=f32
        )
        for p in range(NPAR):
            for s in range(SPLATS):
                first = pl.multiple_of((c * NPAR + p) * SPLATS * BATCH, BATCH) + s * BATCH
                ex_ref[pl.ds(first, BATCH), :] = spread[
                    p * BATCH:(p + 1) * BATCH, s * LANES:(s + 1) * LANES
                ]

    vs = [slice(8 * v, 8 * v + 8) for v in range(nv)]
    xpos = x_row(row8) + x_lane
    ypos = y_row(row8) + y_lane
    step = float(8 * span // TSIDE)

    def first_row(r, p):
        return (r // BATCH * NPAR + p) * (SPLATS * BATCH) + (r & (BATCH - 1))

    def row(r, p, s):
        return ex_ref[pl.ds(first_row(r, p) + s * BATCH, 1), :]

    def forward(r, carry):
        trans = [jnp.ones((8, LANES), f32)] * nv
        color = [[jnp.zeros((8, LANES), f32)] * nv for _ in range(3)]
        for s in range(SPLATS):
            us = (xpos - row(r, 0, s)) * row(r, 2, s)
            m_y, skew, inv_y, level = row(r, 1, s), row(r, 3, s), row(r, 4, s), row(r, 5, s)
            ks = [row(r, 6 + k, s) for k in range(3)]
            dy = ypos - m_y
            w, p = dy * inv_y, us - dy * skew
            rise_w, rise_p = step * inv_y, step * skew
            for v in range(nv):
                if v:
                    w, p = w + rise_w, p - rise_p
                alpha = jnp.exp2(level - (p * p + w * w))
                weight = trans[v] * alpha
                a_ref[r * SPLATS + s, vs[v]] = alpha
                w_ref[r * SPLATS + s, vs[v]] = weight
                for k in range(3):
                    color[k][v] = color[k][v] + weight * ks[k]
                trans[v] = trans[v] - weight
        for v in range(nv):
            for k in range(3):
                tree_ref[inner + r, k, vs[v]] = color[k][v]
            tree_ref[inner + r, 3, vs[v]] = trans[v]
        return carry

    def render(i, carry):
        batch = lax.rem(me // BATCH + i, batches)

        @pl.when(i == 0)
        def _():
            arrive(batch, BATCH - 1)

        @pl.when(i > 0)
        def _():
            arrive(batch, BATCH)

        expand(batch)
        lax.fori_loop(0, BATCH, lambda j, c: forward(batch * BATCH + j, c), 0, unroll=FUNROLL)
        return carry

    lax.fori_loop(0, batches, render, 0)
    everyone = pl.ds(0, regions - 1)
    pltpu.make_async_remote_copy(
        src_ref=send_ref.at[:, everyone, :], dst_ref=recv_ref.at[:, everyone, :],
        send_sem=send_sem, recv_sem=recv_sem.at[0], device_id=(me,), device_id_type=MESH,
    ).wait_send()

    def flipped(n):
        return jnp.broadcast_to(flip_ref[pl.ds(n, 1), :], (8, LANES)) > 0.0

    def merge(n, v):
        if n >= inner:
            return [tree_ref[n, k, vs[v]] for k in range(4)]
        low, high = merge(2 * n + 1, v), merge(2 * n + 2, v)
        flip = flipped(n)
        over_low = jnp.where(flip, high[3], 1.0)
        over_high = jnp.where(flip, 1.0, low[3])
        both = [over_low * low[k] + over_high * high[k] for k in range(3)] + [low[3] * high[3]]
        for k in range(4):
            tree_ref[n, k, vs[v]] = both[k]
        return both

    for v in range(nv):
        merge(0, v)

    for v in range(nv):
        logit = spread_ref[vs[v]]
        spread = 0.5 + jnp.maximum(logit, 0.0) + jnp.log1p(jnp.exp(-jnp.abs(logit)))
        inv_square = 1.0 / (spread * spread)
        clear = tree_ref[0, 3, vs[v]]
        residual = [tree_ref[0, k, vs[v]] + clear - wanted_ref[k, vs[v]] for k in range(3)]
        total = residual[0] * residual[0] + residual[1] * residual[1] + residual[2] * residual[2]
        lossy_ref[vs[v]] = 0.5 * total * inv_square + jnp.log(spread)
        gs = [res * inv_square for res in residual]
        for k in range(3):
            g_ref[k, vs[v]] = gs[k]

    def split(n, v, g, front, behind):
        if n >= inner:
            down_ref[n - inner, 0, vs[v]] = front
            down_ref[n - inner, 1, vs[v]] = behind
            return
        flip = flipped(n)
        low = [tree_ref[2 * n + 1, k, vs[v]] for k in range(4)]
        high = [tree_ref[2 * n + 2, k, vs[v]] for k in range(4)]
        back = [jnp.where(flip, l, h) for l, h in zip(low, high)]
        through = front * jnp.where(flip, high[3], low[3])
        value = g[0] * back[0] + g[1] * back[1] + g[2] * back[2] + back[3] * behind
        split(2 * n + 1, v, g, jnp.where(flip, through, front), jnp.where(flip, behind, value))
        split(2 * n + 2, v, g, jnp.where(flip, front, through), jnp.where(flip, value, behind))

    for v in range(nv):
        g = [g_ref[k, vs[v]] for k in range(3)]
        split(0, v, g, jnp.ones((8, LANES), f32), g[0] + g[1] + g[2])

    def backward(r, slot):
        front = [down_ref[r, 0, vs[v]] for v in range(nv)]
        gs = [[front[v] * g_ref[k, vs[v]] for v in range(nv)] for k in range(3)]
        behind = [front[v] * down_ref[r, 1, vs[v]] for v in range(nv)]
        colors = [[], [], []]
        for s in reversed(range(SPLATS)):
            ks = [row(r, 6 + k, s) for k in range(3)]
            pulls, tones = [], [None] * 3
            for v in range(nv):
                alpha = a_ref[r * SPLATS + s, vs[v]]
                weight = w_ref[r * SPLATS + s, vs[v]]
                shade = ks[0] * gs[0][v] + ks[1] * gs[1][v] + ks[2] * gs[2][v]
                diff = shade - behind[v]
                behind[v] = behind[v] + alpha * diff
                pulls.append(weight * diff)
                for k in range(3):
                    tone = weight * gs[k][v]
                    tones[k] = tone if v == 0 else tones[k] + tone
            rhs_ref[slot, s * rows:(s + 1) * rows, :] = jnp.concatenate(pulls, 0).astype(bf16)
            for k in range(3):
                colors[k].insert(0, tones[k])
            if s % 2 == 0:
                for k in range(3):
                    tone_ref[slot, s * 8:(s + 2) * 8, k * LANES:(k + 1) * LANES] = (
                        jnp.concatenate(colors[k][:2], 0).astype(bf16)
                    )

    def reduce(r, slot):
        summed = jnp.dot(basis_ref[...], rhs_ref[slot], preferred_element_type=f32)
        toned = jnp.dot(ones_ref[...], tone_ref[slot], preferred_element_type=f32)
        h, hx, hy, hxx, hxy, hyy = [
            summed[b * SPLATS:(b + 1) * SPLATS] for b in range(NMOM)
        ]
        dx = x_lane - ex_ref[pl.ds(first_row(r, 0), SPLATS, stride=BATCH), :]
        dy = y_lane - ex_ref[pl.ds(first_row(r, 1), SPLATS, stride=BATCH), :]
        about_x = hx + dx * h
        about_y = hy + dy * h
        moments = [
            h,
            about_x,
            about_y,
            hxx + dx * (hx + about_x),
            hxy + dx * hy + dy * about_x,
            hyy + dy * (hy + about_y),
        ]
        for k in range(3):
            moments.append(toned[0:SPLATS, k * LANES:(k + 1) * LANES])
        for p in range(9):
            first = p * SPLATS * BATCH + (r & (BATCH - 1))
            stage_ref[pl.ds(first, SPLATS, stride=BATCH), :] = moments[p]

    def fold(base):
        wide = [
            jnp.concatenate(
                [stage_ref[(p * SPLATS + s) * BATCH:(p * SPLATS + s + 1) * BATCH, :] for s in range(SPLATS)], 1
            )
            for p in range(9)
        ]
        whole = jnp.concatenate(wide, 0)
        coarse = whole.astype(bf16).astype(f32)
        folded = jnp.dot(
            jnp.concatenate([coarse, whole - coarse], 0).astype(bf16), fold_ref[...],
            preferred_element_type=f32,
        )
        folded = folded[:9 * BATCH] + folded[9 * BATCH:]
        for p in range(9):
            gsend_ref[p, pl.ds(base, BATCH), :] = folded[p * BATCH:(p + 1) * BATCH]

    def give_back(base):
        def back(j, carry):
            peer = base + j

            @pl.when(peer != me)
            def _():
                pltpu.make_async_remote_copy(
                    src_ref=gsend_ref.at[:, pl.ds(peer, 1), :],
                    dst_ref=grads_hbm.at[:, pl.ds(me, 1), :],
                    send_sem=gsend_sem, recv_sem=grecv_sem,
                    device_id=(peer,), device_id_type=MESH,
                ).start()

            return carry

        lax.fori_loop(0, BATCH, back, 0)

    def base_of(i):
        return pl.multiple_of(lax.rem(i + batches - 1, batches) * BATCH, BATCH)

    def finish(i, carry):
        base, past = base_of(i + 1), base_of(i)
        for k in range(2):
            reduce(past + BATCH - 2 + k, k)
        fold(past)
        for k in range(2):
            backward(base + k, k)

        @pl.when(i > 0)
        def _():
            give_back(past)

        def pair(j, carry):
            r = base + 2 * j
            for k in range(2):
                reduce(r - 2 + k, k)
            for k in range(2):
                backward(r + k, k)
            return carry

        lax.fori_loop(1, BATCH // 2, pair, 0, unroll=PUNROLL)
        return carry

    lax.fori_loop(0, batches, finish, 0)
    last = base_of(batches)
    for k in range(2):
        reduce(last + BATCH - 2 + k, k)
    fold(last)
    give_back(last)
    own = pltpu.make_async_copy(
        gsend_ref.at[:, pl.ds(me, 1), :], grads_hbm.at[:, pl.ds(me, 1), :], own_sem
    )
    own.start()

    lane_tile = same((stripe_tiles, LANES), lambda i: i, lambda j: j // span)
    pixel_row = same((pixels, rows), lambda i: i // span, lambda j: j)
    pixel_lane = same((pixels, LANES), lambda i: i & (span - 1), lambda j: j & (span - 1))
    flat = dot(
        lane_tile, dot(pixel_row, lossy_ref[...], selector=0, pieces=2) * pixel_lane, True,
        selector=0, pieces=2,
    )
    for t in range(stripe_tiles):
        loss_ref[0:1, t * pixels:(t + 1) * pixels] = flat[t:t + 1]
    for c in range(tile_count // LANES):
        part = slice(8 * c, 8 * c + 8)
        place_ref[part, :] = (lane8 & -SPLATS) + to_lanes(depth_ref[:, c * LANES:(c + 1) * LANES])
        x = [gauss_ref[p, part, :] for p in range(9)]
        squash = jnp.tanh(x[4])
        rho = 0.9 * squash
        inv = 1.0 / (1.0 - rho * rho)
        tones = [jax.nn.sigmoid(x[6 + k]) for k in range(3)]
        factors = [
            jnp.exp(-x[2]), jnp.exp(-x[3]), inv, inv * rho,
            inv * (0.9 * (1.0 - squash * squash)), inv * rho * (0.9 * (1.0 - squash * squash)),
            jax.nn.sigmoid(-x[5]),
        ] + [tone * (1.0 - tone) for tone in tones]
        for p in range(10):
            factor_ref[p, part, :] = factors[p]
    keeps = [
        pltpu.make_async_copy(loss_ref, loss_hbm, keep_sem.at[0]),
        pltpu.make_async_copy(factor_ref, factor_hbm, keep_sem.at[1]),
        pltpu.make_async_copy(place_ref, place_hbm, keep_sem.at[2]),
    ]
    for keep in keeps:
        keep.start()

    pltpu.make_async_remote_copy(
        src_ref=gsend_ref.at[:, everyone, :], dst_ref=grads_hbm.at[:, everyone, :],
        send_sem=gsend_sem, recv_sem=grecv_sem, device_id=(me,), device_id_type=MESH,
    ).wait()
    own.wait()
    for keep in keeps:
        keep.wait()


def chain_kernel(moment_ref, factor_ref, place_ref, loss_in, grads_ref, loss_out):
    loss_out[...] = loss_in[...]
    regions, count = moment_ref.shape[1], place_ref.shape[0]
    per = regions // count
    group = LANES // per
    lane8 = iota((8, LANES), 1)
    for c in range(count // 8):
        part = slice(8 * c, 8 * c + 8)
        index = place_ref[part, :]
        sums = []
        for p in range(9):
            if per == 1:
                value = moment_ref[p, part, :]
            else:
                value = jnp.zeros((8, LANES), jnp.float32)
                for j in range(per):
                    piece = moment_ref[p, pl.ds(8 * c * per + j, 8, stride=per), :]
                    piece = pltpu.roll(piece, j * group, 1) if j else piece
                    value = jnp.where(lane8 // group == j, piece, value)
            sums.append(along_lanes(value, index))
        inv_x, inv_y, inv, skew, bend, lean, hide = [factor_ref[p, part, :] for p in range(7)]
        hu, hv = inv_x * sums[1], inv_y * sums[2]
        huu = inv_x * (inv_x * sums[3])
        huv = inv_x * (inv_y * sums[4])
        hvv = inv_y * (inv_y * sums[5])
        wide = inv * huu - skew * huv
        tall = inv * hvv - skew * huv
        results = [
            inv_x * (inv * hu - skew * hv),
            inv_y * (inv * hv - skew * hu),
            wide,
            tall,
            bend * huv - lean * (wide + tall),
            hide * sums[0],
        ]
        for k in range(3):
            results.append(sums[6 + k] * factor_ref[7 + k, part, :])
        for p in range(9):
            grads_ref[p, part, :] = results[p]


def shards(gaussians, depth, coverage, flips, features, w_first, b_first, w_second, target):
    regions = lax.axis_size("region")
    tile_count = depth.shape[1]
    stripe_tiles = tile_count // regions
    pixels = TSIDE * TSIDE
    rows = pixels * stripe_tiles // LANES
    nodes = 2 * regions - 1
    width = features.shape[1]
    f32, bf16 = jnp.float32, jnp.bfloat16
    dma = pltpu.SemaphoreType.DMA
    dense = gaussians.reshape(9, tile_count * SPLATS // LANES, LANES)
    ranks = depth[0].T
    anywhere = pl.BlockSpec(memory_space=pl.ANY)
    vmem = pl.BlockSpec(memory_space=pltpu.VMEM)
    operands = (
        dense,
        ranks,
        coverage,
        flips.T,
        features.reshape(stripe_tiles, pixels, width),
        w_first,
        b_first,
        w_second,
        target,
    )
    loss, moments, factors, places = pl.pallas_call(
        splat_kernel,
        out_shape=(
            jax.ShapeDtypeStruct((1, stripe_tiles * pixels), f32),
            jax.ShapeDtypeStruct((9, regions, LANES), f32),
            jax.ShapeDtypeStruct((10,) + dense.shape[1:], f32),
            jax.ShapeDtypeStruct(dense.shape[1:], jnp.int32),
        ),
        in_specs=[anywhere] * 9,
        out_specs=(anywhere,) * 4,
        scratch_shapes=[pltpu.VMEM(x.shape, x.dtype) for x in operands] + [
            dma((9,)),
            pltpu.VMEM(w_first.shape, w_first.dtype),
            pltpu.VMEM((1, stripe_tiles * pixels), f32),
            pltpu.VMEM((10,) + dense.shape[1:], f32),
            pltpu.VMEM(dense.shape[1:], jnp.int32),
            dma((3,)),
            dma(()),
            pltpu.VMEM((9, regions, LANES), f32),
            pltpu.VMEM((9, regions, LANES), f32),
            dma(()),
            dma((regions // BATCH,)),
            pltpu.VMEM((9, regions, LANES), f32),
            dma(()),
            dma(()),
            pltpu.VMEM((regions - 1, LANES), f32),
            pltpu.VMEM((rows, LANES), f32),
            pltpu.VMEM((3, rows, LANES), f32),
            pltpu.VMEM((NPAR * SPLATS * regions, LANES), f32),
            pltpu.VMEM((regions * SPLATS, rows, LANES), f32),
            pltpu.VMEM((regions * SPLATS, rows, LANES), f32),
            pltpu.VMEM((nodes, 4, rows, LANES), f32),
            pltpu.VMEM((regions, 2, rows, LANES), f32),
            pltpu.VMEM((3, rows, LANES), f32),
            pltpu.VMEM((rows, LANES), f32),
            pltpu.VMEM((2, SPLATS * rows, LANES), bf16),
            pltpu.VMEM((2, SPLATS * 8, 3 * LANES), bf16),
            pltpu.VMEM((9 * BATCH * SPLATS, LANES), f32),
            pltpu.VMEM((NMOM * SPLATS, SPLATS * rows), bf16),
            pltpu.VMEM((16, SPLATS * 8), bf16),
            pltpu.VMEM((SPLATS * LANES, LANES), bf16),
            pltpu.VMEM((3 * LANES, SPLATS * LANES), bf16),
        ],
        compiler_params=pltpu.CompilerParams(
            vmem_limit_bytes=56 * 1024 * 1024, collective_id=0, has_side_effects=True
        ),
    )(*operands)
    grads, loss = pl.pallas_call(
        chain_kernel,
        out_shape=(
            jax.ShapeDtypeStruct(dense.shape, f32), jax.ShapeDtypeStruct(loss.shape, f32)
        ),
        in_specs=[vmem] * 4,
        out_specs=(vmem, vmem),
    )(moments, factors, places, loss)
    return (loss.reshape(-1), grads.reshape(gaussians.shape))


def solution(mesh):
    placed = (
        P("region", None, None),
        P("region", None, None),
        P("region", None),
        P(),
        P("region", None),
        P(),
        P(),
        P(),
        P(None, "region"),
    )
    return jax.shard_map(
        shards,
        mesh=mesh,
        in_specs=placed,
        out_specs=(P("region"), P("region", None, None)),
        check_vma=False,
    )
```

```python
import jax
import jax.numpy as jnp
from jax import lax
from jax.experimental import pallas as pl
from jax.experimental.pallas import tpu as pltpu
from jax.sharding import PartitionSpec as P

TSIDE = 16
LANES = 128
SPLATS = 8
NPAR = 9
NMOM = 6
BATCH = 8
BLOCK = 32
UNROLL = 2
GELU = (2.0 / 3.141592653589793) ** 0.5
EARLY = 3
LOWEST = -1e4
FUNROLL = 8
PUNROLL = 3
LOG2E = 1.4426950408889634
MESH = pl.DeviceIdType.MESH


def iota(shape, dim):
    return lax.broadcasted_iota(jnp.int32, shape, dim)


def dot(x, y, transposed=False, selector=1, pieces=3):
    dims = (((1,), (1 if transposed else 0,)), ((), ()))
    bf16 = jnp.bfloat16
    sel, val = (y, x) if selector == 1 else (x, y)
    sel = sel.astype(bf16)
    total = None
    for _ in range(pieces):
        piece = val.astype(bf16)
        val = val - piece.astype(jnp.float32)
        pair = (piece, sel) if selector == 1 else (sel, piece)
        part = lax.dot_general(*pair, dims, preferred_element_type=jnp.float32)
        total = part if total is None else total + part
    return total


def same(shape, first, second):
    return (first(iota(shape, 0)) == second(iota(shape, 1))).astype(jnp.float32)


def along_lanes(x, index):
    return jnp.take_along_axis(x, index, axis=1)


def to_lanes(x):
    row, lane = iota((8, LANES), 0), iota((8, LANES), 1)
    x = along_lanes(x, ((lane // 16 - row) & 7) * 16 + (lane & 15))
    x = jnp.take_along_axis(x, (lane // 16 - row) & 7, axis=0)
    return along_lanes(x, ((row + (lane & 7)) & 7) * 16 + lane // 8)


def splat_kernel(
    gauss_hbm, depth_hbm, cover_hbm, flips_hbm, feat_hbm, first_hbm, bias_hbm, second_hbm,
    target_hbm, loss_hbm, grads_hbm, factor_hbm, place_hbm,
    gauss_ref, depth_ref, cover_ref, flips_ref, feat_ref, first_ref, bias_ref, second_ref,
    target_ref, load_sem, half_ref, loss_ref, factor_ref, place_ref, keep_sem, own_sem, send_ref, recv_ref, send_sem, recv_sem, gsend_ref, gsend_sem,
    grecv_sem, flip_ref, spread_ref, wanted_ref,
    ex_ref, a_ref, w_ref, tree_ref, down_ref, g_ref, lossy_ref, rhs_ref, tone_ref, stage_ref,
    basis_ref, ones_ref, fold_ref, widen_ref,
):
    regions = recv_ref.shape[1]
    rows = wanted_ref.shape[1]
    nv = rows // 8
    tile_count = depth_ref.shape[1]
    stripe_tiles = tile_count // regions
    group = stripe_tiles * SPLATS
    per = LANES // group
    span = LANES // stripe_tiles
    inner = regions - 1
    batches = regions // BATCH
    pixels = TSIDE * TSIDE
    f32, bf16 = jnp.float32, jnp.bfloat16
    me = lax.axis_index("region")

    barrier = pltpu.get_barrier_semaphore()

    def greet(i, carry):
        pl.semaphore_signal(
            barrier, inc=1, device_id=(lax.rem(me + i, regions),), device_id_type=MESH
        )
        return carry

    lax.fori_loop(1, regions, greet, 0, unroll=True)
    pairs = [
        (gauss_hbm, gauss_ref), (depth_hbm, depth_ref), (cover_hbm, cover_ref),
        (feat_hbm, feat_ref), (first_hbm, first_ref), (bias_hbm, bias_ref),
        (second_hbm, second_ref), (target_hbm, target_ref), (flips_hbm, flips_ref),
    ]
    loads = [pltpu.make_async_copy(*x, load_sem.at[i]) for i, x in enumerate(pairs)]
    for load in loads:
        load.start()
    for load in loads[:3]:
        load.wait()

    row8, lane8 = iota((8, LANES), 0), iota((8, LANES), 1)

    for c in range(tile_count // LANES):
        tiles = slice(c * LANES, (c + 1) * LANES)
        order = jnp.zeros((SPLATS, LANES), jnp.int32)
        for g in range(SPLATS):
            order = jnp.where(depth_ref[g:g + 1, tiles] == row8, g, order)
        index = (lane8 & -SPLATS) + to_lanes(order)
        cover = along_lanes(
            jnp.broadcast_to(cover_ref[:, tiles], (8, LANES)), row8 * 16 + lane8 // SPLATS
        )
        part = slice(8 * c, 8 * c + 8)
        x = [gauss_ref[p, part, :] for p in range(9)]
        rho = 0.9 * jnp.tanh(x[4])
        scale = (0.5 * LOG2E) ** 0.5
        norm = lax.rsqrt(1.0 - rho * rho) * scale
        inv_y = jnp.exp(-x[3])
        values = [
            x[0],
            x[1],
            jnp.exp(-x[2]) * norm,
            inv_y * (rho * norm),
            inv_y * scale,
            0.99 * jax.nn.sigmoid(x[5]),
            jax.nn.sigmoid(x[6]),
            jax.nn.sigmoid(x[7]),
            jax.nn.sigmoid(x[8]),
        ]
        for p in range(9):
            value = along_lanes(values[p], index)
            if p == 5:
                value = jnp.maximum(jnp.log2(value * cover.astype(f32)), LOWEST)
            for j in range(per):
                shifted = pltpu.roll(value, LANES - j * group, 1) if j else value
                if per == 1:
                    send_ref[p, part, :] = shifted
                else:
                    send_ref[p, pl.ds(8 * c * per + j, 8, stride=per), :] = shifted

    for load in loads[3:7]:
        load.wait()
    bias = 0.5 * bias_ref[...].reshape(1, bias_ref.shape[0])
    half_ref[...] = first_ref[...] * bf16(0.5)
    second = jnp.broadcast_to(
        second_ref[...].astype(f32).reshape(1, second_ref.shape[0]), (16, second_ref.shape[0])
    ).astype(bf16)

    block = max(BLOCK, span)
    per_block = block // span

    def network(j, carry):
        feats = feat_ref[:, pl.ds(pl.multiple_of(j * block, block), block), :]
        feats = feats.reshape(stripe_tiles * block, feat_ref.shape[2])
        z = jnp.dot(feats, half_ref[...], preferred_element_type=f32) + bias
        hidden = z + z * jnp.tanh(z * (2.0 * GELU + (8.0 * 0.044715 * GELU) * (z * z)))
        hidden = hidden.reshape(stripe_tiles, per_block, span, hidden.shape[-1])
        for i in range(per_block):
            part = hidden[:, i].reshape(LANES, hidden.shape[-1]).astype(bf16)
            logits = lax.dot_general(
                second, part, (((1,), (1,)), ((), ())), preferred_element_type=f32,
            )
            spread_ref[pl.ds(j * per_block + i, 1), :] = logits[0:1]
        return carry

    steps = pixels // block
    early = min(EARLY, steps // 2)
    if early:
        lax.fori_loop(0, early, network, 0, unroll=UNROLL)
    pl.semaphore_wait(barrier, regions - 1)

    def send(i, carry):
        peer = lax.rem(me + i, regions)
        pltpu.make_async_remote_copy(
            src_ref=send_ref.at[:, pl.ds(peer, 1), :], dst_ref=recv_ref.at[:, pl.ds(me, 1), :],
            send_sem=send_sem, recv_sem=recv_sem.at[me // BATCH], device_id=(peer,),
            device_id_type=MESH,
        ).start()
        return carry

    lax.fori_loop(1, regions, send, 0, unroll=True)
    for p in range(9):
        recv_ref[p, pl.ds(me, 1), :] = send_ref[p, pl.ds(me, 1), :]
    lax.fori_loop(early, steps, network, 0, unroll=UNROLL)

    for load in loads[7:]:
        load.wait()
    tile_lane = same((LANES, stripe_tiles), lambda i: i // span, lambda j: j)
    lane_pixel = same((LANES, pixels), lambda i: i & (span - 1), lambda j: j & (span - 1))
    row_pixel = same((rows, pixels), lambda i: i, lambda j: j // span)
    for k in range(3):
        flat = jnp.concatenate(
            [target_ref[k:k + 1, t * pixels:(t + 1) * pixels] for t in range(stripe_tiles)], 0
        )
        wanted_ref[k] = dot(
            row_pixel, dot(tile_lane, flat, selector=0, pieces=2) * lane_pixel, True, selector=0, pieces=2
        )
    my_tiles = same(
        (tile_count, LANES), lambda i: i - me * stripe_tiles, lambda j: j // span
    ).astype(bf16)
    flip_ref[...] = jnp.dot(
        flips_ref[...].astype(f32).astype(bf16), my_tiles, preferred_element_type=f32,
    )

    wide = min(span, TSIDE)
    half = (TSIDE - wide) / 2

    def x_row(i):
        return ((i * span) & (TSIDE - 1)).astype(f32) - half

    def y_row(i):
        return (i * span // TSIDE).astype(f32) - 7.5

    x_lane = (lane8 & (wide - 1)).astype(f32) + (half + 0.5)
    y_lane = ((lane8 & (span - 1)) // TSIDE).astype(f32) + 8.0
    depth_rows = SPLATS * rows
    at = iota((SPLATS, depth_rows), 1)
    mine = at // rows == iota((SPLATS, depth_rows), 0)
    xr, yr = x_row(at & (rows - 1)), y_row(at & (rows - 1))
    terms = [jnp.ones_like(xr), xr, yr, xr * xr, xr * yr, yr * yr]
    basis_ref[...] = jnp.concatenate([jnp.where(mine, term, 0.0) for term in terms], 0).astype(bf16)
    ones_ref[...] = (
        iota(ones_ref.shape, 1) // 8 == iota(ones_ref.shape, 0)
    ).astype(f32).astype(bf16)
    for s in range(SPLATS):
        fold_ref[s * LANES:(s + 1) * LANES, :] = same(
            (LANES, LANES), lambda i: i // span * SPLATS + s, lambda j: j
        ).astype(bf16)

    for s in range(SPLATS):
        picks = same((LANES, LANES), lambda i: i, lambda j: j // span * SPLATS + s).astype(bf16)
        widen_ref[:, s * LANES:(s + 1) * LANES] = picks
    for buf in (rhs_ref, tone_ref, stage_ref):
        buf[...] = jnp.zeros(buf.shape, buf.dtype)

    def arrive(batch, count):
        some = pl.ds(0, count)
        pltpu.make_async_remote_copy(
            src_ref=send_ref.at[:, some, :], dst_ref=recv_ref.at[:, some, :],
            send_sem=send_sem, recv_sem=recv_sem.at[batch], device_id=(me,), device_id_type=MESH,
        ).wait_recv()

    def expand(c):
        base = pl.multiple_of(c * BATCH, BATCH)
        value = jnp.concatenate(
            [recv_ref[p, pl.ds(base, BATCH), :] for p in range(NPAR)], 0
        )
        pieces = []
        for _ in range(3):
            piece = value.astype(bf16).astype(f32)
            value = value - piece
            pieces.append(piece)
        spread = jnp.dot(
            jnp.concatenate(pieces, 0).astype(bf16), widen_ref[...], preferred_element_type=f32
        )
        count = NPAR * BATCH
        spread = spread[:count] + spread[count:2 * count] + spread[2 * count:]
        for p in range(NPAR):
            for s in range(SPLATS):
                first = pl.multiple_of((c * NPAR + p) * SPLATS * BATCH, BATCH) + s * BATCH
                ex_ref[pl.ds(first, BATCH), :] = spread[
                    p * BATCH:(p + 1) * BATCH, s * LANES:(s + 1) * LANES
                ]

    vs = [slice(8 * v, 8 * v + 8) for v in range(nv)]
    xpos = x_row(row8) + x_lane
    ypos = y_row(row8) + y_lane
    step = float(8 * span // TSIDE)

    def first_row(r, p):
        return (r // BATCH * NPAR + p) * (SPLATS * BATCH) + (r & (BATCH - 1))

    def row(r, p, s):
        return ex_ref[pl.ds(first_row(r, p) + s * BATCH, 1), :]

    def forward(r, carry):
        trans = [jnp.ones((8, LANES), f32)] * nv
        color = [[jnp.zeros((8, LANES), f32)] * nv for _ in range(3)]
        for s in range(SPLATS):
            us = (xpos - row(r, 0, s)) * row(r, 2, s)
            m_y, skew, inv_y, level = row(r, 1, s), row(r, 3, s), row(r, 4, s), row(r, 5, s)
            ks = [row(r, 6 + k, s) for k in range(3)]
            dy = ypos - m_y
            w, p = dy * inv_y, us - dy * skew
            rise_w, rise_p = step * inv_y, step * skew
            for v in range(nv):
                if v:
                    w, p = w + rise_w, p - rise_p
                alpha = jnp.exp2(level - (p * p + w * w))
                weight = trans[v] * alpha
                a_ref[r * SPLATS + s, vs[v]] = alpha
                w_ref[r * SPLATS + s, vs[v]] = weight
                for k in range(3):
                    color[k][v] = color[k][v] + weight * ks[k]
                trans[v] = trans[v] - weight
        for v in range(nv):
            for k in range(3):
                tree_ref[inner + r, k, vs[v]] = color[k][v]
            tree_ref[inner + r, 3, vs[v]] = trans[v]
        return carry

    def render(i, carry):
        batch = lax.rem(me // BATCH + i, batches)

        @pl.when(i == 0)
        def _():
            arrive(batch, BATCH - 1)

        @pl.when(i > 0)
        def _():
            arrive(batch, BATCH)

        expand(batch)
        lax.fori_loop(0, BATCH, lambda j, c: forward(batch * BATCH + j, c), 0, unroll=FUNROLL)
        return carry

    lax.fori_loop(0, batches, render, 0)
    everyone = pl.ds(0, regions - 1)
    pltpu.make_async_remote_copy(
        src_ref=send_ref.at[:, everyone, :], dst_ref=recv_ref.at[:, everyone, :],
        send_sem=send_sem, recv_sem=recv_sem.at[0], device_id=(me,), device_id_type=MESH,
    ).wait_send()

    def flipped(n):
        return jnp.broadcast_to(flip_ref[pl.ds(n, 1), :], (8, LANES)) > 0.0

    def merge(n, v):
        if n >= inner:
            return [tree_ref[n, k, vs[v]] for k in range(4)]
        low, high = merge(2 * n + 1, v), merge(2 * n + 2, v)
        flip = flipped(n)
        over_low = jnp.where(flip, high[3], 1.0)
        over_high = jnp.where(flip, 1.0, low[3])
        both = [over_low * low[k] + over_high * high[k] for k in range(3)] + [low[3] * high[3]]
        for k in range(4):
            tree_ref[n, k, vs[v]] = both[k]
        return both

    for v in range(nv):
        merge(0, v)

    for v in range(nv):
        logit = spread_ref[vs[v]]
        spread = 0.5 + jnp.maximum(logit, 0.0) + jnp.log1p(jnp.exp(-jnp.abs(logit)))
        inv_square = 1.0 / (spread * spread)
        clear = tree_ref[0, 3, vs[v]]
        residual = [tree_ref[0, k, vs[v]] + clear - wanted_ref[k, vs[v]] for k in range(3)]
        total = residual[0] * residual[0] + residual[1] * residual[1] + residual[2] * residual[2]
        lossy_ref[vs[v]] = 0.5 * total * inv_square + jnp.log(spread)
        gs = [res * inv_square for res in residual]
        for k in range(3):
            g_ref[k, vs[v]] = gs[k]

    def split(n, v, g, front, behind):
        if n >= inner:
            down_ref[n - inner, 0, vs[v]] = front
            down_ref[n - inner, 1, vs[v]] = behind
            return
        flip = flipped(n)
        low = [tree_ref[2 * n + 1, k, vs[v]] for k in range(4)]
        high = [tree_ref[2 * n + 2, k, vs[v]] for k in range(4)]
        back = [jnp.where(flip, l, h) for l, h in zip(low, high)]
        through = front * jnp.where(flip, high[3], low[3])
        value = g[0] * back[0] + g[1] * back[1] + g[2] * back[2] + back[3] * behind
        split(2 * n + 1, v, g, jnp.where(flip, through, front), jnp.where(flip, behind, value))
        split(2 * n + 2, v, g, jnp.where(flip, front, through), jnp.where(flip, value, behind))

    for v in range(nv):
        g = [g_ref[k, vs[v]] for k in range(3)]
        split(0, v, g, jnp.ones((8, LANES), f32), g[0] + g[1] + g[2])

    def backward(r, slot):
        front = [down_ref[r, 0, vs[v]] for v in range(nv)]
        gs = [[front[v] * g_ref[k, vs[v]] for v in range(nv)] for k in range(3)]
        behind = [front[v] * down_ref[r, 1, vs[v]] for v in range(nv)]
        colors = [[], [], []]
        for s in reversed(range(SPLATS)):
            ks = [row(r, 6 + k, s) for k in range(3)]
            pulls, tones = [], [None] * 3
            for v in range(nv):
                alpha = a_ref[r * SPLATS + s, vs[v]]
                weight = w_ref[r * SPLATS + s, vs[v]]
                shade = ks[0] * gs[0][v] + ks[1] * gs[1][v] + ks[2] * gs[2][v]
                diff = shade - behind[v]
                behind[v] = behind[v] + alpha * diff
                pulls.append(weight * diff)
                for k in range(3):
                    tone = weight * gs[k][v]
                    tones[k] = tone if v == 0 else tones[k] + tone
            rhs_ref[slot, s * rows:(s + 1) * rows, :] = jnp.concatenate(pulls, 0).astype(bf16)
            for k in range(3):
                colors[k].insert(0, tones[k])
            if s % 2 == 0:
                for k in range(3):
                    tone_ref[slot, s * 8:(s + 2) * 8, k * LANES:(k + 1) * LANES] = (
                        jnp.concatenate(colors[k][:2], 0).astype(bf16)
                    )

    def reduce(r, slot):
        summed = jnp.dot(basis_ref[...], rhs_ref[slot], preferred_element_type=f32)
        toned = jnp.dot(ones_ref[...], tone_ref[slot], preferred_element_type=f32)
        h, hx, hy, hxx, hxy, hyy = [
            summed[b * SPLATS:(b + 1) * SPLATS] for b in range(NMOM)
        ]
        dx = x_lane - ex_ref[pl.ds(first_row(r, 0), SPLATS, stride=BATCH), :]
        dy = y_lane - ex_ref[pl.ds(first_row(r, 1), SPLATS, stride=BATCH), :]
        about_x = hx + dx * h
        about_y = hy + dy * h
        moments = [
            h,
            about_x,
            about_y,
            hxx + dx * (hx + about_x),
            hxy + dx * hy + dy * about_x,
            hyy + dy * (hy + about_y),
        ]
        for k in range(3):
            moments.append(toned[0:SPLATS, k * LANES:(k + 1) * LANES])
        for p in range(9):
            first = p * SPLATS * BATCH + (r & (BATCH - 1))
            stage_ref[pl.ds(first, SPLATS, stride=BATCH), :] = moments[p]

    def fold(base):
        wide = [
            jnp.concatenate(
                [stage_ref[(p * SPLATS + s) * BATCH:(p * SPLATS + s + 1) * BATCH, :] for s in range(SPLATS)], 1
            )
            for p in range(9)
        ]
        whole = jnp.concatenate(wide, 0)
        coarse = whole.astype(bf16).astype(f32)
        folded = jnp.dot(
            jnp.concatenate([coarse, whole - coarse], 0).astype(bf16), fold_ref[...],
            preferred_element_type=f32,
        )
        folded = folded[:9 * BATCH] + folded[9 * BATCH:]
        for p in range(9):
            gsend_ref[p, pl.ds(base, BATCH), :] = folded[p * BATCH:(p + 1) * BATCH]

    def give_back(base):
        def back(j, carry):
            peer = base + j

            @pl.when(peer != me)
            def _():
                pltpu.make_async_remote_copy(
                    src_ref=gsend_ref.at[:, pl.ds(peer, 1), :],
                    dst_ref=grads_hbm.at[:, pl.ds(me, 1), :],
                    send_sem=gsend_sem, recv_sem=grecv_sem,
                    device_id=(peer,), device_id_type=MESH,
                ).start()

            return carry

        lax.fori_loop(0, BATCH, back, 0, unroll=True)

    def base_of(i):
        return pl.multiple_of(lax.rem(i + batches - 1, batches) * BATCH, BATCH)

    def finish(i, carry):
        base, past = base_of(i + 1), base_of(i)
        for k in range(2):
            reduce(past + BATCH - 2 + k, k)
        fold(past)
        for k in range(2):
            backward(base + k, k)

        @pl.when(i > 0)
        def _():
            give_back(past)

        def pair(j, carry):
            r = base + 2 * j
            for k in range(2):
                reduce(r - 2 + k, k)
            for k in range(2):
                backward(r + k, k)
            return carry

        lax.fori_loop(1, BATCH // 2, pair, 0, unroll=PUNROLL)
        return carry

    lax.fori_loop(0, batches, finish, 0)
    last = base_of(batches)
    for k in range(2):
        reduce(last + BATCH - 2 + k, k)
    fold(last)
    give_back(last)
    own = pltpu.make_async_copy(
        gsend_ref.at[:, pl.ds(me, 1), :], grads_hbm.at[:, pl.ds(me, 1), :], own_sem
    )
    own.start()

    lane_tile = same((stripe_tiles, LANES), lambda i: i, lambda j: j // span)
    pixel_row = same((pixels, rows), lambda i: i // span, lambda j: j)
    pixel_lane = same((pixels, LANES), lambda i: i & (span - 1), lambda j: j & (span - 1))
    flat = dot(
        lane_tile, dot(pixel_row, lossy_ref[...], selector=0, pieces=2) * pixel_lane, True,
        selector=0, pieces=2,
    )
    for t in range(stripe_tiles):
        loss_ref[0:1, t * pixels:(t + 1) * pixels] = flat[t:t + 1]
    for c in range(tile_count // LANES):
        part = slice(8 * c, 8 * c + 8)
        place_ref[part, :] = (lane8 & -SPLATS) + to_lanes(depth_ref[:, c * LANES:(c + 1) * LANES])
        x = [gauss_ref[p, part, :] for p in range(9)]
        squash = jnp.tanh(x[4])
        rho = 0.9 * squash
        inv = 1.0 / (1.0 - rho * rho)
        tones = [jax.nn.sigmoid(x[6 + k]) for k in range(3)]
        factors = [
            jnp.exp(-x[2]), jnp.exp(-x[3]), inv, inv * rho,
            inv * (0.9 * (1.0 - squash * squash)), inv * rho * (0.9 * (1.0 - squash * squash)),
            jax.nn.sigmoid(-x[5]),
        ] + [tone * (1.0 - tone) for tone in tones]
        for p in range(10):
            factor_ref[p, part, :] = factors[p]
    keeps = [
        pltpu.make_async_copy(loss_ref, loss_hbm, keep_sem.at[0]),
        pltpu.make_async_copy(factor_ref, factor_hbm, keep_sem.at[1]),
        pltpu.make_async_copy(place_ref, place_hbm, keep_sem.at[2]),
    ]
    for keep in keeps:
        keep.start()

    pltpu.make_async_remote_copy(
        src_ref=gsend_ref.at[:, everyone, :], dst_ref=grads_hbm.at[:, everyone, :],
        send_sem=gsend_sem, recv_sem=grecv_sem, device_id=(me,), device_id_type=MESH,
    ).wait()
    own.wait()
    for keep in keeps:
        keep.wait()


def chain_kernel(moment_ref, factor_ref, place_ref, loss_in, grads_ref, loss_out):
    loss_out[...] = loss_in[...]
    regions, count = moment_ref.shape[1], place_ref.shape[0]
    per = regions // count
    group = LANES // per
    lane8 = iota((8, LANES), 1)
    for c in range(count // 8):
        part = slice(8 * c, 8 * c + 8)
        index = place_ref[part, :]
        sums = []
        for p in range(9):
            if per == 1:
                value = moment_ref[p, part, :]
            else:
                value = jnp.zeros((8, LANES), jnp.float32)
                for j in range(per):
                    piece = moment_ref[p, pl.ds(8 * c * per + j, 8, stride=per), :]
                    piece = pltpu.roll(piece, j * group, 1) if j else piece
                    value = jnp.where(lane8 // group == j, piece, value)
            sums.append(along_lanes(value, index))
        inv_x, inv_y, inv, skew, bend, lean, hide = [factor_ref[p, part, :] for p in range(7)]
        hu, hv = inv_x * sums[1], inv_y * sums[2]
        huu = inv_x * (inv_x * sums[3])
        huv = inv_x * (inv_y * sums[4])
        hvv = inv_y * (inv_y * sums[5])
        wide = inv * huu - skew * huv
        tall = inv * hvv - skew * huv
        results = [
            inv_x * (inv * hu - skew * hv),
            inv_y * (inv * hv - skew * hu),
            wide,
            tall,
            bend * huv - lean * (wide + tall),
            hide * sums[0],
        ]
        for k in range(3):
            results.append(sums[6 + k] * factor_ref[7 + k, part, :])
        for p in range(9):
            grads_ref[p, part, :] = results[p]


def shards(gaussians, depth, coverage, flips, features, w_first, b_first, w_second, target):
    regions = lax.axis_size("region")
    tile_count = depth.shape[1]
    stripe_tiles = tile_count // regions
    pixels = TSIDE * TSIDE
    rows = pixels * stripe_tiles // LANES
    nodes = 2 * regions - 1
    width = features.shape[1]
    f32, bf16 = jnp.float32, jnp.bfloat16
    dma = pltpu.SemaphoreType.DMA
    dense = gaussians.reshape(9, tile_count * SPLATS // LANES, LANES)
    ranks = depth[0].T
    anywhere = pl.BlockSpec(memory_space=pl.ANY)
    vmem = pl.BlockSpec(memory_space=pltpu.VMEM)
    operands = (
        dense,
        ranks,
        coverage,
        flips.T,
        features.reshape(stripe_tiles, pixels, width),
        w_first,
        b_first,
        w_second,
        target,
    )
    loss, moments, factors, places = pl.pallas_call(
        splat_kernel,
        out_shape=(
            jax.ShapeDtypeStruct((1, stripe_tiles * pixels), f32),
            jax.ShapeDtypeStruct((9, regions, LANES), f32),
            jax.ShapeDtypeStruct((10,) + dense.shape[1:], f32),
            jax.ShapeDtypeStruct(dense.shape[1:], jnp.int32),
        ),
        in_specs=[anywhere] * 9,
        out_specs=(anywhere,) * 4,
        scratch_shapes=[pltpu.VMEM(x.shape, x.dtype) for x in operands] + [
            dma((9,)),
            pltpu.VMEM(w_first.shape, w_first.dtype),
            pltpu.VMEM((1, stripe_tiles * pixels), f32),
            pltpu.VMEM((10,) + dense.shape[1:], f32),
            pltpu.VMEM(dense.shape[1:], jnp.int32),
            dma((3,)),
            dma(()),
            pltpu.VMEM((9, regions, LANES), f32),
            pltpu.VMEM((9, regions, LANES), f32),
            dma(()),
            dma((regions // BATCH,)),
            pltpu.VMEM((9, regions, LANES), f32),
            dma(()),
            dma(()),
            pltpu.VMEM((regions - 1, LANES), f32),
            pltpu.VMEM((rows, LANES), f32),
            pltpu.VMEM((3, rows, LANES), f32),
            pltpu.VMEM((NPAR * SPLATS * regions, LANES), f32),
            pltpu.VMEM((regions * SPLATS, rows, LANES), f32),
            pltpu.VMEM((regions * SPLATS, rows, LANES), f32),
            pltpu.VMEM((nodes, 4, rows, LANES), f32),
            pltpu.VMEM((regions, 2, rows, LANES), f32),
            pltpu.VMEM((3, rows, LANES), f32),
            pltpu.VMEM((rows, LANES), f32),
            pltpu.VMEM((2, SPLATS * rows, LANES), bf16),
            pltpu.VMEM((2, SPLATS * 8, 3 * LANES), bf16),
            pltpu.VMEM((9 * BATCH * SPLATS, LANES), f32),
            pltpu.VMEM((NMOM * SPLATS, SPLATS * rows), bf16),
            pltpu.VMEM((16, SPLATS * 8), bf16),
            pltpu.VMEM((SPLATS * LANES, LANES), bf16),
            pltpu.VMEM((LANES, SPLATS * LANES), bf16),
        ],
        compiler_params=pltpu.CompilerParams(
            vmem_limit_bytes=56 * 1024 * 1024, collective_id=0, has_side_effects=True
        ),
    )(*operands)
    grads, loss = pl.pallas_call(
        chain_kernel,
        out_shape=(
            jax.ShapeDtypeStruct(dense.shape, f32), jax.ShapeDtypeStruct(loss.shape, f32)
        ),
        in_specs=[vmem] * 4,
        out_specs=(vmem, vmem),
    )(moments, factors, places, loss)
    return (loss.reshape(-1), grads.reshape(gaussians.shape))


def solution(mesh):
    placed = (
        P("region", None, None),
        P("region", None, None),
        P("region", None),
        P(),
        P("region", None),
        P(),
        P(),
        P(),
        P(None, "region"),
    )
    return jax.shard_map(
        shards,
        mesh=mesh,
        in_specs=placed,
        out_specs=(P("region"), P("region", None, None)),
        check_vma=False,
    )
```

```python
import jax
import jax.numpy as jnp
from jax import lax
from jax.experimental import pallas as pl
from jax.experimental.pallas import tpu as pltpu
from jax.sharding import PartitionSpec as P

TSIDE = 16
LANES = 128
SPLATS = 8
NPAR = 9
NMOM = 6
BATCH = 8
BLOCK = 32
UNROLL = 2
GELU = (2.0 / 3.141592653589793) ** 0.5
EARLY = 3
LOWEST = -1e4
FUNROLL = 8
PUNROLL = 3
LOG2E = 1.4426950408889634
MESH = pl.DeviceIdType.MESH


def iota(shape, dim):
    return lax.broadcasted_iota(jnp.int32, shape, dim)


def dot(x, y, transposed=False, selector=1, pieces=3):
    dims = (((1,), (1 if transposed else 0,)), ((), ()))
    bf16 = jnp.bfloat16
    sel, val = (y, x) if selector == 1 else (x, y)
    sel = sel.astype(bf16)
    total = None
    for _ in range(pieces):
        piece = val.astype(bf16)
        val = val - piece.astype(jnp.float32)
        pair = (piece, sel) if selector == 1 else (sel, piece)
        part = lax.dot_general(*pair, dims, preferred_element_type=jnp.float32)
        total = part if total is None else total + part
    return total


def same(shape, first, second):
    return (first(iota(shape, 0)) == second(iota(shape, 1))).astype(jnp.float32)


def along_lanes(x, index):
    return jnp.take_along_axis(x, index, axis=1)


def to_lanes(x):
    row, lane = iota((8, LANES), 0), iota((8, LANES), 1)
    x = along_lanes(x, ((lane // 16 - row) & 7) * 16 + (lane & 15))
    x = jnp.take_along_axis(x, (lane // 16 - row) & 7, axis=0)
    return along_lanes(x, ((row + (lane & 7)) & 7) * 16 + lane // 8)


def splat_kernel(
    gauss_hbm, depth_hbm, cover_hbm, flips_hbm, feat_hbm, first_hbm, bias_hbm, second_hbm,
    target_hbm, loss_hbm, grads_hbm, factor_hbm, place_hbm,
    gauss_ref, depth_ref, cover_ref, flips_ref, feat_ref, first_ref, bias_ref, second_ref,
    target_ref, load_sem, half_ref, loss_ref, factor_ref, place_ref, keep_sem, own_sem, send_ref, recv_ref, send_sem, recv_sem, gsend_ref, gsend_sem,
    grecv_sem, flip_ref, spread_ref, wanted_ref,
    ex_ref, a_ref, w_ref, tree_ref, down_ref, g_ref, lossy_ref, rhs_ref, tone_ref, stage_ref,
    basis_ref, ones_ref, fold_ref, widen_ref,
):
    regions = recv_ref.shape[1]
    rows = wanted_ref.shape[1]
    nv = rows // 8
    tile_count = depth_ref.shape[1]
    stripe_tiles = tile_count // regions
    group = stripe_tiles * SPLATS
    per = LANES // group
    span = LANES // stripe_tiles
    inner = regions - 1
    batches = regions // BATCH
    pixels = TSIDE * TSIDE
    f32, bf16 = jnp.float32, jnp.bfloat16
    me = lax.axis_index("region")

    barrier = pltpu.get_barrier_semaphore()

    def greet(i, carry):
        pl.semaphore_signal(
            barrier, inc=1, device_id=(lax.rem(me + i, regions),), device_id_type=MESH
        )
        return carry

    pairs = [
        (gauss_hbm, gauss_ref), (depth_hbm, depth_ref), (cover_hbm, cover_ref),
        (feat_hbm, feat_ref), (first_hbm, first_ref), (bias_hbm, bias_ref),
        (second_hbm, second_ref), (target_hbm, target_ref), (flips_hbm, flips_ref),
    ]
    loads = [pltpu.make_async_copy(*x, load_sem.at[i]) for i, x in enumerate(pairs)]
    for load in loads[:3]:
        load.start()
    lax.fori_loop(1, regions, greet, 0, unroll=True)
    for load in loads[3:]:
        load.start()
    for load in loads[:3]:
        load.wait()

    row8, lane8 = iota((8, LANES), 0), iota((8, LANES), 1)

    for c in range(tile_count // LANES):
        tiles = slice(c * LANES, (c + 1) * LANES)
        order = jnp.zeros((SPLATS, LANES), jnp.int32)
        for g in range(SPLATS):
            order = jnp.where(depth_ref[g:g + 1, tiles] == row8, g, order)
        index = (lane8 & -SPLATS) + to_lanes(order)
        cover = along_lanes(
            jnp.broadcast_to(cover_ref[:, tiles], (8, LANES)), row8 * 16 + lane8 // SPLATS
        )
        part = slice(8 * c, 8 * c + 8)
        x = [gauss_ref[p, part, :] for p in range(9)]
        rho = 0.9 * jnp.tanh(x[4])
        scale = (0.5 * LOG2E) ** 0.5
        norm = lax.rsqrt(1.0 - rho * rho) * scale
        inv_y = jnp.exp(-x[3])
        values = [
            x[0],
            x[1],
            jnp.exp(-x[2]) * norm,
            inv_y * (rho * norm),
            inv_y * scale,
            0.99 * jax.nn.sigmoid(x[5]),
            jax.nn.sigmoid(x[6]),
            jax.nn.sigmoid(x[7]),
            jax.nn.sigmoid(x[8]),
        ]
        for p in range(9):
            value = along_lanes(values[p], index)
            if p == 5:
                value = jnp.maximum(jnp.log2(value * cover.astype(f32)), LOWEST)
            for j in range(per):
                shifted = pltpu.roll(value, LANES - j * group, 1) if j else value
                if per == 1:
                    send_ref[p, part, :] = shifted
                else:
                    send_ref[p, pl.ds(8 * c * per + j, 8, stride=per), :] = shifted

    for load in loads[3:7]:
        load.wait()
    bias = 0.5 * bias_ref[...].reshape(1, bias_ref.shape[0])
    half_ref[...] = first_ref[...] * bf16(0.5)
    second = jnp.broadcast_to(
        second_ref[...].astype(f32).reshape(1, second_ref.shape[0]), (16, second_ref.shape[0])
    ).astype(bf16)

    block = max(BLOCK, span)
    per_block = block // span

    def network(j, carry):
        feats = feat_ref[:, pl.ds(pl.multiple_of(j * block, block), block), :]
        feats = feats.reshape(stripe_tiles * block, feat_ref.shape[2])
        z = jnp.dot(feats, half_ref[...], preferred_element_type=f32) + bias
        hidden = z + z * jnp.tanh(z * (2.0 * GELU + (8.0 * 0.044715 * GELU) * (z * z)))
        hidden = hidden.reshape(stripe_tiles, per_block, span, hidden.shape[-1])
        for i in range(per_block):
            part = hidden[:, i].reshape(LANES, hidden.shape[-1]).astype(bf16)
            logits = lax.dot_general(
                second, part, (((1,), (1,)), ((), ())), preferred_element_type=f32,
            )
            spread_ref[pl.ds(j * per_block + i, 1), :] = logits[0:1]
        return carry

    steps = pixels // block
    early = min(EARLY, steps // 2)
    if early:
        lax.fori_loop(0, early, network, 0, unroll=UNROLL)
    pl.semaphore_wait(barrier, regions - 1)

    def send(i, carry):
        peer = lax.rem(me + i, regions)
        pltpu.make_async_remote_copy(
            src_ref=send_ref.at[:, pl.ds(peer, 1), :], dst_ref=recv_ref.at[:, pl.ds(me, 1), :],
            send_sem=send_sem, recv_sem=recv_sem.at[me // BATCH], device_id=(peer,),
            device_id_type=MESH,
        ).start()
        return carry

    lax.fori_loop(1, regions, send, 0, unroll=True)
    for p in range(9):
        recv_ref[p, pl.ds(me, 1), :] = send_ref[p, pl.ds(me, 1), :]
    lax.fori_loop(early, steps, network, 0, unroll=UNROLL)

    for load in loads[7:]:
        load.wait()
    tile_lane = same((LANES, stripe_tiles), lambda i: i // span, lambda j: j)
    lane_pixel = same((LANES, pixels), lambda i: i & (span - 1), lambda j: j & (span - 1))
    row_pixel = same((rows, pixels), lambda i: i, lambda j: j // span)
    for k in range(3):
        flat = jnp.concatenate(
            [target_ref[k:k + 1, t * pixels:(t + 1) * pixels] for t in range(stripe_tiles)], 0
        )
        wanted_ref[k] = dot(
            row_pixel, dot(tile_lane, flat, selector=0, pieces=2) * lane_pixel, True, selector=0, pieces=2
        )
    my_tiles = same(
        (tile_count, LANES), lambda i: i - me * stripe_tiles, lambda j: j // span
    ).astype(bf16)
    flip_ref[...] = jnp.dot(
        flips_ref[...].astype(f32).astype(bf16), my_tiles, preferred_element_type=f32,
    )

    wide = min(span, TSIDE)
    half = (TSIDE - wide) / 2

    def x_row(i):
        return ((i * span) & (TSIDE - 1)).astype(f32) - half

    def y_row(i):
        return (i * span // TSIDE).astype(f32) - 7.5

    x_lane = (lane8 & (wide - 1)).astype(f32) + (half + 0.5)
    y_lane = ((lane8 & (span - 1)) // TSIDE).astype(f32) + 8.0
    depth_rows = SPLATS * rows
    at = iota((SPLATS, depth_rows), 1)
    mine = at // rows == iota((SPLATS, depth_rows), 0)
    xr, yr = x_row(at & (rows - 1)), y_row(at & (rows - 1))
    terms = [jnp.ones_like(xr), xr, yr, xr * xr, xr * yr, yr * yr]
    basis_ref[...] = jnp.concatenate([jnp.where(mine, term, 0.0) for term in terms], 0).astype(bf16)
    ones_ref[...] = (
        iota(ones_ref.shape, 1) // 8 == iota(ones_ref.shape, 0)
    ).astype(f32).astype(bf16)
    for s in range(SPLATS):
        fold_ref[s * LANES:(s + 1) * LANES, :] = same(
            (LANES, LANES), lambda i: i // span * SPLATS + s, lambda j: j
        ).astype(bf16)

    for s in range(SPLATS):
        picks = same((LANES, LANES), lambda i: i, lambda j: j // span * SPLATS + s).astype(bf16)
        widen_ref[:, s * LANES:(s + 1) * LANES] = picks
    for buf in (rhs_ref, tone_ref, stage_ref):
        buf[...] = jnp.zeros(buf.shape, buf.dtype)

    def arrive(batch, count):
        some = pl.ds(0, count)
        pltpu.make_async_remote_copy(
            src_ref=send_ref.at[:, some, :], dst_ref=recv_ref.at[:, some, :],
            send_sem=send_sem, recv_sem=recv_sem.at[batch], device_id=(me,), device_id_type=MESH,
        ).wait_recv()

    def expand(c):
        base = pl.multiple_of(c * BATCH, BATCH)
        value = jnp.concatenate(
            [recv_ref[p, pl.ds(base, BATCH), :] for p in range(NPAR)], 0
        )
        pieces = []
        for _ in range(3):
            piece = value.astype(bf16).astype(f32)
            value = value - piece
            pieces.append(piece)
        spread = jnp.dot(
            jnp.concatenate(pieces, 0).astype(bf16), widen_ref[...], preferred_element_type=f32
        )
        count = NPAR * BATCH
        spread = spread[:count] + spread[count:2 * count] + spread[2 * count:]
        for p in range(NPAR):
            for s in range(SPLATS):
                first = pl.multiple_of((c * NPAR + p) * SPLATS * BATCH, BATCH) + s * BATCH
                ex_ref[pl.ds(first, BATCH), :] = spread[
                    p * BATCH:(p + 1) * BATCH, s * LANES:(s + 1) * LANES
                ]

    vs = [slice(8 * v, 8 * v + 8) for v in range(nv)]
    xpos = x_row(row8) + x_lane
    ypos = y_row(row8) + y_lane
    step = float(8 * span // TSIDE)

    def first_row(r, p):
        return (r // BATCH * NPAR + p) * (SPLATS * BATCH) + (r & (BATCH - 1))

    def row(r, p, s):
        return ex_ref[pl.ds(first_row(r, p) + s * BATCH, 1), :]

    def forward(r, carry):
        trans = [jnp.ones((8, LANES), f32)] * nv
        color = [[jnp.zeros((8, LANES), f32)] * nv for _ in range(3)]
        for s in range(SPLATS):
            us = (xpos - row(r, 0, s)) * row(r, 2, s)
            m_y, skew, inv_y, level = row(r, 1, s), row(r, 3, s), row(r, 4, s), row(r, 5, s)
            ks = [row(r, 6 + k, s) for k in range(3)]
            dy = ypos - m_y
            w, p = dy * inv_y, us - dy * skew
            rise_w, rise_p = step * inv_y, step * skew
            for v in range(nv):
                if v:
                    w, p = w + rise_w, p - rise_p
                alpha = jnp.exp2(level - (p * p + w * w))
                weight = trans[v] * alpha
                a_ref[r * SPLATS + s, vs[v]] = alpha
                w_ref[r * SPLATS + s, vs[v]] = weight
                for k in range(3):
                    color[k][v] = color[k][v] + weight * ks[k]
                trans[v] = trans[v] - weight
        for v in range(nv):
            for k in range(3):
                tree_ref[inner + r, k, vs[v]] = color[k][v]
            tree_ref[inner + r, 3, vs[v]] = trans[v]
        return carry

    def render(i, carry):
        batch = lax.rem(me // BATCH + i, batches)

        @pl.when(i == 0)
        def _():
            arrive(batch, BATCH - 1)

        @pl.when(i > 0)
        def _():
            arrive(batch, BATCH)

        expand(batch)
        lax.fori_loop(0, BATCH, lambda j, c: forward(batch * BATCH + j, c), 0, unroll=FUNROLL)
        return carry

    lax.fori_loop(0, batches, render, 0)
    everyone = pl.ds(0, regions - 1)
    pltpu.make_async_remote_copy(
        src_ref=send_ref.at[:, everyone, :], dst_ref=recv_ref.at[:, everyone, :],
        send_sem=send_sem, recv_sem=recv_sem.at[0], device_id=(me,), device_id_type=MESH,
    ).wait_send()

    def flipped(n):
        return jnp.broadcast_to(flip_ref[pl.ds(n, 1), :], (8, LANES)) > 0.0

    def merge(n, v):
        if n >= inner:
            return [tree_ref[n, k, vs[v]] for k in range(4)]
        low, high = merge(2 * n + 1, v), merge(2 * n + 2, v)
        flip = flipped(n)
        over_low = jnp.where(flip, high[3], 1.0)
        over_high = jnp.where(flip, 1.0, low[3])
        both = [over_low * low[k] + over_high * high[k] for k in range(3)] + [low[3] * high[3]]
        for k in range(4):
            tree_ref[n, k, vs[v]] = both[k]
        return both

    for v in range(nv):
        merge(0, v)

    for v in range(nv):
        logit = spread_ref[vs[v]]
        spread = 0.5 + jnp.maximum(logit, 0.0) + jnp.log1p(jnp.exp(-jnp.abs(logit)))
        inv_square = 1.0 / (spread * spread)
        clear = tree_ref[0, 3, vs[v]]
        residual = [tree_ref[0, k, vs[v]] + clear - wanted_ref[k, vs[v]] for k in range(3)]
        total = residual[0] * residual[0] + residual[1] * residual[1] + residual[2] * residual[2]
        lossy_ref[vs[v]] = 0.5 * total * inv_square + jnp.log(spread)
        gs = [res * inv_square for res in residual]
        for k in range(3):
            g_ref[k, vs[v]] = gs[k]

    def split(n, v, g, front, behind):
        if n >= inner:
            down_ref[n - inner, 0, vs[v]] = front
            down_ref[n - inner, 1, vs[v]] = behind
            return
        flip = flipped(n)
        low = [tree_ref[2 * n + 1, k, vs[v]] for k in range(4)]
        high = [tree_ref[2 * n + 2, k, vs[v]] for k in range(4)]
        back = [jnp.where(flip, l, h) for l, h in zip(low, high)]
        through = front * jnp.where(flip, high[3], low[3])
        value = g[0] * back[0] + g[1] * back[1] + g[2] * back[2] + back[3] * behind
        split(2 * n + 1, v, g, jnp.where(flip, through, front), jnp.where(flip, behind, value))
        split(2 * n + 2, v, g, jnp.where(flip, front, through), jnp.where(flip, value, behind))

    for v in range(nv):
        g = [g_ref[k, vs[v]] for k in range(3)]
        split(0, v, g, jnp.ones((8, LANES), f32), g[0] + g[1] + g[2])

    def backward(r, slot):
        front = [down_ref[r, 0, vs[v]] for v in range(nv)]
        gs = [[front[v] * g_ref[k, vs[v]] for v in range(nv)] for k in range(3)]
        behind = [front[v] * down_ref[r, 1, vs[v]] for v in range(nv)]
        colors = [[], [], []]
        for s in reversed(range(SPLATS)):
            ks = [row(r, 6 + k, s) for k in range(3)]
            pulls, tones = [], [None] * 3
            for v in range(nv):
                alpha = a_ref[r * SPLATS + s, vs[v]]
                weight = w_ref[r * SPLATS + s, vs[v]]
                shade = ks[0] * gs[0][v] + ks[1] * gs[1][v] + ks[2] * gs[2][v]
                diff = shade - behind[v]
                behind[v] = behind[v] + alpha * diff
                pulls.append(weight * diff)
                for k in range(3):
                    tone = weight * gs[k][v]
                    tones[k] = tone if v == 0 else tones[k] + tone
            rhs_ref[slot, s * rows:(s + 1) * rows, :] = jnp.concatenate(pulls, 0).astype(bf16)
            for k in range(3):
                colors[k].insert(0, tones[k])
            if s % 2 == 0:
                for k in range(3):
                    tone_ref[slot, s * 8:(s + 2) * 8, k * LANES:(k + 1) * LANES] = (
                        jnp.concatenate(colors[k][:2], 0).astype(bf16)
                    )

    def reduce(r, slot):
        summed = jnp.dot(basis_ref[...], rhs_ref[slot], preferred_element_type=f32)
        toned = jnp.dot(ones_ref[...], tone_ref[slot], preferred_element_type=f32)
        h, hx, hy, hxx, hxy, hyy = [
            summed[b * SPLATS:(b + 1) * SPLATS] for b in range(NMOM)
        ]
        dx = x_lane - ex_ref[pl.ds(first_row(r, 0), SPLATS, stride=BATCH), :]
        dy = y_lane - ex_ref[pl.ds(first_row(r, 1), SPLATS, stride=BATCH), :]
        about_x = hx + dx * h
        about_y = hy + dy * h
        moments = [
            h,
            about_x,
            about_y,
            hxx + dx * (hx + about_x),
            hxy + dx * hy + dy * about_x,
            hyy + dy * (hy + about_y),
        ]
        for k in range(3):
            moments.append(toned[0:SPLATS, k * LANES:(k + 1) * LANES])
        for p in range(9):
            first = p * SPLATS * BATCH + (r & (BATCH - 1))
            stage_ref[pl.ds(first, SPLATS, stride=BATCH), :] = moments[p]

    def fold(base):
        wide = [
            jnp.concatenate(
                [stage_ref[(p * SPLATS + s) * BATCH:(p * SPLATS + s + 1) * BATCH, :] for s in range(SPLATS)], 1
            )
            for p in range(9)
        ]
        whole = jnp.concatenate(wide, 0)
        coarse = whole.astype(bf16).astype(f32)
        folded = jnp.dot(
            jnp.concatenate([coarse, whole - coarse], 0).astype(bf16), fold_ref[...],
            preferred_element_type=f32,
        )
        folded = folded[:9 * BATCH] + folded[9 * BATCH:]
        for p in range(9):
            gsend_ref[p, pl.ds(base, BATCH), :] = folded[p * BATCH:(p + 1) * BATCH]

    def give_back(base):
        def back(j, carry):
            peer = base + j

            @pl.when(peer != me)
            def _():
                pltpu.make_async_remote_copy(
                    src_ref=gsend_ref.at[:, pl.ds(peer, 1), :],
                    dst_ref=grads_hbm.at[:, pl.ds(me, 1), :],
                    send_sem=gsend_sem, recv_sem=grecv_sem,
                    device_id=(peer,), device_id_type=MESH,
                ).start()

            return carry

        lax.fori_loop(0, BATCH, back, 0, unroll=True)

    def base_of(i):
        return pl.multiple_of(lax.rem(i + batches - 1, batches) * BATCH, BATCH)

    def pairs_after(base):
        def pair(j, carry):
            r = base + 2 * j
            for k in range(2):
                reduce(r - 2 + k, k)
            for k in range(2):
                backward(r + k, k)
            return carry

        lax.fori_loop(1, BATCH // 2, pair, 0, unroll=PUNROLL)

    def finish(i, carry):
        base, past = base_of(i + 1), base_of(i)
        for k in range(2):
            reduce(past + BATCH - 2 + k, k)
        fold(past)
        for k in range(2):
            backward(base + k, k)

        give_back(past)
        pairs_after(base)
        return carry

    for k in range(2):
        backward(base_of(1) + k, k)
    pairs_after(base_of(1))
    lax.fori_loop(1, batches, finish, 0)
    last = base_of(batches)
    for k in range(2):
        reduce(last + BATCH - 2 + k, k)
    fold(last)
    give_back(last)
    own = pltpu.make_async_copy(
        gsend_ref.at[:, pl.ds(me, 1), :], grads_hbm.at[:, pl.ds(me, 1), :], own_sem
    )
    own.start()

    lane_tile = same((stripe_tiles, LANES), lambda i: i, lambda j: j // span)
    pixel_row = same((pixels, rows), lambda i: i // span, lambda j: j)
    pixel_lane = same((pixels, LANES), lambda i: i & (span - 1), lambda j: j & (span - 1))
    flat = dot(
        lane_tile, dot(pixel_row, lossy_ref[...], selector=0, pieces=2) * pixel_lane, True,
        selector=0, pieces=2,
    )
    for t in range(stripe_tiles):
        loss_ref[0:1, t * pixels:(t + 1) * pixels] = flat[t:t + 1]
    for c in range(tile_count // LANES):
        part = slice(8 * c, 8 * c + 8)
        place_ref[part, :] = (lane8 & -SPLATS) + to_lanes(depth_ref[:, c * LANES:(c + 1) * LANES])
        x = [gauss_ref[p, part, :] for p in range(9)]
        squash = jnp.tanh(x[4])
        rho = 0.9 * squash
        inv = 1.0 / (1.0 - rho * rho)
        tones = [jax.nn.sigmoid(x[6 + k]) for k in range(3)]
        factors = [
            jnp.exp(-x[2]), jnp.exp(-x[3]), inv, inv * rho,
            inv * (0.9 * (1.0 - squash * squash)), inv * rho * (0.9 * (1.0 - squash * squash)),
            jax.nn.sigmoid(-x[5]),
        ] + [tone * (1.0 - tone) for tone in tones]
        for p in range(10):
            factor_ref[p, part, :] = factors[p]
    keeps = [
        pltpu.make_async_copy(loss_ref, loss_hbm, keep_sem.at[0]),
        pltpu.make_async_copy(factor_ref, factor_hbm, keep_sem.at[1]),
        pltpu.make_async_copy(place_ref, place_hbm, keep_sem.at[2]),
    ]
    for keep in keeps:
        keep.start()

    pltpu.make_async_remote_copy(
        src_ref=gsend_ref.at[:, everyone, :], dst_ref=grads_hbm.at[:, everyone, :],
        send_sem=gsend_sem, recv_sem=grecv_sem, device_id=(me,), device_id_type=MESH,
    ).wait()
    own.wait()
    for keep in keeps:
        keep.wait()


def chain_kernel(moment_ref, factor_ref, place_ref, loss_in, grads_ref, loss_out):
    loss_out[...] = loss_in[...]
    regions, count = moment_ref.shape[1], place_ref.shape[0]
    per = regions // count
    group = LANES // per
    lane8 = iota((8, LANES), 1)
    for c in range(count // 8):
        part = slice(8 * c, 8 * c + 8)
        index = place_ref[part, :]
        sums = []
        for p in range(9):
            if per == 1:
                value = moment_ref[p, part, :]
            else:
                value = jnp.zeros((8, LANES), jnp.float32)
                for j in range(per):
                    piece = moment_ref[p, pl.ds(8 * c * per + j, 8, stride=per), :]
                    piece = pltpu.roll(piece, j * group, 1) if j else piece
                    value = jnp.where(lane8 // group == j, piece, value)
            sums.append(along_lanes(value, index))
        inv_x, inv_y, inv, skew, bend, lean, hide = [factor_ref[p, part, :] for p in range(7)]
        hu, hv = inv_x * sums[1], inv_y * sums[2]
        huu = inv_x * (inv_x * sums[3])
        huv = inv_x * (inv_y * sums[4])
        hvv = inv_y * (inv_y * sums[5])
        wide = inv * huu - skew * huv
        tall = inv * hvv - skew * huv
        results = [
            inv_x * (inv * hu - skew * hv),
            inv_y * (inv * hv - skew * hu),
            wide,
            tall,
            bend * huv - lean * (wide + tall),
            hide * sums[0],
        ]
        for k in range(3):
            results.append(sums[6 + k] * factor_ref[7 + k, part, :])
        for p in range(9):
            grads_ref[p, part, :] = results[p]


def shards(gaussians, depth, coverage, flips, features, w_first, b_first, w_second, target):
    regions = lax.axis_size("region")
    tile_count = depth.shape[1]
    stripe_tiles = tile_count // regions
    pixels = TSIDE * TSIDE
    rows = pixels * stripe_tiles // LANES
    nodes = 2 * regions - 1
    width = features.shape[1]
    f32, bf16 = jnp.float32, jnp.bfloat16
    dma = pltpu.SemaphoreType.DMA
    dense = gaussians.reshape(9, tile_count * SPLATS // LANES, LANES)
    ranks = depth[0].T
    anywhere = pl.BlockSpec(memory_space=pl.ANY)
    vmem = pl.BlockSpec(memory_space=pltpu.VMEM)
    operands = (
        dense,
        ranks,
        coverage,
        flips.T,
        features.reshape(stripe_tiles, pixels, width),
        w_first,
        b_first,
        w_second,
        target,
    )
    loss, moments, factors, places = pl.pallas_call(
        splat_kernel,
        out_shape=(
            jax.ShapeDtypeStruct((1, stripe_tiles * pixels), f32),
            jax.ShapeDtypeStruct((9, regions, LANES), f32),
            jax.ShapeDtypeStruct((10,) + dense.shape[1:], f32),
            jax.ShapeDtypeStruct(dense.shape[1:], jnp.int32),
        ),
        in_specs=[anywhere] * 9,
        out_specs=(anywhere,) * 4,
        scratch_shapes=[pltpu.VMEM(x.shape, x.dtype) for x in operands] + [
            dma((9,)),
            pltpu.VMEM(w_first.shape, w_first.dtype),
            pltpu.VMEM((1, stripe_tiles * pixels), f32),
            pltpu.VMEM((10,) + dense.shape[1:], f32),
            pltpu.VMEM(dense.shape[1:], jnp.int32),
            dma((3,)),
            dma(()),
            pltpu.VMEM((9, regions, LANES), f32),
            pltpu.VMEM((9, regions, LANES), f32),
            dma(()),
            dma((regions // BATCH,)),
            pltpu.VMEM((9, regions, LANES), f32),
            dma(()),
            dma(()),
            pltpu.VMEM((regions - 1, LANES), f32),
            pltpu.VMEM((rows, LANES), f32),
            pltpu.VMEM((3, rows, LANES), f32),
            pltpu.VMEM((NPAR * SPLATS * regions, LANES), f32),
            pltpu.VMEM((regions * SPLATS, rows, LANES), f32),
            pltpu.VMEM((regions * SPLATS, rows, LANES), f32),
            pltpu.VMEM((nodes, 4, rows, LANES), f32),
            pltpu.VMEM((regions, 2, rows, LANES), f32),
            pltpu.VMEM((3, rows, LANES), f32),
            pltpu.VMEM((rows, LANES), f32),
            pltpu.VMEM((2, SPLATS * rows, LANES), bf16),
            pltpu.VMEM((2, SPLATS * 8, 3 * LANES), bf16),
            pltpu.VMEM((9 * BATCH * SPLATS, LANES), f32),
            pltpu.VMEM((NMOM * SPLATS, SPLATS * rows), bf16),
            pltpu.VMEM((16, SPLATS * 8), bf16),
            pltpu.VMEM((SPLATS * LANES, LANES), bf16),
            pltpu.VMEM((LANES, SPLATS * LANES), bf16),
        ],
        compiler_params=pltpu.CompilerParams(
            vmem_limit_bytes=56 * 1024 * 1024, collective_id=0, has_side_effects=True
        ),
    )(*operands)
    grads, loss = pl.pallas_call(
        chain_kernel,
        out_shape=(
            jax.ShapeDtypeStruct(dense.shape, f32), jax.ShapeDtypeStruct(loss.shape, f32)
        ),
        in_specs=[vmem] * 4,
        out_specs=(vmem, vmem),
    )(moments, factors, places, loss)
    return (loss.reshape(-1), grads.reshape(gaussians.shape))


def solution(mesh):
    placed = (
        P("region", None, None),
        P("region", None, None),
        P("region", None),
        P(),
        P("region", None),
        P(),
        P(),
        P(),
        P(None, "region"),
    )
    return jax.shard_map(
        shards,
        mesh=mesh,
        in_specs=placed,
        out_specs=(P("region"), P("region", None, None)),
        check_vma=False,
    )
```
